32 devices in a mesh: dp: 8 (over z, x), tensor: 4 (over y, core).
Axes of the slice: x: 2, y: 2, z: 4, core: 2. Of those that a mesh axis runs over, the one named last changes fastest.
Arguments:
- frames: bfloat16 [12288, 768], P(('dp', 'tensor')), may hold values from -6 to 6
- segments: int32 [8, 1536], P('dp'), may hold values from 0 to 15, never falling along the last dimension, each value on 1 to 768 neighbouring positions
- norm1_gain: float32 [768], P(('dp', 'tensor')), may hold values from 0.25 to 1.75
- norm1_shift: float32 [768], P(('dp', 'tensor')), may hold values from -1.5 to 1.5
- in_weight: bfloat16 [768, 3, 768], P('dp', None, 'tensor'), may hold values from -0.21875 to 0.21875
- proj_bias: bfloat16 [2, 12, 64], P(None, 'tensor', 'dp'), may hold values from -1.5 to 1.5
- out_weight: bfloat16 [768, 768], P('tensor', 'dp'), may hold values from -0.875 to 0.875
- out_bias: float32 [768], P(('dp', 'tensor')), may hold values from -1.5 to 1.5
- norm2_gain: float32 [768], P(('dp', 'tensor')), may hold values from 0.25 to 1.75
- norm2_shift: float32 [768], P(('dp', 'tensor')), may hold values from -1.5 to 1.5
- fc1_weight: bfloat16 [768, 3072], P('dp', 'tensor'), may hold values from -0.21875 to 0.21875
- fc1_bias: bfloat16 [48, 64], P('tensor', 'dp'), may hold values from -1.5 to 1.5
- fc2_weight: bfloat16 [3072, 768], P('tensor', 'dp'), may hold values from -0.109375 to 0.109375
- fc2_bias: float32 [768], P(('dp', 'tensor')), may hold values from -1.5 to 1.5
- cotangent: bfloat16 [12288, 768], P(('dp', 'tensor')), may hold values from -6 to 6
Outputs:
- output: bfloat16 [12288, 768], P(('dp', 'tensor'))
- grad_frames: float32 [12288, 768], P(('dp', 'tensor'))
- grad_norm1_gain: float32 [768], P(('dp', 'tensor'))
- grad_norm1_shift: float32 [768], P(('dp', 'tensor'))
- grad_in_weight: float32 [768, 3, 768], P('dp', None, 'tensor')
- grad_proj_bias: float32 [2, 12, 64], P(None, 'tensor', 'dp')
- grad_out_weight: float32 [768, 768], P('tensor', 'dp')
- grad_out_bias: float32 [768], P(('dp', 'tensor'))
- grad_norm2_gain: float32 [768], P(('dp', 'tensor'))
- grad_norm2_shift: float32 [768], P(('dp', 'tensor'))
- grad_fc1_weight: float32 [768, 3072], P('dp', 'tensor')
- grad_fc1_bias: float32 [48, 64], P('tensor', 'dp')
- grad_fc2_weight: float32 [3072, 768], P('tensor', 'dp')
- grad_fc2_bias: float32 [768], P(('dp', 'tensor'))
The draws below stay inside these ranges and needn't reach their ends.
Inputs may be any that keep to these rules, and one draw needn't show every extreme that they name: `segments`: within each sequence the numbers never fall, every number appears, each covers 1 to 768 frames, and one covers exactly 768.
All inputs are finite; a program needn't handle non-finite values.
Results may differ from the reference program's by a relative error of at most 0.015.
Values may be sent and summed in bfloat16 or wider, within the bound.
A program may use at most 128 MiB of HBM per device.

```python
import math
import jax
import jax.numpy as jnp
import numpy as np
from jax import lax

D = 768
H = 12
HD = 64
FF = 3072
TOK_DEV = 1536
SEQS = 8
TOKENS = 12288


def spiked(entries, key, source, target, blocks, factor):
    def block_of(dim):
        return (jnp.arange(entries.shape[dim]) // (entries.shape[dim] // blocks)).reshape((-1,) + (1,) * (entries.ndim - 1 - dim))

    one_side = jax.random.permutation(key, blocks)[block_of(target)]
    other_side = (block_of(target) + blocks // 2) % blocks
    return jnp.where((block_of(source) == one_side) | (block_of(source) == other_side), factor * entries, entries)


def block_scale(key, extent, split, low, high):
    loudness, own = 1.0, jax.random.fold_in(key, 6)
    for axis_at, shards_of in split:
        heights = jnp.exp(jax.random.uniform(jax.random.fold_in(own, axis_at), (shards_of,), jnp.float32, low / len(split), high / len(split)))
        loudness = loudness * jnp.repeat(heights, extent[axis_at] // shards_of).reshape([-1 if axis == axis_at else 1 for axis in range(len(extent))])
    return loudness


def split_up(count, total, limit, skew):
    portions = [(1 << 20) // math.isqrt(standing ** skew) + 1 for standing in range(2, count + 1)]
    rest, holding = total - limit - (count - 1), [1] * (count - 1)
    while rest > 0:
        free = [i for i in range(count - 1) if holding[i] < limit]
        pool, budget = sum([portions[i] for i in free]), rest
        for i in free:
            extra = min(limit - holding[i], max(1, budget * portions[i] // pool), rest)
            holding[i] = holding[i] + extra
            rest = rest - extra
    return np.array([limit] + holding)


def uneven(own_key, count, total, bound, skew):
    if count == 2:
        one = jax.random.randint(own_key, (), max(1, total - bound), min(bound, total - 1) + 1)
        return jnp.stack([one, total - one])
    sizes = jnp.asarray(split_up(count, total, bound, skew), jnp.int32)
    pairs = (count - 1) // 2
    source_of, sink = sizes[1:1 + 2 * pairs:2], sizes[2:2 + 2 * pairs:2]
    margin = jnp.minimum(source_of - 1, bound - sink)
    moved = jax.random.randint(jax.random.fold_in(own_key, 1), (pairs,), 0, 1 << 20) % (margin + 1)
    sizes = sizes.at[1:1 + 2 * pairs:2].set(source_of - moved).at[2:2 + 2 * pairs:2].set(sink + moved)
    return sizes[jax.random.permutation(jax.random.fold_in(own_key, 2), count)]


def gaussian(key, dims, width, limit, split=(), kind=jnp.bfloat16):
    drawn = width * jax.random.normal(key, dims, jnp.float32)
    if split:
        drawn = drawn * block_scale(key, dims, split, -0.22, 0.18)
    return jnp.clip(drawn, -limit, limit).astype(kind)


def heavy_noise(own_key, dims, deviation, bound, shards, heavy, held_as=jnp.bfloat16):
    entries = deviation * jax.random.normal(own_key, dims, jnp.float32)
    if shards:
        entries = entries * block_scale(own_key, dims, shards, -0.22, 0.18)
    return jnp.clip(spiked(entries, jax.random.fold_in(own_key, 3), *heavy), -bound, bound).astype(held_as)


def setup_inputs(seed: int = 0) -> dict:
    splits = jax.random.split(jax.random.key(seed), 16)
    frames = heavy_noise(splits[0], (TOKENS, D), 1.0, 6.0, ((0, 32),), (0, 1, 32, 2.75))
    segments = jax.vmap(lambda own: jnp.searchsorted(jnp.cumsum(uneven(own, 16, TOK_DEV, TOK_DEV // 2, 2)), jnp.arange(TOK_DEV), side="right"))(jax.random.split(splits[1], SEQS)).reshape((SEQS, TOK_DEV)).astype(jnp.int32)
    norm1_gain = jnp.clip(1.0 + 0.15 * jax.random.normal(splits[2], (D,), jnp.float32), 0.25, 1.75)
    norm1_shift = gaussian(splits[3], (D,), 0.3, 1.5, ((0, 32),), jnp.float32)
    in_weight = gaussian(splits[4], (D, 3, D), D ** -0.5, 0.21875, ((0, 8), (2, 4)))
    proj_bias = gaussian(splits[5], (2, H, HD), 0.3, 1.5, ((1, 4), (2, 8)))
    out_weight = gaussian(splits[6], (D, D), (D // 16) ** -0.5, 0.875, ((0, 4), (1, 8)))
    out_bias = gaussian(splits[7], (D,), 0.3, 1.5, ((0, 32),), jnp.float32)
    norm2_gain = jnp.clip(1.0 + 0.15 * jax.random.normal(splits[8], (D,), jnp.float32), 0.25, 1.75)
    norm2_shift = gaussian(splits[9], (D,), 0.3, 1.5, ((0, 32),), jnp.float32)
    fc1_weight = gaussian(splits[10], (D, FF), D ** -0.5, 0.21875, ((0, 8), (1, 4)))
    fc1_bias = gaussian(splits[11], (FF // HD, HD), 0.3, 1.5, ((0, 4), (1, 8)))
    fc2_weight = gaussian(splits[12], (FF, D), FF ** -0.5, 0.109375, ((0, 4), (1, 8)))
    fc2_bias = gaussian(splits[13], (D,), 0.3, 1.5, ((0, 32),), jnp.float32)
    cotangent = heavy_noise(splits[14], (TOKENS, D), 1.0, 6.0, ((0, 32),), (0, 1, 32, 2.75))
    return dict(frames=frames, segments=segments, norm1_gain=norm1_gain, norm1_shift=norm1_shift, in_weight=in_weight, proj_bias=proj_bias, out_weight=out_weight, out_bias=out_bias, norm2_gain=norm2_gain, norm2_shift=norm2_shift, fc1_weight=fc1_weight, fc1_bias=fc1_bias, fc2_weight=fc2_weight, fc2_bias=fc2_bias, cotangent=cotangent)


@jax.custom_vjp
def low(v):
    return lax.optimization_barrier(v.astype(jnp.bfloat16)).astype(jnp.float32)

@jax.custom_vjp
def low_back(v):
    return v

def low_keep(v):
    return (low(v), None)

def low_pass(kept, grad):
    return (grad,)

def back_keep(v):
    return (v, None)

def back_low(kept, grad):
    return (low(grad),)
low.defvjp(low_keep, low_pass)
low_back.defvjp(back_keep, back_low)

def layer_norm(row_block, norm_gain, norm_shift):
    row_mean = lax.optimization_barrier(jnp.mean(row_block, axis=-1, keepdims=True))
    centred = row_block - row_mean
    row_var = lax.optimization_barrier(jnp.mean(centred * centred, axis=-1, keepdims=True))
    return centred * lax.rsqrt(row_var + 1e-05) * norm_gain + norm_shift

def product(left, right):
    return jnp.dot(left, right, precision=lax.Precision.HIGHEST)

def sequence_layer(row_block, doc_ids, params):
    gain_one, shift_one, in_w, proj_b, out_w, out_b, gain_two, shift_two, fc1_w, fc1_b, fc2_w, fc2_b = params
    seq_length = row_block.shape[0]
    normed = low(layer_norm(row_block, gain_one, shift_one))
    projected = product(normed, in_w.reshape(D, 3 * D)).reshape(seq_length, 3, D)
    bias_pair = proj_b.reshape(2, D)
    query = low(low_back(projected[:, 0] + bias_pair[0])).reshape(seq_length, H, HD)
    keys_all = low(low_back(projected[:, 1])).reshape(seq_length, H, HD)
    values_all = low(low_back(projected[:, 2] + bias_pair[1])).reshape(seq_length, H, HD)
    scores = low_back(jnp.einsum('qhe,khe->hqk', query, keys_all, precision=lax.Precision.HIGHEST) * 0.125)
    same_doc = doc_ids[:, None] == doc_ids[None, :]
    scores = jnp.where(same_doc[None], scores, -1e+30)
    row_max = lax.optimization_barrier(jnp.max(scores, axis=-1, keepdims=True))
    exp_scores = jnp.exp(scores - row_max)
    attn_probs = low(exp_scores / lax.optimization_barrier(jnp.sum(exp_scores, axis=-1, keepdims=True)))
    attn_mixed = jnp.einsum('hqk,khe->qhe', attn_probs, values_all, precision=lax.Precision.HIGHEST)
    attn_mixed = low(low_back(attn_mixed.reshape(seq_length, D)))
    attended = low_back(product(attn_mixed, out_w) + out_b)
    middle = row_block + attended
    normed_two = low(layer_norm(middle, gain_two, shift_two))
    hidden = low_back(product(normed_two, fc1_w) + fc1_b.reshape(FF))
    active = low(jax.nn.gelu(hidden, approximate=False))
    branch = low_back(product(active, fc2_w) + fc2_b)
    return middle + branch

def reference(frames, segments, norm1_gain, norm1_shift, in_weight, proj_bias, out_weight, out_bias, norm2_gain, norm2_shift, fc1_weight, fc1_bias, fc2_weight, fc2_bias, cotangent):
    params = tuple((param.astype(jnp.float32) for param in (norm1_gain, norm1_shift, in_weight, proj_bias, out_weight, out_bias, norm2_gain, norm2_shift, fc1_weight, fc1_bias, fc2_weight, fc2_bias)))
    flat = frames.astype(jnp.float32)

    def forward(flat_rows, weights):
        stacked = flat_rows.reshape(SEQS, TOK_DEV, D)

        def per_sequence(pair):
            return sequence_layer(pair[0], pair[1], weights)
        mapped = lax.map(jax.checkpoint(per_sequence), (stacked, segments))
        return mapped.reshape(TOKENS, D)
    result, pullback = jax.vjp(forward, flat, params)
    grad_flat, grad_params = pullback(cotangent.astype(jnp.float32))
    return (result.astype(jnp.bfloat16), grad_flat, grad_params[0], grad_params[1], grad_params[2], grad_params[3], grad_params[4], grad_params[5], grad_params[6], grad_params[7], grad_params[8], grad_params[9], grad_params[10], grad_params[11])
```

```python
import functools

import jax
import jax.numpy as jnp
from jax import lax
from jax.experimental import pallas as pl
from jax.experimental.pallas import tpu as pltpu
from jax.sharding import PartitionSpec as P

HD = 64
BF = jnp.bfloat16
F32 = jnp.float32
VMEM_BYTES = 56 << 20


def gelu_exact(values_in):
    return jax.nn.gelu(values_in, approximate=False)


def contract(pattern, left, right):
    return jnp.einsum(pattern, left, right, preferred_element_type=F32)


def layer_norm(row_block, norm_gain, norm_shift):
    row_mean = jnp.mean(row_block, axis=-1, keepdims=True)
    centred = row_block - row_mean
    row_var = jnp.mean(centred * centred, axis=-1, keepdims=True)
    return centred * lax.rsqrt(row_var + 1e-05) * norm_gain + norm_shift


class Links:
    def __init__(self, num_dp, send_sems, recv_sems):
        self.num_dp, self.num_far = num_dp, num_dp // 2
        self.dp, self.tensor = lax.axis_index("dp"), lax.axis_index("tensor")
        self.send_sems, self.recv_sems, self.used = send_sems, recv_sems, 0
        self.started = []
        self.sibling = (self.dp, self.tensor ^ 1)
        self.across = (self.dp, self.tensor ^ 2)
        self.corner = (self.dp, self.tensor ^ 3)
        self.beside = (self.dp ^ 1, self.tensor)

    def far(self, step):
        return lax.rem(self.dp + 2 * step, self.num_dp)

    def far_from(self, step):
        return lax.rem(self.dp + self.num_dp - 2 * step, self.num_dp)

    def copy(self, src, dst, device):
        at = self.used
        self.used += 1
        made = pltpu.make_async_remote_copy(
            src_ref=src,
            dst_ref=dst,
            send_sem=self.send_sems.at[at],
            recv_sem=self.recv_sems.at[at],
            device_id=device,
            device_id_type=pl.DeviceIdType.MESH,
        )
        return made

    def send(self, src, dst, device):
        made = self.copy(src, dst, device)
        made.start()
        self.started.append(made)
        return made

    def greet(self, devices):
        barrier = pltpu.get_barrier_semaphore()
        for device in devices:
            pl.semaphore_signal(
                barrier, inc=1, device_id=device, device_id_type=pl.DeviceIdType.MESH
            )
        pl.semaphore_wait(barrier, len(devices))

    def finish(self):
        for made in self.started:
            made.wait_send()


def weight_spread(links, local_sems, shard, gathered, halves):
    columns = shard.shape[-1] // halves
    arrived = {}

    def part(ref, half, *lead):
        return ref.at[(*lead, slice(None), pl.ds(half * columns, columns))]

    own = pltpu.make_async_copy(shard, gathered.at[links.dp], local_sems)

    def begin():
        own.start()
        for half in range(halves):
            for step in range(1, links.num_far):
                arrived[half, step] = links.send(
                    part(shard, half), part(gathered, half, links.dp), (links.far(step), links.tensor)
                )
            arrived[half, 0] = links.send(
                part(shard, half), part(gathered, half, links.dp), links.beside
            )

    def forward(half, step):
        arrived[half, step].wait_recv()
        origin = links.far_from(step)
        place = part(gathered, half, origin)
        arrived[half, -step] = links.send(place, place, links.beside)

    def end():
        for half in range(halves):
            for step in range(1, links.num_far):
                arrived[half, -step].wait_recv()
            arrived[half, 0].wait_recv()
        own.wait()

    steps = [
        functools.partial(forward, half, step)
        for half in range(halves)
        for step in range(1, links.num_far)
    ]
    return begin, steps, end


def spread_count(num_dp, halves):
    return halves * (2 * (num_dp // 2 - 1) + 1)


def gather_kernel(num_dp, pieces, frames, shard, small, frames_all, gathered, small_all, send_sems, recv_sems, local_sems):
    links = Links(num_dp, send_sems, recv_sems)
    others = [lax.rem(links.dp + step, num_dp) for step in range(1, num_dp)]
    links.greet(
        [(other, links.tensor) for other in others] + [links.sibling, links.across, links.corner]
    )
    me = links.tensor
    rows = frames.shape[0] // pieces
    local = pltpu.make_async_copy(frames, frames_all.at[me], local_sems.at[1])
    local.start()
    mine = pltpu.make_async_copy(small, small_all.at[me, links.dp], local_sems.at[2])
    mine.start()
    small_in = [
        links.send(small, small_all.at[me, links.dp], (other, links.tensor)) for other in others
    ]
    begin, steps, end = weight_spread(links, local_sems.at[0], shard, gathered, 2)
    across_in = []
    for piece in range(pieces):
        cut = pl.ds(piece * rows, rows)
        across_in.append(links.send(frames.at[cut], frames_all.at[me, cut], links.across))
    begin()
    sibling_in = links.send(frames, frames_all.at[me], links.sibling)
    for copy in small_in:
        copy.wait_recv()
    mine.wait()
    small_far = [
        links.send(small_all.at[me], small_all.at[me], device)
        for device in (links.sibling, links.across, links.corner)
    ]
    corner_in = []
    waiting = list(steps)
    for piece in range(pieces):
        across_in[piece].wait_recv()
        cut = pl.ds(piece * rows, rows)
        place = frames_all.at[me ^ 2, cut]
        corner_in.append(links.send(place, place, links.sibling))
        share = -(-len(waiting) // (pieces - piece))
        for step in waiting[:share]:
            step()
        waiting = waiting[share:]
    sibling_in.wait_recv()
    for copy in corner_in + small_far:
        copy.wait_recv()
    end()
    local.wait()
    links.finish()


def gather_inputs(num_dp, frames, shard, small):
    pieces = 3
    count = spread_count(num_dp, 2) + num_dp - 1 + 3 + 1 + 2 * pieces
    any_spec = pl.BlockSpec(memory_space=pl.ANY)
    return pl.pallas_call(
        functools.partial(gather_kernel, num_dp, pieces),
        out_shape=(
            jax.ShapeDtypeStruct((4, *frames.shape), BF),
            jax.ShapeDtypeStruct((num_dp, *shard.shape), BF),
            jax.ShapeDtypeStruct((4, num_dp, *small.shape), F32),
        ),
        in_specs=[any_spec] * 3,
        out_specs=[any_spec] * 3,
        scratch_shapes=[
            pltpu.SemaphoreType.DMA((count,)),
            pltpu.SemaphoreType.DMA((count,)),
            pltpu.SemaphoreType.DMA((3,)),
        ],
        compiler_params=pltpu.CompilerParams(
            collective_id=0, has_side_effects=True, vmem_limit_bytes=4 << 20
        ),
        name="gather_inputs",
    )(frames, shard, small)


class RowSum:
    def __init__(self, links, part, side, home, far, staged, chunks):
        self.links, self.part, self.chunks = links, part, chunks
        self.side, self.home, self.far, self.staged = side, home, far, staged
        self.rows = part.shape[1] // chunks
        self.side_in, self.home_in, self.far_in = [], [], []

    def cut(self, chunk):
        return pl.ds(chunk * self.rows, self.rows)

    def begin(self):
        links, me = self.links, self.links.tensor
        for chunk in range(self.chunks):
            cut = self.cut(chunk)
            self.side_in.append(links.send(self.part.at[me ^ 3, cut], self.side.at[cut], links.sibling))
        for chunk in range(self.chunks):
            cut = self.cut(chunk)
            self.home_in.append(links.send(self.part.at[me ^ 1, cut], self.home.at[cut], links.sibling))

    def pass_on(self, chunk):
        links, cut = self.links, self.cut(chunk)
        self.side_in[chunk].wait_recv()
        total = self.part[links.tensor ^ 2, cut, :].astype(F32) + self.side[cut, :].astype(F32)
        self.staged[cut, :] = total.astype(BF)
        self.far_in.append(links.send(self.staged.at[cut], self.far.at[cut], links.across))

    def total(self, chunk):
        cut = self.cut(chunk)
        self.home_in[chunk].wait_recv()
        self.far_in[chunk].wait_recv()
        return (
            self.part[self.links.tensor, cut, :].astype(F32)
            + self.home[cut, :].astype(F32)
            + self.far[cut, :].astype(F32)
        )


class RowSpread:
    def __init__(self, links, own, gathered, local_sem, chunks):
        self.links, self.own, self.gathered, self.local_sem = links, own, gathered, local_sem
        self.chunks, self.rows = chunks, own.shape[0] // chunks
        self.across_in, self.waits = [], []

    def cut(self, chunk):
        return pl.ds(chunk * self.rows, self.rows)

    def give(self, chunk):
        links, cut = self.links, self.cut(chunk)
        place = self.gathered.at[links.tensor, cut]
        self.across_in.append(links.send(self.own.at[cut], place, links.across))
        self.waits.append(links.send(self.own.at[cut], place, links.sibling))

    def hand_over(self, chunk):
        links, cut = self.links, self.cut(chunk)
        self.across_in[chunk].wait_recv()
        place = self.gathered.at[links.tensor ^ 2, cut]
        self.waits.append(links.send(place, place, links.sibling))

    def end(self):
        local = pltpu.make_async_copy(self.own, self.gathered.at[self.links.tensor], self.local_sem)
        local.start()
        for copy in self.waits:
            copy.wait_recv()
        local.wait()


def dp_peers(links):
    return [(links.far(step), links.tensor) for step in range(1, links.num_far)] + [links.beside]


def middle_kernel(num_dp, chunks, part, frames, vecs, shard_a, shard_b, middle, normed_all, full_a, full_b, side, home, far, staged, own, send_sems, recv_sems, local_sems):
    links = Links(num_dp, send_sems, recv_sems)
    links.greet(dp_peers(links) + [links.sibling, links.across])
    sums = RowSum(links, part, side, home, far, staged, chunks)
    spread = RowSpread(links, own, normed_all, local_sems.at[2], chunks)
    sums.begin()
    begin_a, steps_a, end_a = weight_spread(links, local_sems.at[0], shard_a, full_a, 2)
    begin_b, steps_b, end_b = weight_spread(links, local_sems.at[1], shard_b, full_b, 2)
    begin_a()
    begin_b()
    waiting = steps_a + steps_b
    for chunk in range(chunks):
        sums.pass_on(chunk)
    slots = 2 * chunks
    for slot in range(slots):
        if slot < chunks:
            cut = sums.cut(slot)
            row = frames[cut, :].astype(F32) + (sums.total(slot) + vecs[2:3, :])
            middle[cut, :] = row
            own[cut, :] = layer_norm(row, vecs[0:1, :], vecs[1:2, :]).astype(BF)
            spread.give(slot)
        else:
            spread.hand_over(slot - chunks)
        share = -(-len(waiting) // (slots - slot))
        for step in waiting[:share]:
            step()
        waiting = waiting[share:]
    spread.end()
    end_a()
    end_b()
    links.finish()


def middle_rows(num_dp, part, frames, vecs, shard_a, shard_b):
    chunks = 3
    count = 2 * spread_count(num_dp, 2) + 6 * chunks
    any_spec = pl.BlockSpec(memory_space=pl.ANY)
    vmem_spec = pl.BlockSpec(memory_space=pltpu.VMEM)
    block = frames.shape
    return pl.pallas_call(
        functools.partial(middle_kernel, num_dp, chunks),
        out_shape=(
            jax.ShapeDtypeStruct(block, F32),
            jax.ShapeDtypeStruct((4, *block), BF),
            jax.ShapeDtypeStruct((num_dp, *shard_a.shape), BF),
            jax.ShapeDtypeStruct((num_dp, *shard_b.shape), BF),
        ),
        in_specs=[vmem_spec, vmem_spec, vmem_spec, any_spec, any_spec],
        out_specs=[vmem_spec, any_spec, any_spec, any_spec],
        scratch_shapes=[pltpu.VMEM(block, BF)] * 5
        + [
            pltpu.SemaphoreType.DMA((count,)),
            pltpu.SemaphoreType.DMA((count,)),
            pltpu.SemaphoreType.DMA((3,)),
        ],
        compiler_params=pltpu.CompilerParams(
            collective_id=1, has_side_effects=True, vmem_limit_bytes=32 << 20
        ),
        name="middle_rows",
    )(part, frames, vecs, shard_a, shard_b)


class GradScatter:
    def __init__(self, links, grads, beside, staged, landed, result):
        self.links, self.grads, self.beside = links, grads, beside
        self.staged, self.landed, self.result = staged, landed, result
        self.beside_in, self.far_in = {}, {}

    def begin(self):
        links = self.links
        for step in range(1, links.num_far + 1):
            at = step % links.num_far
            target = links.far(at) ^ 1
            self.beside_in[at] = links.send(self.grads.at[target], self.beside.at[at], links.beside)

    def pass_on(self, step):
        links = self.links
        self.beside_in[step].wait_recv()
        target = links.far(step)
        total = self.grads[target].astype(F32) + self.beside[step].astype(F32)
        self.staged[step] = total.astype(BF)
        self.far_in[step] = links.send(
            self.staged.at[step], self.landed.at[step], (target, links.tensor)
        )

    def end(self):
        links = self.links
        self.beside_in[0].wait_recv()
        total = self.grads[links.dp].astype(F32) + self.beside[0].astype(F32)
        for step in range(1, links.num_far):
            self.far_in[step].wait_recv()
            total = total + self.landed[step].astype(F32)
        self.result[...] = total

    def steps(self):
        return [functools.partial(self.pass_on, step) for step in range(1, self.links.num_far)]


def scatter_count(num_dp):
    return 2 * (num_dp // 2) - 1


def scatter_scratch(num_dp, grads):
    return [pltpu.VMEM((num_dp // 2, *grads.shape[1:]), BF)] * 3


def layer_norm_back(row, grad, gain):
    mean = jnp.mean(row, axis=-1, keepdims=True)
    centred = row - mean
    scale = lax.rsqrt(jnp.mean(centred * centred, axis=-1, keepdims=True) + 1e-05)
    unit = centred * scale
    scaled = grad * gain
    back = scale * (
        scaled
        - jnp.mean(scaled, axis=-1, keepdims=True)
        - unit * jnp.mean(scaled * unit, axis=-1, keepdims=True)
    )
    return back, unit


def turn_kernel(num_dp, chunks, part, middle_in, cotangent, vecs, grads_a, grads_b, grad_middle, attended_all, result_a, result_b, sums_out, side, home, far, staged, own, beside_a, staged_a, landed_a, beside_b, staged_b, landed_b, send_sems, recv_sems, local_sems):
    links = Links(num_dp, send_sems, recv_sems)
    links.greet(dp_peers(links) + [links.sibling, links.across])
    sums = RowSum(links, part, side, home, far, staged, chunks)
    spread = RowSpread(links, own, attended_all, local_sems.at[0], chunks)
    sums.begin()
    scatter_a = GradScatter(links, grads_a, beside_a, staged_a, landed_a, result_a)
    scatter_b = GradScatter(links, grads_b, beside_b, staged_b, landed_b, result_b)
    scatter_a.begin()
    scatter_b.begin()
    waiting = scatter_a.steps() + scatter_b.steps()
    for chunk in range(chunks):
        sums.pass_on(chunk)
    sums_out[...] = jnp.zeros_like(sums_out)
    slots = 2 * chunks
    for slot in range(slots):
        if slot < chunks:
            cut = sums.cut(slot)
            grad = sums.total(slot)
            back, unit = layer_norm_back(middle_in[cut, :], grad, vecs[0:1, :])
            given = cotangent[cut, :].astype(F32)
            row = given + back
            grad_middle[cut, :] = row
            low = row.astype(BF)
            own[cut, :] = low
            spread.give(slot)
            sums_out[0:1, :] += jnp.sum(grad * unit, axis=0, keepdims=True)
            sums_out[1:2, :] += jnp.sum(grad, axis=0, keepdims=True)
            sums_out[2:3, :] += jnp.sum(low.astype(F32), axis=0, keepdims=True)
            sums_out[3:4, :] += jnp.sum(given, axis=0, keepdims=True)
        else:
            spread.hand_over(slot - chunks)
        share = -(-len(waiting) // (slots - slot))
        for step in waiting[:share]:
            step()
        waiting = waiting[share:]
    spread.end()
    scatter_a.end()
    scatter_b.end()
    links.finish()


def turn_rows(num_dp, part, middle, cotangent, vecs, grads_a, grads_b):
    chunks = 3
    count = 2 * scatter_count(num_dp) + 6 * chunks
    any_spec = pl.BlockSpec(memory_space=pl.ANY)
    vmem_spec = pl.BlockSpec(memory_space=pltpu.VMEM)
    block = middle.shape
    return pl.pallas_call(
        functools.partial(turn_kernel, num_dp, chunks),
        out_shape=(
            jax.ShapeDtypeStruct(block, F32),
            jax.ShapeDtypeStruct((4, *block), BF),
            jax.ShapeDtypeStruct(grads_a.shape[1:], F32),
            jax.ShapeDtypeStruct(grads_b.shape[1:], F32),
            jax.ShapeDtypeStruct((8, block[1]), F32),
        ),
        in_specs=[vmem_spec] * 6,
        out_specs=[vmem_spec, any_spec, vmem_spec, vmem_spec, vmem_spec],
        scratch_shapes=[pltpu.VMEM(block, BF)] * 5
        + scatter_scratch(num_dp, grads_a)
        + scatter_scratch(num_dp, grads_b)
        + [
            pltpu.SemaphoreType.DMA((count,)),
            pltpu.SemaphoreType.DMA((count,)),
            pltpu.SemaphoreType.DMA((1,)),
        ],
        compiler_params=pltpu.CompilerParams(
            collective_id=2, has_side_effects=True, vmem_limit_bytes=48 << 20
        ),
        name="turn_rows",
    )(part, middle, cotangent, vecs, grads_a, grads_b)


def last_kernel(num_dp, chunks, part, frames, grad_middle, vecs, grads, small, sums_in, grad_frames, result, small_sum, side, home, far, staged, beside, staged_g, landed, small_group, small_mine, small_all, send_sems, recv_sems):
    links = Links(num_dp, send_sems, recv_sems)
    others = [lax.rem(links.dp + step, num_dp) for step in range(1, num_dp)]
    links.greet(
        [(other, links.tensor) for other in others] + [links.sibling, links.across, links.corner]
    )
    sums = RowSum(links, part, side, home, far, staged, chunks)
    sums.begin()
    scatter = GradScatter(links, grads, beside, staged_g, landed, result)
    scatter.begin()
    waiting = scatter.steps()
    for chunk in range(chunks):
        sums.pass_on(chunk)
    small_mine[0, 0:8, :] = jnp.zeros_like(small_mine[0, 0:8, :])
    small_mine[0, 2:6, :] = sums_in[0:4, :]
    small_mine[1] = small[...]
    for slot in range(chunks):
        cut = sums.cut(slot)
        grad = sums.total(slot)
        back, unit = layer_norm_back(frames[cut, :].astype(F32), grad, vecs[0:1, :])
        grad_frames[cut, :] = grad_middle[cut, :] + back
        small_mine[0, 0:1, :] += jnp.sum(grad * unit, axis=0, keepdims=True)
        small_mine[0, 1:2, :] += jnp.sum(grad, axis=0, keepdims=True)
        share = -(-len(waiting) // (chunks - slot))
        for step in waiting[:share]:
            step()
        waiting = waiting[share:]
    group_in = [
        links.send(small_mine.at[0], small_group.at[at], device)
        for at, device in enumerate((links.sibling, links.across, links.corner))
    ]
    for copy in group_in:
        copy.wait_recv()
        copy.wait_send()
    small_mine[0] = small_mine[0] + small_group[0] + small_group[1] + small_group[2]
    all_in = [
        links.send(small_mine, small_all.at[at], (other, links.tensor))
        for at, other in enumerate(others)
    ]
    scatter.end()
    total = small_mine[...]
    for at, copy in enumerate(all_in):
        copy.wait_recv()
        total = total + small_all[at]
    small_sum[...] = total
    for made in links.started:
        if not any(made is copy for copy in group_in):
            made.wait_send()


def last_rows(num_dp, part, frames, grad_middle, vecs, grads, small, sums_in):
    chunks = 3
    count = scatter_count(num_dp) + 3 * chunks + 3 + num_dp - 1
    vmem_spec = pl.BlockSpec(memory_space=pltpu.VMEM)
    block = frames.shape
    width = block[1]
    return pl.pallas_call(
        functools.partial(last_kernel, num_dp, chunks),
        out_shape=(
            jax.ShapeDtypeStruct(block, F32),
            jax.ShapeDtypeStruct(grads.shape[1:], F32),
            jax.ShapeDtypeStruct((2, 8, width), F32),
        ),
        in_specs=[vmem_spec] * 7,
        out_specs=[vmem_spec] * 3,
        scratch_shapes=[pltpu.VMEM(block, BF)] * 4
        + scatter_scratch(num_dp, grads)
        + [
            pltpu.VMEM((3, 8, width), F32),
            pltpu.VMEM((2, 8, width), F32),
            pltpu.VMEM((num_dp - 1, 2, 8, width), F32),
            pltpu.SemaphoreType.DMA((count,)),
            pltpu.SemaphoreType.DMA((count,)),
        ],
        compiler_params=pltpu.CompilerParams(
            collective_id=3, has_side_effects=True, vmem_limit_bytes=48 << 20
        ),
        name="last_rows",
    )(part, frames, grad_middle, vecs, grads, small, sums_in)


def attention_forward(query, keys_all, values_all, doc_ids):
    seq_length, heads_width = query.shape
    local_heads = heads_width // HD
    block_rows = min(512, seq_length)
    num_blocks = seq_length // block_rows
    query = query.reshape(seq_length, local_heads, HD)
    keys_all = keys_all.reshape(seq_length, local_heads, HD)
    values_all = values_all.reshape(seq_length, local_heads, HD)

    def forward_block(block_index):
        block_start = block_index * block_rows
        query_block = lax.dynamic_slice_in_dim(query, block_start, block_rows, 0)
        doc_block = lax.dynamic_slice_in_dim(doc_ids, block_start, block_rows, 0)
        raw_scores = contract("qhe,khe->hqk", query_block, keys_all) * 0.125
        scores = jnp.where((doc_block[:, None] == doc_ids[None, :])[None], raw_scores, -1e30)
        row_max = jnp.max(scores, axis=-1, keepdims=True)
        exp_scores = jnp.exp(scores - row_max)
        row_total = jnp.sum(exp_scores, axis=-1, keepdims=True)
        attn_probs = (exp_scores / row_total).astype(BF)
        block_mixed = contract("hqk,khe->qhe", attn_probs, values_all)
        log_total = (row_max + jnp.log(row_total))[..., 0]
        return (block_mixed.astype(BF).reshape(block_rows, heads_width), log_total)

    mixed_blocks, log_totals = lax.map(forward_block, jnp.arange(num_blocks, dtype=jnp.int32))
    return mixed_blocks.reshape(seq_length, heads_width), log_totals


def attention_backward(query, keys_all, values_all, doc_ids, log_totals, grad_mixed):
    seq_length, heads_width = query.shape
    local_heads = heads_width // HD
    block_rows = min(512, seq_length)
    num_blocks = seq_length // block_rows
    query = query.reshape(seq_length, local_heads, HD)
    keys_all = keys_all.reshape(seq_length, local_heads, HD)
    values_all = values_all.reshape(seq_length, local_heads, HD)
    grad_mixed = grad_mixed.reshape(seq_length, local_heads, HD)

    def backward_block(carried, block_index):
        grad_keys_acc, grad_values_acc = carried
        block_start = block_index * block_rows
        query_block = lax.dynamic_slice_in_dim(query, block_start, block_rows, 0)
        doc_block = lax.dynamic_slice_in_dim(doc_ids, block_start, block_rows, 0)
        grad_block = lax.dynamic_slice_in_dim(grad_mixed, block_start, block_rows, 0)
        raw_scores = contract("qhe,khe->hqk", query_block, keys_all) * 0.125
        scores = jnp.where((doc_block[:, None] == doc_ids[None, :])[None], raw_scores, -1e30)
        attn_probs = jnp.exp(scores - log_totals[block_index][..., None])
        grad_probs = contract("qhe,khe->hqk", grad_block, values_all)
        row_inner = jnp.sum(attn_probs * grad_probs, axis=-1, keepdims=True)
        grad_scores = (attn_probs * (grad_probs - row_inner)).astype(BF)
        grad_query_block = contract("hqk,khe->qhe", grad_scores, keys_all) * 0.125
        grad_keys_acc = grad_keys_acc + contract("hqk,qhe->khe", grad_scores, query_block) * 0.125
        grad_values_acc = grad_values_acc + contract(
            "hqk,qhe->khe", attn_probs.astype(BF), grad_block
        )
        return ((grad_keys_acc, grad_values_acc), grad_query_block)

    empty_acc = jnp.zeros((seq_length, local_heads, HD), F32)
    (grad_keys_all, grad_values_all), grad_query_blocks = lax.scan(
        backward_block, (empty_acc, empty_acc), jnp.arange(num_blocks, dtype=jnp.int32)
    )
    return jnp.concatenate(
        [
            grad_query_blocks.reshape(seq_length, heads_width),
            grad_keys_all.reshape(seq_length, heads_width),
            grad_values_all.reshape(seq_length, heads_width),
        ],
        axis=1,
    ).astype(BF)


def on_device(
    num_dp,
    frames,
    segments,
    norm1_gain,
    norm1_shift,
    in_weight,
    proj_bias,
    out_weight,
    out_bias,
    norm2_gain,
    norm2_shift,
    fc1_weight,
    fc1_bias,
    fc2_weight,
    fc2_bias,
    cotangent,
):
    width = frames.shape[1]
    heads_width = in_weight.shape[2]
    local_heads = heads_width // HD
    doc_ids = segments[0]
    seq_length = doc_ids.shape[0]
    slab = in_weight.shape[0]
    own_vecs = norm1_gain.shape[0]
    bias_part, fc1b_part = proj_bias.size, fc1_bias.size

    cot_all = lax.all_gather(cotangent, "tensor", axis=0, tiled=True)

    shard_a = jnp.concatenate([in_weight.reshape(slab, 3 * heads_width), out_weight.T], axis=1)
    small = jnp.concatenate(
        [norm1_gain, norm1_shift, norm2_gain, norm2_shift, out_bias, fc2_bias]
        + [proj_bias.astype(F32).reshape(-1), fc1_bias.astype(F32).reshape(-1)]
    )
    small_len = small.shape[0]
    padded = -(-small_len // 1024) * 1024
    small = jnp.pad(small, (0, padded - small_len)).reshape(padded // 128, 128)
    frames_all, full_a, small_all = gather_inputs(num_dp, frames, shard_a, small)
    small_flat = small_all.reshape(4, num_dp, padded)
    vecs = (
        small_flat[:, :, : 6 * own_vecs]
        .reshape(4, num_dp, 6, own_vecs)
        .transpose(2, 1, 0, 3)
        .reshape(6, width)
    )
    gain_one, shift_one, gain_two, shift_two, bias_out, bias_fc2 = vecs
    local_small = lax.dynamic_index_in_dim(
        small_flat, lax.axis_index("tensor"), 0, keepdims=False
    )
    bias_pair = (
        local_small[:, 6 * own_vecs : 6 * own_vecs + bias_part]
        .reshape(num_dp, 2, local_heads, HD // num_dp)
        .transpose(1, 2, 0, 3)
        .reshape(2, heads_width)
    )
    fc1b_full = (
        local_small[:, 6 * own_vecs + bias_part : small_len]
        .reshape(num_dp, *fc1_bias.shape)
        .transpose(1, 0, 2)
        .reshape(-1)
    )
    full_a = full_a.reshape(width, 4 * heads_width)
    in_full, out_t = full_a[:, : 3 * heads_width], full_a[:, 3 * heads_width :]

    rows_all = frames_all.reshape(seq_length, width).astype(F32)
    normed_all = layer_norm(rows_all, gain_one, shift_one).astype(BF)
    projected = jnp.dot(normed_all, in_full, preferred_element_type=F32)
    query = (projected[:, :heads_width] + bias_pair[0]).astype(BF)
    keys_all = projected[:, heads_width : 2 * heads_width].astype(BF)
    values_all = (projected[:, 2 * heads_width :] + bias_pair[1]).astype(BF)
    attn_mixed, log_totals = attention_forward(query, keys_all, values_all, doc_ids)
    part = contract("lh,dh->ld", attn_mixed, out_t).astype(BF).reshape(4, -1, width)

    vecs_two = jnp.pad(jnp.stack([gain_two, shift_two, bias_out]), ((0, 5), (0, 0)))
    middle, normed_two, fc1_full, fc2_t = middle_rows(
        num_dp, part, frames, vecs_two, fc1_weight, fc2_weight.T
    )
    normed_two = normed_two.reshape(seq_length, width)
    fc1_full = fc1_full.reshape(width, -1)
    fc2_t = fc2_t.reshape(width, -1)

    hidden = jnp.dot(normed_two, fc1_full, preferred_element_type=F32) + fc1b_full
    active = gelu_exact(hidden).astype(BF)
    branch_part = contract("lf,df->ld", active, fc2_t).astype(BF)
    grad_active = jnp.dot(cot_all, fc2_t, preferred_element_type=F32)
    grad_hidden = jax.vjp(gelu_exact, hidden)[1](grad_active)[0].astype(BF)
    grad_two_part = contract("lf,df->ld", grad_hidden, fc1_full).astype(BF).reshape(4, -1, width)
    grads_fc1 = contract("ld,lf->df", normed_two, grad_hidden).astype(BF)
    grads_fc2 = contract("ld,lf->df", cot_all, active).astype(BF)
    grads_fc1b = jnp.sum(grad_hidden.astype(F32), axis=0)
    branch = lax.psum_scatter(branch_part, "tensor", scatter_dimension=0, tiled=True)

    grad_middle, attended_all, g_fc1, g_fc2t, sums_two = turn_rows(
        num_dp,
        grad_two_part,
        middle,
        cotangent,
        vecs_two,
        grads_fc1.reshape(num_dp, slab, -1),
        grads_fc2.reshape(num_dp, slab, -1),
    )
    attended_all = attended_all.reshape(seq_length, width)
    grads_out = contract("ld,lh->dh", attended_all, attn_mixed)
    grad_mixed = jnp.dot(attended_all, out_t, preferred_element_type=F32).astype(BF)
    grad_proj = attention_backward(
        query, keys_all, values_all, doc_ids, log_totals, grad_mixed
    )
    proj_sums = jnp.sum(grad_proj.astype(F32), axis=0)
    grads_in = contract("ld,lf->df", normed_all, grad_proj)
    grad_one_part = contract("lf,df->ld", grad_proj, in_full).astype(BF).reshape(4, -1, width)
    grads_a = jnp.concatenate([grads_in, grads_out], axis=1).astype(BF)
    small_grads = jnp.concatenate(
        [proj_sums[:heads_width], proj_sums[2 * heads_width :], grads_fc1b]
    )
    small_rows = -(-small_grads.shape[0] // width)
    small_grads = jnp.pad(small_grads, (0, 8 * width - small_grads.shape[0])).reshape(8, width)
    vecs_one = jnp.pad(gain_one[None], ((0, 7), (0, 0)))
    grad_frames, g_a, small_sum = last_rows(
        num_dp,
        grad_one_part,
        frames,
        grad_middle,
        vecs_one,
        grads_a.reshape(num_dp, slab, -1),
        small_grads,
        sums_two,
    )
    output = (middle + (branch.astype(F32) + bias_fc2)).astype(BF)
    dp, tensor = lax.axis_index("dp"), lax.axis_index("tensor")
    at = (dp * 4 + tensor) * own_vecs
    mine = lax.dynamic_slice(small_sum[0], (0, at), (8, own_vecs))
    small_flat = small_sum[1].reshape(-1)
    proj_grad = small_flat[: 2 * heads_width].reshape(2, local_heads, num_dp, HD // num_dp)
    g_proj = lax.dynamic_index_in_dim(proj_grad, dp, 2, keepdims=False)
    fc1b_grad = small_flat[2 * heads_width : 2 * heads_width + fc1b_full.shape[0]]
    fc1b_grad = fc1b_grad.reshape(fc1_bias.shape[0], num_dp, fc1_bias.shape[1])
    g_fc1b = lax.dynamic_index_in_dim(fc1b_grad, dp, 1, keepdims=False)
    g_in = g_a[:, : 3 * heads_width].reshape(slab, 3, heads_width)
    g_out = g_a[:, 3 * heads_width :].T
    return (
        output,
        grad_frames,
        mine[0],
        mine[1],
        g_in,
        g_proj,
        g_out,
        mine[4],
        mine[2],
        mine[3],
        g_fc1,
        g_fc1b,
        g_fc2t.T,
        mine[5],
    )


def solution(mesh):
    in_specs = (
        P(("dp", "tensor"), None),
        P("dp", None),
        P(("dp", "tensor")),
        P(("dp", "tensor")),
        P("dp", None, "tensor"),
        P(None, "tensor", "dp"),
        P("tensor", "dp"),
        P(("dp", "tensor")),
        P(("dp", "tensor")),
        P(("dp", "tensor")),
        P("dp", "tensor"),
        P("tensor", "dp"),
        P("tensor", "dp"),
        P(("dp", "tensor")),
        P(("dp", "tensor"), None),
    )
    out_specs = (
        P(("dp", "tensor"), None),
        P(("dp", "tensor"), None),
        P(("dp", "tensor")),
        P(("dp", "tensor")),
        P("dp", None, "tensor"),
        P(None, "tensor", "dp"),
        P("tensor", "dp"),
        P(("dp", "tensor")),
        P(("dp", "tensor")),
        P(("dp", "tensor")),
        P("dp", "tensor"),
        P("tensor", "dp"),
        P("tensor", "dp"),
        P(("dp", "tensor")),
    )
    return jax.shard_map(
        functools.partial(on_device, mesh.shape["dp"]),
        mesh=mesh,
        in_specs=in_specs,
        out_specs=out_specs,
        check_vma=False,
    )
```

```python
import functools

import jax
import jax.numpy as jnp
from jax import lax
from jax.experimental import pallas as pl
from jax.experimental.pallas import tpu as pltpu
from jax.sharding import PartitionSpec as P

HD = 64
BF = jnp.bfloat16
F32 = jnp.float32
VMEM_BYTES = 62 << 20
BLOCK = 256
CHUNKS = 3
LANE_GAP = 256


def layer_norm(row_block, norm_gain, norm_shift):
    row_mean = jnp.mean(row_block, axis=-1, keepdims=True)
    centred = row_block - row_mean
    row_var = jnp.mean(centred * centred, axis=-1, keepdims=True)
    return centred * lax.rsqrt(row_var + 1e-05) * norm_gain + norm_shift


def layer_norm_back(row, grad, gain):
    mean = jnp.mean(row, axis=-1, keepdims=True)
    centred = row - mean
    scale = lax.rsqrt(jnp.mean(centred * centred, axis=-1, keepdims=True) + 1e-05)
    unit = centred * scale
    scaled = grad * gain
    back = scale * (
        scaled
        - jnp.mean(scaled, axis=-1, keepdims=True)
        - unit * jnp.mean(scaled * unit, axis=-1, keepdims=True)
    )
    return back, unit


def dot_nn(left, right):
    return jnp.dot(left, right, preferred_element_type=F32)


def dot_nt(left, right):
    return lax.dot_general(left, right, (((1,), (1,)), ((), ())), preferred_element_type=F32)


def dot_tn(left, right):
    return lax.dot_general(left, right, (((0,), (0,)), ((), ())), preferred_element_type=F32)


def column_sum(block):
    return jnp.sum(block, axis=0, keepdims=True)


def head_part(block, head):
    lanes = lax.broadcasted_iota(jnp.int32, block.shape, 1)
    inside = (lanes >= head * HD) & (lanes < (head + 1) * HD)
    return jnp.where(inside, block, jnp.zeros_like(block))


def rows_at(start, size):
    return pl.ds(pl.multiple_of(start, 128), size)


class Links:
    def __init__(self, num_dp, send_sems, recv_sems):
        self.num_dp, self.num_far = num_dp, num_dp // 2
        self.dp, self.tensor = lax.axis_index("dp"), lax.axis_index("tensor")
        self.send_sems, self.recv_sems, self.made, self.done = send_sems, recv_sems, [], []
        self.sibling = (self.dp, self.tensor ^ 1)
        self.across = (self.dp, self.tensor ^ 2)
        self.corner = (self.dp, self.tensor ^ 3)
        self.beside = (self.dp ^ 1, self.tensor)
        self.others = [(lax.rem(self.dp + step, num_dp), self.tensor) for step in range(1, num_dp)]

    def far(self, step):
        return lax.rem(self.dp + 2 * step, self.num_dp)

    def far_from(self, step):
        return lax.rem(self.dp + self.num_dp - 2 * step, self.num_dp)

    def copy(self, src, dst, device):
        at = len(self.made)
        made = pltpu.make_async_remote_copy(
            src_ref=src,
            dst_ref=dst,
            send_sem=self.send_sems.at[at],
            recv_sem=self.recv_sems.at[at],
            device_id=device,
            device_id_type=pl.DeviceIdType.MESH,
        )
        self.made.append(made)
        return made

    def greet(self, devices):
        barrier = pltpu.get_barrier_semaphore()
        for device in devices:
            pl.semaphore_signal(
                barrier, inc=1, device_id=device, device_id_type=pl.DeviceIdType.MESH
            )
        pl.semaphore_wait(barrier, len(devices))

    def sent(self, copies):
        for made in copies:
            made.wait_send()
            self.done.append(made)

    def finish(self):
        for made in self.made:
            if not any(made is other for other in self.done):
                made.wait_send()


class WeightSpread:
    def __init__(self, links, shard, full, halves):
        self.links, self.shard, self.full, self.halves = links, shard, full, halves
        columns = shard.shape[-1] // halves

        def part(ref, half):
            return ref.at[:, pl.ds(half * columns, columns)]

        def place(origin, half):
            return full.at[origin, :, pl.ds(half * columns, columns)]

        self.first, self.second = {}, {}
        for half in range(halves):
            for step in range(1, links.num_far):
                self.first[half, step] = links.copy(
                    part(shard, half), place(links.dp, half), (links.far(step), links.tensor)
                )
            self.second[half, 0] = links.copy(
                part(shard, half), place(links.dp, half), links.beside
            )
            for step in range(1, links.num_far):
                spot = place(links.far_from(step), half)
                self.second[half, step] = links.copy(spot, spot, links.beside)

    def begin(self):
        for made in self.first.values():
            made.start()
        for half in range(self.halves):
            self.second[half, 0].start()
        self.full[self.links.dp] = self.shard[...]

    def forward(self, half):
        for step in range(1, self.links.num_far):
            self.first[half, step].wait_recv()
            self.second[half, step].start()

    def end(self):
        for made in self.second.values():
            made.wait_recv()


class RowSum:
    def __init__(self, links, part, side, home, far):
        self.links, self.part = links, part
        self.side, self.home, self.far = side, home, far
        self.block = part.shape[0] // 4
        self.rows = self.block // CHUNKS
        me = links.tensor
        cuts = [self.cut(chunk) for chunk in range(CHUNKS)]
        self.side_in = [
            links.copy(part.at[self.of(me ^ 3, chunk)], side.at[cuts[chunk]], links.sibling)
            for chunk in range(CHUNKS)
        ]
        self.home_in = [
            links.copy(part.at[self.of(me ^ 1, chunk)], home.at[cuts[chunk]], links.sibling)
            for chunk in range(CHUNKS)
        ]
        self.far_in = [
            links.copy(side.at[cuts[chunk]], far.at[cuts[chunk]], links.across)
            for chunk in range(CHUNKS)
        ]

    def cut(self, chunk):
        return pl.ds(chunk * self.rows, self.rows)

    def of(self, member, chunk):
        return rows_at(member * self.block + chunk * self.rows, self.rows)

    def begin_side(self):
        for made in self.side_in:
            made.start()

    def begin_home(self):
        for made in self.home_in:
            made.start()

    def pass_on(self, chunk):
        cut = self.cut(chunk)
        self.side_in[chunk].wait_recv()
        mine = self.part[self.of(self.links.tensor ^ 2, chunk), :]
        self.side[cut, :] = (mine.astype(F32) + self.side[cut, :].astype(F32)).astype(BF)
        self.far_in[chunk].start()

    def total(self, chunk):
        cut = self.cut(chunk)
        self.home_in[chunk].wait_recv()
        self.far_in[chunk].wait_recv()
        return (
            self.part[self.of(self.links.tensor, chunk), :].astype(F32)
            + self.home[cut, :].astype(F32)
            + self.far[cut, :].astype(F32)
        )


class RowSpread:
    def __init__(self, links, own, gathered):
        self.block = own.shape[0]
        self.rows = self.block // CHUNKS
        self.own, self.gathered, self.links = own, gathered, links
        me = links.tensor
        self.across_in, self.sibling_in, self.corner_in = [], [], []
        for chunk in range(CHUNKS):
            source, place = own.at[self.cut(chunk)], gathered.at[self.of(me, chunk)]
            self.across_in.append(links.copy(source, place, links.across))
            self.sibling_in.append(links.copy(source, place, links.sibling))
        for chunk in range(CHUNKS):
            place = gathered.at[self.of(me ^ 2, chunk)]
            self.corner_in.append(links.copy(place, place, links.sibling))

    def cut(self, chunk):
        return pl.ds(chunk * self.rows, self.rows)

    def of(self, member, chunk):
        return rows_at(member * self.block + chunk * self.rows, self.rows)

    def give(self, chunk):
        self.across_in[chunk].start()
        self.sibling_in[chunk].start()
        self.gathered[self.of(self.links.tensor, chunk), :] = self.own[self.cut(chunk), :]

    def hand_over(self, chunk):
        self.across_in[chunk].wait_recv()
        self.corner_in[chunk].start()

    def await_sibling(self):
        for made in self.sibling_in:
            made.wait_recv()

    def await_corner(self):
        for made in self.corner_in:
            made.wait_recv()


class GradScatter:
    def __init__(self, links, grads, beside, landed, result):
        self.links, self.grads, self.beside = links, grads, beside
        self.landed, self.result = landed, result
        self.slab = beside.shape[1]
        self.beside_in, self.far_in = {}, {}
        for step in range(links.num_far):
            target = links.far(step)
            self.beside_in[step] = links.copy(
                grads.at[target ^ 1], beside.at[step], links.beside
            )
            if step:
                self.far_in[step] = links.copy(
                    beside.at[step], landed.at[step], (target, links.tensor)
                )

    def begin(self):
        for step in range(1, self.links.num_far + 1):
            self.beside_in[step % self.links.num_far].start()

    def pass_on(self, step):
        self.beside_in[step].wait_recv()
        mine = self.grads[self.links.far(step)]
        self.beside[step] = (mine.astype(F32) + self.beside[step].astype(F32)).astype(BF)
        self.far_in[step].start()

    def end(self):
        self.beside_in[0].wait_recv()
        total = self.grads[self.links.dp].astype(F32) + self.beside[0].astype(F32)
        for step in range(1, self.links.num_far):
            self.far_in[step].wait_recv()
            total = total + self.landed[step].astype(F32)
        self.result[...] = total


class Refs:
    def __init__(self, names, refs):
        for name, ref in zip(names, refs, strict=True):
            setattr(self, name, ref)


def flat_weight(full, wide):
    count, slab, width = full.shape
    if slab % 16 == 0:
        return full[...].reshape(count * slab, width)
    for at in range(count):
        wide[at * slab : (at + 1) * slab, :] = full[at].astype(F32)
    return wide[...].astype(BF)


def split_rows(value, grads, start, wide):
    count, slab, width = grads.shape
    rows = value.shape[0]
    if slab % 16 == 0:
        grads[pl.ds(start // slab, rows // slab)] = value.astype(BF).reshape(
            rows // slab, slab, width
        )
        return
    wide[0:rows, :] = value
    for at in range(rows // slab):
        grads[start // slab + at] = wide[at * slab : (at + 1) * slab, :].astype(BF)


def layer_kernel(num_dp, names, *refs):
    r = Refs(names, refs)
    links = Links(num_dp, r.send_sems, r.recv_sems)
    me, dp = links.tensor, links.dp
    block, width = r.frames.shape
    length = 4 * block
    num_blocks = length // BLOCK
    heads_width = width // 4
    heads = heads_width // HD
    qkv = 3 * heads_width
    upper = me // 2
    parts = 2 * CHUNKS

    links.greet(links.others + [links.sibling, links.across, links.corner])

    small_dp = [
        links.copy(r.small_mine, r.small_dp.at[at], other) for at, other in enumerate(links.others)
    ]
    small_group = [
        links.copy(r.small_sum, r.small_group.at[at], device)
        for at, device in enumerate((links.sibling, links.across, links.corner))
    ]
    frame_rows = RowSpread(links, r.frames, r.rows_all)
    given_rows = RowSpread(links, r.cotangent, r.given_all)
    spread_a = WeightSpread(links, r.shard_a, r.full_a, 2)
    spread_b = WeightSpread(links, r.shard_b, r.full_b, 2)
    spread_c = WeightSpread(links, r.shard_c, r.full_c, 2)

    placed = pltpu.roll(r.small[0:6, :], (dp * 4 + me) * (width // (4 * num_dp)), 1)
    r.small_mine[0:6, :] = placed
    r.small_mine[6:8, :] = pltpu.roll(r.small[6:8, :], dp * (HD // num_dp), 1)
    for made in small_dp:
        made.start()
    for chunk in range(CHUNKS):
        frame_rows.give(chunk)
    spread_a.begin()
    for chunk in range(CHUNKS):
        given_rows.give(chunk)
    spread_b.begin()
    spread_c.begin()

    ids = r.seg_row[0:1, :].astype(F32)
    r.seg_wide[...] = jnp.transpose(jnp.broadcast_to(ids, (128, length)))

    total = r.small_mine[...]
    for at, made in enumerate(small_dp):
        made.wait_recv()
        total = total + r.small_dp[at]
    r.small_sum[...] = total
    for made in small_group:
        made.start()
    for at, made in enumerate(small_group):
        made.wait_recv()
        total = total + jnp.where(
            lax.broadcasted_iota(jnp.int32, total.shape, 0) < 6, r.small_group[at], 0.0
        )
    r.vecs[...] = total
    gain_one, shift_one, gain_two, shift_two, bias_out, bias_fc2 = range(6)

    def vec(at):
        return r.vecs[at : at + 1, :]

    for chunk in range(CHUNKS):
        frame_rows.hand_over(chunk)
    spread_a.forward(0)
    spread_a.forward(1)
    frame_rows.await_sibling()
    frame_rows.await_corner()
    spread_a.end()
    links.sent(frame_rows.corner_in)

    @pl.loop(0, num_blocks)
    def project(at):
        rows = rows_at(at * BLOCK, BLOCK)
        low = layer_norm(
            r.rows_all[rows, :].astype(F32), vec(gain_one), vec(shift_one)
        ).astype(BF)
        r.normed[rows, :] = low
        made = dot_nn(low, flat_weight(r.full_a, r.wide)[:, :qkv])
        made_query = (made[:, :heads_width] + r.vecs[7:8, 0:heads_width]).astype(BF)
        r.query[rows, :] = made_query * jnp.asarray(0.125, BF)
        r.keys[rows, :] = made[:, heads_width : 2 * heads_width].astype(BF)
        shift = r.vecs[7:8, LANE_GAP : LANE_GAP + heads_width]
        made_values = (made[:, 2 * heads_width :] + shift).astype(BF)
        r.values[rows, :] = made_values
        r.turned[:, rows] = jnp.transpose(made_values)

    sum_one = RowSum(links, r.part_one, r.side_one, r.home_one, r.far_one)
    spread_two = RowSpread(links, r.normed_own, r.normed_two)

    @pl.loop(0, num_blocks)
    def attend(at):
        spot = lax.rem(at + (1 - upper) * (num_blocks // 2), num_blocks)
        rows = rows_at(spot * BLOCK, BLOCK)
        asked = r.query[rows, :]
        keys_ids = jnp.concatenate([r.seg_wide[...]] * (BLOCK // 128), axis=1)
        query_ids = r.seg_row[0:1, rows].astype(F32)
        r.mask[...] = jnp.where(keys_ids == query_ids, 0.0, -1e30)
        made = []
        for head in range(heads):
            scores = dot_nt(r.keys[...], head_part(asked, head)) + r.mask[...]
            top = jnp.max(scores, axis=0, keepdims=True)
            weights = jnp.exp(scores - top)
            whole = column_sum(weights)
            mixed = dot_nn(r.turned[head * HD : (head + 1) * HD, :], weights.astype(BF))
            made.append(mixed / whole)
            r.stats[spot, head : head + 1, :] = top + jnp.log(whole)
        out = jnp.transpose(jnp.concatenate(made, axis=0)).astype(BF)
        r.mixed[rows, :] = out
        r.part_one[rows, :] = dot_nt(out, flat_weight(r.full_a, r.wide)[:, qkv:]).astype(BF)

        @pl.when(at == 0)
        def early():
            given_rows.hand_over(0)
            spread_b.forward(0)

        @pl.when(at == 1)
        def second():
            given_rows.hand_over(1)
            given_rows.hand_over(2)

        @pl.when(at == 2)
        def third():
            sum_one.begin_side()
            spread_b.forward(1)

        @pl.when(at == 3)
        def fourth():
            for chunk in range(CHUNKS):
                sum_one.pass_on(chunk)

        @pl.when(at == 4)
        def fifth():
            spread_c.forward(0)

    sum_one.begin_home()
    spread_c.forward(1)
    for chunk in range(CHUNKS):
        cut = sum_one.cut(chunk)
        row = r.frames[cut, :].astype(F32) + (sum_one.total(chunk) + vec(bias_out))
        r.middle[cut, :] = row
        r.normed_own[cut, :] = layer_norm(row, vec(gain_two), vec(shift_two)).astype(BF)
        spread_two.give(chunk)
    links.sent(sum_one.far_in)
    given_rows.await_sibling()
    given_rows.await_corner()
    spread_b.end()
    spread_c.end()

    sum_two = RowSum(links, r.part_two, r.side_two, r.home_two, r.far_two)
    sum_three = RowSum(links, r.normed_two, r.side_three, r.home_three, r.far_three)
    r.small_grads[...] = jnp.zeros_like(r.small_grads)

    @pl.loop(0, 4)
    def feed(at):
        @pl.when(at == 1)
        def from_sibling():
            for chunk in range(CHUNKS):
                spread_two.hand_over(chunk)
            spread_two.await_sibling()

        @pl.when(at == 3)
        def from_corner():
            spread_two.await_corner()

        rows = rows_at((me ^ at) * block, block)
        fc1 = flat_weight(r.full_b, r.wide)
        hidden = dot_nn(r.normed_two[rows, :], fc1) + r.vecs[6:7, :]
        below = 0.5 + 0.5 * lax.erf(hidden * 0.7071067811865476)
        density = 0.3989422804014327 * jnp.exp(-0.5 * hidden * hidden)
        low = (hidden * below).astype(BF)
        r.active[rows, :] = low
        fc2_t = flat_weight(r.full_c, r.wide)
        grad_active = dot_nn(r.given_all[rows, :], fc2_t)
        back = (grad_active * (below + hidden * density)).astype(BF)
        r.grad_hidden[rows, :] = back
        r.part_two[rows, :] = dot_nt(back, flat_weight(r.full_b, r.wide)).astype(BF)
        r.small_grads[6:7, :] += column_sum(back.astype(F32))

    sum_two.begin_side()
    sum_two.begin_home()
    for chunk in range(CHUNKS):
        sum_two.pass_on(chunk)
    scatter_b = GradScatter(links, r.grads_b, r.beside_b, r.landed_b, r.out_b)
    scatter_c = GradScatter(links, r.grads_c, r.beside_c, r.landed_c, r.out_c)

    @pl.loop(0, width // block)
    def weigh(at):
        columns = rows_at(at * block, block)
        split_rows(
            dot_tn(r.normed_two[:, columns], r.grad_hidden[...]), r.grads_b, at * block, r.wide
        )
        split_rows(dot_tn(r.given_all[:, columns], r.active[...]), r.grads_c, at * block, r.wide)

    scatter_b.begin()
    scatter_c.begin()
    links.sent(spread_two.corner_in)

    @pl.loop(0, 4)
    def branch(at):
        rows = rows_at(at * block, block)
        made = dot_nt(r.active[rows, :], flat_weight(r.full_c, r.wide))
        r.normed_two[rows, :] = made.astype(BF)

    spread_three = RowSpread(links, r.attended_own, r.rows_all)
    for chunk in range(CHUNKS):
        cut = sum_two.cut(chunk)
        grad = sum_two.total(chunk)
        back, unit = layer_norm_back(r.middle[cut, :], grad, vec(gain_two))
        given = r.cotangent[cut, :].astype(F32)
        row = given + back
        r.grad_middle[cut, :] = row
        low = row.astype(BF)
        r.attended_own[cut, :] = low
        spread_three.give(chunk)
        r.small_grads[gain_two : gain_two + 1, :] += column_sum(grad * unit)
        r.small_grads[shift_two : shift_two + 1, :] += column_sum(grad)
        r.small_grads[bias_out : bias_out + 1, :] += column_sum(low.astype(F32))
        r.small_grads[bias_fc2 : bias_fc2 + 1, :] += column_sum(given)
    sum_three.begin_side()
    sum_three.begin_home()
    for step in range(1, links.num_far):
        scatter_b.pass_on(step)
    for chunk in range(CHUNKS):
        spread_three.hand_over(chunk)
    for chunk in range(CHUNKS):
        sum_three.pass_on(chunk)
    spread_three.await_sibling()
    spread_three.await_corner()

    @pl.loop(0, num_blocks)
    def prepare(at):
        rows = rows_at(at * BLOCK, BLOCK)
        low = dot_nn(r.rows_all[rows, :], flat_weight(r.full_a, r.wide)[:, qkv:]).astype(BF)
        r.grad_mixed[rows, :] = low
        r.turned[:, rows] = jnp.transpose(r.keys[rows, :])
        both = jnp.transpose(low.astype(F32) * r.mixed[rows, :].astype(F32))
        for head in range(heads):
            r.inner[at, head : head + 1, :] = column_sum(both[head * HD : (head + 1) * HD, :])

    for step in range(1, links.num_far):
        scatter_c.pass_on(step)
    r.grad_keys[...] = jnp.zeros_like(r.grad_keys)
    r.grad_values[...] = jnp.zeros_like(r.grad_values)

    @pl.loop(0, num_blocks)
    def attend_back(at):
        rows = rows_at(at * BLOCK, BLOCK)
        asked, given = r.query[rows, :], r.grad_mixed[rows, :]
        keys_ids = jnp.concatenate([r.seg_wide[...]] * (BLOCK // 128), axis=1)
        query_ids = r.seg_row[0:1, rows].astype(F32)
        r.mask[...] = jnp.where(keys_ids == query_ids, 0.0, -1e30)
        asked_heads = [head_part(asked, head) for head in range(heads)]
        given_heads = [head_part(given, head) for head in range(heads)]
        made = []
        for head in range(heads):
            lanes = slice(head * BLOCK, (head + 1) * BLOCK)
            scores = dot_nt(r.keys[...], asked_heads[head]) + r.mask[...]
            probs = jnp.exp(scores - r.stats[at, head : head + 1, :])
            slopes = dot_nt(r.values[...], given_heads[head]) - r.inner[at, head : head + 1, :]
            slopes = (probs * slopes).astype(BF)
            r.active[:, lanes] = probs.astype(BF)
            r.grad_hidden[:, lanes] = slopes
            made.append(dot_nn(r.turned[head * HD : (head + 1) * HD, :], slopes))
        r.grad_values[...] += dot_nn(r.active[...], jnp.concatenate(given_heads, axis=0))
        r.grad_keys[...] += dot_nn(r.grad_hidden[...], jnp.concatenate(asked_heads, axis=0))
        turned = jnp.transpose(jnp.concatenate(made, axis=0)) * 0.125
        r.grad_proj[rows, :heads_width] = turned.astype(BF)

    links.sent(sum_one.side_in + sum_one.home_in)
    sum_four = RowSum(links, r.part_one, r.side_one, r.home_one, r.far_one)

    @pl.loop(0, num_blocks)
    def project_back(at):
        spot = lax.rem(at + (1 - upper) * (num_blocks // 2), num_blocks)
        rows = rows_at(spot * BLOCK, BLOCK)
        low_keys = r.grad_keys[rows, :].astype(BF)
        low_values = r.grad_values[rows, :].astype(BF)
        low_query = r.grad_proj[rows, :heads_width]
        whole = jnp.concatenate([low_query, low_keys, low_values], axis=1)
        r.grad_proj[rows, :] = whole
        made = dot_nt(whole, flat_weight(r.full_a, r.wide)[:, :qkv])
        r.part_one[rows, :] = made.astype(BF)
        wide_sum = column_sum(whole.astype(F32))
        r.small_grads[7:8, 0:heads_width] += wide_sum[:, 0:heads_width]
        r.small_grads[7:8, LANE_GAP : LANE_GAP + heads_width] += wide_sum[:, 2 * heads_width :]

        @pl.when(at == num_blocks // 2 - 1)
        def send_side():
            sum_four.begin_side()

    sum_four.begin_home()
    for chunk in range(CHUNKS):
        sum_four.pass_on(chunk)

    scatter_a = GradScatter(links, r.grads_a, r.beside_a, r.landed_a, r.out_a)

    @pl.loop(0, width // block)
    def weigh_in(at):
        columns = rows_at(at * block, block)
        both = jnp.concatenate(
            [
                dot_tn(r.normed[:, columns], r.grad_proj[...]),
                dot_tn(r.rows_all[:, columns], r.mixed[...]),
            ],
            axis=1,
        )
        split_rows(both, r.grads_a, at * block, r.wide)

    scatter_a.begin()
    for chunk in range(CHUNKS):
        cut = sum_three.cut(chunk)
        row = r.middle[cut, :] + (sum_three.total(chunk) + vec(bias_fc2))
        r.output[cut, :] = row.astype(BF)
    for step in range(1, links.num_far):
        scatter_a.pass_on(step)
    scatter_b.end()
    scatter_c.end()

    for chunk in range(CHUNKS):
        cut = sum_four.cut(chunk)
        grad = sum_four.total(chunk)
        back, unit = layer_norm_back(r.frames[cut, :].astype(F32), grad, vec(gain_one))
        r.grad_frames[cut, :] = r.grad_middle[cut, :] + back
        r.small_grads[gain_one : gain_one + 1, :] += column_sum(grad * unit)
        r.small_grads[shift_one : shift_one + 1, :] += column_sum(grad)

    back_group = [
        links.copy(r.small_grads, r.small_group_back.at[at], device)
        for at, device in enumerate((links.sibling, links.across, links.corner))
    ]
    back_dp = [
        links.copy(r.small_total, r.small_dp.at[at], other)
        for at, other in enumerate(links.others)
    ]
    for made in back_group:
        made.start()
    total = r.small_grads[...]
    for at, made in enumerate(back_group):
        made.wait_recv()
        total = total + jnp.where(
            lax.broadcasted_iota(jnp.int32, total.shape, 0) < 6, r.small_group_back[at], 0.0
        )
    r.small_total[...] = total
    for made in back_dp:
        made.start()
    scatter_a.end()
    for at, made in enumerate(back_dp):
        made.wait_recv()
        total = total + r.small_dp[at]
    own = (dp * 4 + me) * (width // (4 * num_dp))
    r.small_out[0:6, :] = pltpu.roll(total[0:6, :], lax.rem(width - own, width), 1)
    own = dp * (HD // num_dp)
    r.small_out[6:8, :] = pltpu.roll(total[6:8, :], lax.rem(width - own, width), 1)
    links.finish()


def copy_count(num_dp):
    far = num_dp // 2
    smalls = 2 * (num_dp - 1 + 3)
    spreads = 4 * 3 * CHUNKS
    weights = 3 * 2 * (2 * far - 1)
    sums = 4 * 3 * CHUNKS
    scatters = 3 * (2 * far - 1)
    return smalls + spreads + weights + sums + scatters


def layer(num_dp, seg, frames, cotangent, small, shard_a, shard_b, shard_c):
    block, width = frames.shape
    length, slab = 4 * block, shard_a.shape[0]
    heads_width = width // 4
    num_blocks = length // BLOCK
    vmem, hbm = pl.BlockSpec(memory_space=pltpu.VMEM), pl.BlockSpec(memory_space=pl.ANY)
    inputs = [
        ("seg_row", seg, vmem),
        ("frames", frames, vmem),
        ("cotangent", cotangent, vmem),
        ("small", small, vmem),
        ("shard_a", shard_a, vmem),
        ("shard_b", shard_b, vmem),
        ("shard_c", shard_c, vmem),
    ]
    outputs = [
        ("output", (block, width), BF),
        ("grad_frames", (block, width), F32),
        ("out_a", (slab, width), F32),
        ("out_b", (slab, width), F32),
        ("out_c", (slab, width), F32),
        ("small_out", (8, width), F32),
    ]
    scratch = [("rows_all", (length, width), BF), ("given_all", (length, width), BF)]
    scratch += [("normed", (length, width), BF), ("normed_two", (length, width), BF)]
    scratch += [("active", (length, width), BF), ("grad_hidden", (length, width), BF)]
    scratch += [(f"full_{tag}", (num_dp, slab, width), BF) for tag in "abc"]
    scratch += [(f"grads_{tag}", (num_dp, slab, width), BF) for tag in "abc"]
    for tag in "abc":
        scratch += [
            (f"{kind}_{tag}", (num_dp // 2, slab, width), BF)
            for kind in ("beside", "landed")
        ]
    for tag in ("one", "two", "three"):
        if tag != "three":
            scratch += [(f"part_{tag}", (length, width), BF)]
        scratch += [
            (f"{kind}_{tag}", (block, width), BF) for kind in ("side", "home", "far")
        ]
    scratch += [
        (name, (length, heads_width), BF)
        for name in ("query", "keys", "values", "mixed", "grad_mixed")
    ]
    scratch += [
        ("turned", (heads_width, length), BF),
        ("grad_keys", (length, heads_width), F32),
        ("grad_values", (length, heads_width), F32),
        ("grad_proj", (length, 3 * heads_width), BF),
        ("mask", (length, BLOCK), F32),
        ("seg_wide", (length, 128), F32),
        ("stats", (num_blocks, 8, BLOCK), F32),
        ("inner", (num_blocks, 8, BLOCK), F32),
        ("middle", (block, width), F32),
        ("grad_middle", (block, width), F32),
        ("normed_own", (block, width), BF),
        ("attended_own", (block, width), BF),
        ("vecs", (8, width), F32),
        ("wide", (width if slab % 16 else 8, width), F32),
    ]
    for name in ("small_mine", "small_sum", "small_grads", "small_total"):
        scratch += [(name, (8, width), F32)]
    for name in ("small_group", "small_group_back"):
        scratch += [(name, (3, 8, width), F32)]
    scratch += [("small_dp", (num_dp - 1, 8, width), F32)]
    count = copy_count(num_dp)
    names = [name for name, _, _ in inputs + outputs + scratch] + ["send_sems", "recv_sems"]
    return pl.pallas_call(
        functools.partial(layer_kernel, num_dp, names),
        out_shape=[jax.ShapeDtypeStruct(shape, kind) for _, shape, kind in outputs],
        in_specs=[spec for _, _, spec in inputs],
        out_specs=[vmem] * len(outputs),
        scratch_shapes=[pltpu.VMEM(shape, kind) for _, shape, kind in scratch]
        + [pltpu.SemaphoreType.DMA((count,))] * 2,
        compiler_params=pltpu.CompilerParams(
            collective_id=0, has_side_effects=True, vmem_limit_bytes=VMEM_BYTES
        ),
        name="layer",
    )(*[value for _, value, _ in inputs])


def on_device(
    num_dp,
    frames,
    segments,
    norm1_gain,
    norm1_shift,
    in_weight,
    proj_bias,
    out_weight,
    out_bias,
    norm2_gain,
    norm2_shift,
    fc1_weight,
    fc1_bias,
    fc2_weight,
    fc2_bias,
    cotangent,
):
    width = frames.shape[1]
    slab, _, heads_width = in_weight.shape
    heads = heads_width // HD
    own = norm1_gain.shape[0]
    share = HD // num_dp
    vecs = jnp.stack([norm1_gain, norm1_shift, norm2_gain, norm2_shift, out_bias, fc2_bias])
    vecs = jnp.pad(vecs, ((0, 0), (0, width - own)))
    fc1_row = jnp.pad(fc1_bias.astype(F32), ((0, 0), (0, HD - share))).reshape(1, width)
    proj_row = jnp.pad(
        proj_bias.astype(F32),
        ((0, 0), (0, LANE_GAP // HD - heads), (0, HD - share)),
    ).reshape(1, 2 * LANE_GAP)
    proj_row = jnp.pad(proj_row, ((0, 0), (0, width - 2 * LANE_GAP)))
    small = jnp.concatenate([vecs, fc1_row, proj_row], axis=0)
    shard_a = jnp.concatenate([in_weight.reshape(slab, 3 * heads_width), out_weight.T], axis=1)
    output, grad_frames, g_a, g_b, g_c, sums = layer(
        num_dp, segments, frames, cotangent, small, shard_a, fc1_weight, fc2_weight.T
    )
    g_in = g_a[:, : 3 * heads_width].reshape(slab, 3, heads_width)
    g_out = g_a[:, 3 * heads_width :].T
    mine = sums[0:6, :own]
    g_fc1b = sums[6].reshape(-1, HD)[:, :share]
    g_proj = sums[7, : 2 * LANE_GAP].reshape(2, LANE_GAP // HD, HD)[:, :heads, :share]
    return (
        output,
        grad_frames,
        mine[0],
        mine[1],
        g_in,
        g_proj,
        g_out,
        mine[4],
        mine[2],
        mine[3],
        g_b,
        g_fc1b,
        g_c.T,
        mine[5],
    )


def solution(mesh):
    in_specs = (
        P(("dp", "tensor"), None),
        P("dp", None),
        P(("dp", "tensor")),
        P(("dp", "tensor")),
        P("dp", None, "tensor"),
        P(None, "tensor", "dp"),
        P("tensor", "dp"),
        P(("dp", "tensor")),
        P(("dp", "tensor")),
        P(("dp", "tensor")),
        P("dp", "tensor"),
        P("tensor", "dp"),
        P("tensor", "dp"),
        P(("dp", "tensor")),
        P(("dp", "tensor"), None),
    )
    out_specs = (
        P(("dp", "tensor"), None),
        P(("dp", "tensor"), None),
        P(("dp", "tensor")),
        P(("dp", "tensor")),
        P("dp", None, "tensor"),
        P(None, "tensor", "dp"),
        P("tensor", "dp"),
        P(("dp", "tensor")),
        P(("dp", "tensor")),
        P(("dp", "tensor")),
        P("dp", "tensor"),
        P("tensor", "dp"),
        P("tensor", "dp"),
        P(("dp", "tensor")),
    )
    return jax.shard_map(
        functools.partial(on_device, mesh.shape["dp"]),
        mesh=mesh,
        in_specs=in_specs,
        out_specs=out_specs,
        check_vma=False,
    )
```

```python
import functools

import jax
import jax.numpy as jnp
from jax import lax
from jax.experimental import pallas as pl
from jax.experimental.pallas import tpu as pltpu
from jax.sharding import PartitionSpec as P

HD = 64
BF = jnp.bfloat16
F32 = jnp.float32
VMEM_BYTES = 62 << 20
BLOCK = 256
CHUNKS = 3
LANE_GAP = 256


def layer_norm(row_block, norm_gain, norm_shift):
    row_mean = jnp.mean(row_block, axis=-1, keepdims=True)
    centred = row_block - row_mean
    row_var = jnp.mean(centred * centred, axis=-1, keepdims=True)
    return centred * lax.rsqrt(row_var + 1e-05) * norm_gain + norm_shift


def layer_norm_back(row, grad, gain):
    mean = jnp.mean(row, axis=-1, keepdims=True)
    centred = row - mean
    scale = lax.rsqrt(jnp.mean(centred * centred, axis=-1, keepdims=True) + 1e-05)
    unit = centred * scale
    scaled = grad * gain
    back = scale * (
        scaled
        - jnp.mean(scaled, axis=-1, keepdims=True)
        - unit * jnp.mean(scaled * unit, axis=-1, keepdims=True)
    )
    return back, unit


def dot_nn(left, right):
    return jnp.dot(left, right, preferred_element_type=F32)


def dot_nt(left, right):
    return lax.dot_general(left, right, (((1,), (1,)), ((), ())), preferred_element_type=F32)


def dot_tn(left, right):
    return lax.dot_general(left, right, (((0,), (0,)), ((), ())), preferred_element_type=F32)


def column_sum(block):
    return jnp.sum(block, axis=0, keepdims=True)


def head_part(block, head):
    lanes = lax.broadcasted_iota(jnp.int32, block.shape, 1)
    inside = (lanes >= head * HD) & (lanes < (head + 1) * HD)
    return jnp.where(inside, block, jnp.zeros_like(block))


def rows_at(start, size):
    return pl.ds(pl.multiple_of(start, 128), size)


class Links:
    def __init__(self, num_dp, send_sems, recv_sems):
        self.num_dp, self.num_far = num_dp, num_dp // 2
        self.dp, self.tensor = lax.axis_index("dp"), lax.axis_index("tensor")
        self.send_sems, self.recv_sems, self.made, self.done = send_sems, recv_sems, [], []
        self.sibling = (self.dp, self.tensor ^ 1)
        self.across = (self.dp, self.tensor ^ 2)
        self.corner = (self.dp, self.tensor ^ 3)
        self.beside = (self.dp ^ 1, self.tensor)
        self.others = [(lax.rem(self.dp + step, num_dp), self.tensor) for step in range(1, num_dp)]

    def far(self, step):
        return lax.rem(self.dp + 2 * step, self.num_dp)

    def far_from(self, step):
        return lax.rem(self.dp + self.num_dp - 2 * step, self.num_dp)

    def copy(self, src, dst, device):
        at = len(self.made)
        made = pltpu.make_async_remote_copy(
            src_ref=src,
            dst_ref=dst,
            send_sem=self.send_sems.at[at],
            recv_sem=self.recv_sems.at[at],
            device_id=device,
            device_id_type=pl.DeviceIdType.MESH,
        )
        self.made.append(made)
        return made

    def greet(self, devices):
        barrier = pltpu.get_barrier_semaphore()
        for device in devices:
            pl.semaphore_signal(
                barrier, inc=1, device_id=device, device_id_type=pl.DeviceIdType.MESH
            )
        pl.semaphore_wait(barrier, len(devices))

    def sent(self, copies):
        for made in copies:
            made.wait_send()
            self.done.append(made)

    def finish(self):
        for made in self.made:
            if not any(made is other for other in self.done):
                made.wait_send()


class WeightSpread:
    def __init__(self, links, shard, full, halves):
        self.links, self.shard, self.full, self.halves = links, shard, full, halves
        columns = shard.shape[-1] // halves

        def part(ref, half):
            return ref.at[:, pl.ds(half * columns, columns)]

        def place(origin, half):
            return full.at[origin, :, pl.ds(half * columns, columns)]

        self.first, self.second = {}, {}
        for half in range(halves):
            for step in range(1, links.num_far):
                self.first[half, step] = links.copy(
                    part(shard, half), place(links.dp, half), (links.far(step), links.tensor)
                )
            self.second[half, 0] = links.copy(
                part(shard, half), place(links.dp, half), links.beside
            )
            for step in range(1, links.num_far):
                spot = place(links.far_from(step), half)
                self.second[half, step] = links.copy(spot, spot, links.beside)

    def begin(self):
        for made in self.first.values():
            made.start()
        self.full[self.links.dp] = self.shard[...]

    def begin_beside(self):
        for half in range(self.halves):
            self.second[half, 0].start()

    def forward(self, half):
        for step in range(1, self.links.num_far):
            self.first[half, step].wait_recv()
            self.second[half, step].start()

    def end(self):
        for made in self.second.values():
            made.wait_recv()


class RowSum:
    def __init__(self, links, part, side, home, far):
        self.links, self.part = links, part
        self.side, self.home, self.far = side, home, far
        self.block = part.shape[0] // 4
        self.rows = self.block // CHUNKS
        me = links.tensor
        cuts = [self.cut(chunk) for chunk in range(CHUNKS)]
        self.side_in = [
            links.copy(part.at[self.of(me ^ 3, chunk)], side.at[cuts[chunk]], links.sibling)
            for chunk in range(CHUNKS)
        ]
        self.home_in = [
            links.copy(part.at[self.of(me ^ 1, chunk)], home.at[cuts[chunk]], links.sibling)
            for chunk in range(CHUNKS)
        ]
        self.far_in = [
            links.copy(side.at[cuts[chunk]], far.at[cuts[chunk]], links.across)
            for chunk in range(CHUNKS)
        ]

    def cut(self, chunk):
        return pl.ds(chunk * self.rows, self.rows)

    def of(self, member, chunk):
        return rows_at(member * self.block + chunk * self.rows, self.rows)

    def begin_side(self):
        for made in self.side_in:
            made.start()

    def begin_home(self):
        for made in self.home_in:
            made.start()

    def pass_on(self, chunk):
        cut = self.cut(chunk)
        self.side_in[chunk].wait_recv()
        mine = self.part[self.of(self.links.tensor ^ 2, chunk), :]
        self.side[cut, :] = (mine.astype(F32) + self.side[cut, :].astype(F32)).astype(BF)
        self.far_in[chunk].start()

    def total(self, chunk):
        cut = self.cut(chunk)
        self.home_in[chunk].wait_recv()
        self.far_in[chunk].wait_recv()
        return (
            self.part[self.of(self.links.tensor, chunk), :].astype(F32)
            + self.home[cut, :].astype(F32)
            + self.far[cut, :].astype(F32)
        )


class RowSpread:
    def __init__(self, links, own, gathered):
        self.block = own.shape[0]
        self.rows = self.block // CHUNKS
        self.own, self.gathered, self.links = own, gathered, links
        me = links.tensor
        self.across_in, self.sibling_in, self.corner_in = [], [], []
        for chunk in range(CHUNKS):
            source, place = own.at[self.cut(chunk)], gathered.at[self.of(me, chunk)]
            self.across_in.append(links.copy(source, place, links.across))
            self.sibling_in.append(links.copy(source, place, links.sibling))
        for chunk in range(CHUNKS):
            place = gathered.at[self.of(me ^ 2, chunk)]
            self.corner_in.append(links.copy(place, place, links.sibling))

    def cut(self, chunk):
        return pl.ds(chunk * self.rows, self.rows)

    def of(self, member, chunk):
        return rows_at(member * self.block + chunk * self.rows, self.rows)

    def give(self, chunk):
        self.across_in[chunk].start()
        self.sibling_in[chunk].start()
        self.gathered[self.of(self.links.tensor, chunk), :] = self.own[self.cut(chunk), :]

    def hand_over(self, chunk):
        self.across_in[chunk].wait_recv()
        self.corner_in[chunk].start()

    def await_sibling(self):
        for made in self.sibling_in:
            made.wait_recv()

    def await_corner(self):
        for made in self.corner_in:
            made.wait_recv()


class GradScatter:
    def __init__(self, links, grads, beside, landed, result):
        self.links, self.grads, self.beside = links, grads, beside
        self.landed, self.result = landed, result
        self.slab = beside.shape[1]
        self.beside_in, self.far_in = {}, {}
        for step in range(links.num_far):
            target = links.far(step)
            self.beside_in[step] = links.copy(
                grads.at[target ^ 1], beside.at[step], links.beside
            )
            if step:
                self.far_in[step] = links.copy(
                    beside.at[step], landed.at[step], (target, links.tensor)
                )

    def begin(self):
        for step in range(1, self.links.num_far + 1):
            self.beside_in[step % self.links.num_far].start()

    def pass_on(self, step):
        self.beside_in[step].wait_recv()
        mine = self.grads[self.links.far(step)]
        self.beside[step] = (mine.astype(F32) + self.beside[step].astype(F32)).astype(BF)
        self.far_in[step].start()

    def end(self):
        self.beside_in[0].wait_recv()
        total = self.grads[self.links.dp].astype(F32) + self.beside[0].astype(F32)
        for step in range(1, self.links.num_far):
            self.far_in[step].wait_recv()
            total = total + self.landed[step].astype(F32)
        self.result[...] = total


class Refs:
    def __init__(self, names, refs):
        for name, ref in zip(names, refs, strict=True):
            setattr(self, name, ref)


def flat_weight(full, wide):
    count, slab, width = full.shape
    if slab % 16 == 0:
        return full[...].reshape(count * slab, width)
    for at in range(count):
        wide[at * slab : (at + 1) * slab, :] = full[at].astype(F32)
    return wide[...].astype(BF)


def split_rows(value, grads, start, wide):
    count, slab, width = grads.shape
    rows = value.shape[0]
    if slab % 16 == 0:
        grads[pl.ds(start // slab, rows // slab)] = value.astype(BF).reshape(
            rows // slab, slab, width
        )
        return
    wide[0:rows, :] = value
    for at in range(rows // slab):
        grads[start // slab + at] = wide[at * slab : (at + 1) * slab, :].astype(BF)


def layer_kernel(num_dp, names, *refs):
    r = Refs(names, refs)
    links = Links(num_dp, r.send_sems, r.recv_sems)
    me, dp = links.tensor, links.dp
    block, width = r.frames.shape
    length = 4 * block
    num_blocks = length // BLOCK
    heads_width = width // 4
    heads = heads_width // HD
    qkv = 3 * heads_width
    upper = me // 2

    links.greet(links.others + [links.sibling, links.across, links.corner])

    small_dp = [
        links.copy(r.small_mine, r.small_dp.at[at], other) for at, other in enumerate(links.others)
    ]
    small_group = [
        links.copy(r.small_sum, r.small_group.at[at], device)
        for at, device in enumerate((links.sibling, links.across, links.corner))
    ]
    frame_rows = RowSpread(links, r.frames, r.rows_all)
    given_rows = RowSpread(links, r.cotangent, r.given_all)
    spread_a = WeightSpread(links, r.shard_a, r.full_a, 2)
    spread_b = WeightSpread(links, r.shard_b, r.full_b, 2)
    spread_c = WeightSpread(links, r.shard_c, r.full_c, 2)

    placed = pltpu.roll(r.small[0:6, :], (dp * 4 + me) * (width // (4 * num_dp)), 1)
    r.small_mine[0:6, :] = placed
    r.small_mine[6:8, :] = pltpu.roll(r.small[6:8, :], dp * (HD // num_dp), 1)
    for made in small_dp:
        made.start()
    for chunk in range(CHUNKS):
        frame_rows.give(chunk)
    spread_a.begin()
    spread_a.begin_beside()
    for chunk in range(CHUNKS):
        given_rows.give(chunk)
    spread_b.begin()
    spread_c.begin()

    ids = r.seg_row[0:1, :].astype(F32)
    r.seg_wide[...] = jnp.transpose(jnp.broadcast_to(ids, (128, length)))

    total = r.small_mine[...]
    for at, made in enumerate(small_dp):
        made.wait_recv()
        total = total + r.small_dp[at]
    r.small_sum[...] = total
    for made in small_group:
        made.start()
    for at, made in enumerate(small_group):
        made.wait_recv()
        total = total + jnp.where(
            lax.broadcasted_iota(jnp.int32, total.shape, 0) < 6, r.small_group[at], 0.0
        )
    r.vecs[...] = total
    gain_one, shift_one, gain_two, shift_two, bias_out, bias_fc2 = range(6)

    def vec(at):
        return r.vecs[at : at + 1, :]

    spread_a.forward(0)
    frame_rows.hand_over(0)
    spread_a.forward(1)
    spread_b.begin_beside()
    spread_c.begin_beside()
    frame_rows.hand_over(1)
    frame_rows.await_sibling()
    spread_a.end()

    @pl.loop(0, num_blocks)
    def project(at):
        spot = lax.rem(at + upper * (num_blocks // 2), num_blocks)
        rows = rows_at(spot * BLOCK, BLOCK)

        @pl.when(at == num_blocks // 2)
        def from_across():
            frame_rows.hand_over(2)
            frame_rows.await_corner()

        low = layer_norm(
            r.rows_all[rows, :].astype(F32), vec(gain_one), vec(shift_one)
        ).astype(BF)
        r.normed[rows, :] = low
        made = dot_nn(low, flat_weight(r.full_a, r.wide)[:, :qkv])
        made_query = (made[:, :heads_width] + r.vecs[7:8, 0:heads_width]).astype(BF)
        r.query[rows, :] = made_query * jnp.asarray(0.125, BF)
        r.keys[rows, :] = made[:, heads_width : 2 * heads_width].astype(BF)
        shift = r.vecs[7:8, LANE_GAP : LANE_GAP + heads_width]
        made_values = (made[:, 2 * heads_width :] + shift).astype(BF)
        r.values[rows, :] = made_values
        r.turned[:, rows] = jnp.transpose(made_values)

    sum_one = RowSum(links, r.part_one, r.side_one, r.home_one, r.far_one)
    spread_two = RowSpread(links, r.normed_own, r.normed_two)

    @pl.loop(0, num_blocks)
    def attend(at):
        spot = lax.rem(at + (1 - upper) * (num_blocks // 2), num_blocks)
        rows = rows_at(spot * BLOCK, BLOCK)
        asked = r.query[rows, :]
        keys_ids = jnp.concatenate([r.seg_wide[...]] * (BLOCK // 128), axis=1)
        query_ids = r.seg_row[0:1, rows].astype(F32)
        r.mask[...] = jnp.where(keys_ids == query_ids, 0.0, -1e30)
        made = []
        for head in range(heads):
            scores = dot_nt(r.keys[...], head_part(asked, head)) + r.mask[...]
            top = jnp.max(scores, axis=0, keepdims=True)
            weights = jnp.exp(scores - top)
            whole = column_sum(weights)
            mixed = dot_nn(r.turned[head * HD : (head + 1) * HD, :], weights.astype(BF))
            made.append(mixed / whole)
            r.stats[spot, head : head + 1, :] = top + jnp.log(whole)
        out = jnp.transpose(jnp.concatenate(made, axis=0)).astype(BF)
        r.mixed[rows, :] = out
        r.part_one[rows, :] = dot_nt(out, flat_weight(r.full_a, r.wide)[:, qkv:]).astype(BF)

        def after(step, core=None):
            return pl.when((at == step) if core is None else ((at == step) & (me % 2 == core)))

        @after(0, 1)
        def upper_first():
            sum_one.side_in[0].start()
            sum_one.side_in[1].start()

        @after(0)
        def weights_first():
            spread_b.forward(0)

        @after(1, 0)
        def lower_second():
            sum_one.pass_on(0)
            sum_one.pass_on(1)
            sum_one.side_in[0].start()

        @after(1, 1)
        def upper_second():
            sum_one.side_in[2].start()

        @after(1)
        def rows_first():
            given_rows.hand_over(0)

        @after(2, 0)
        def lower_third():
            sum_one.side_in[1].start()
            sum_one.side_in[2].start()
            sum_one.pass_on(2)

        @after(2, 1)
        def upper_third():
            sum_one.pass_on(0)

        @after(3, 1)
        def upper_fourth():
            sum_one.pass_on(1)
            sum_one.pass_on(2)

        @after(3)
        def rows_second():
            given_rows.hand_over(1)

        @after(4)
        def weights_second():
            spread_b.forward(1)

    sum_one.begin_home()
    given_rows.hand_over(2)
    for chunk in range(CHUNKS):
        cut = sum_one.cut(chunk)
        row = r.frames[cut, :].astype(F32) + (sum_one.total(chunk) + vec(bias_out))
        r.middle[cut, :] = row
        r.normed_own[cut, :] = layer_norm(row, vec(gain_two), vec(shift_two)).astype(BF)
        spread_two.give(chunk)
        if chunk < 2:
            spread_c.forward(chunk)
    links.sent(sum_one.far_in + frame_rows.corner_in)
    given_rows.await_sibling()
    given_rows.await_corner()
    spread_b.end()
    spread_c.end()

    sum_two = RowSum(links, r.part_two, r.side_two, r.home_two, r.far_two)
    sum_three = RowSum(links, r.normed_two, r.side_three, r.home_three, r.far_three)
    r.small_grads[...] = jnp.zeros_like(r.small_grads)

    @pl.loop(0, 2 * CHUNKS)
    def feed(at):
        def when_at(step):
            return pl.when(at == step)

        for chunk in range(CHUNKS):

            @when_at(2 * chunk)
            def near(chunk=chunk):
                spread_two.sibling_in[chunk].wait_recv()

            @when_at(2 * chunk + 1)
            def remote(chunk=chunk):
                spread_two.hand_over(chunk)
                if chunk:
                    sum_two.pass_on(chunk - 1)
                spread_two.corner_in[chunk].wait_recv()

        chunk_start = (at // 2) * (block // CHUNKS)
        member = me ^ (2 * (at % 2))
        rows = rows_at(member * block + chunk_start, block // CHUNKS)
        rows_too = rows_at((member ^ 1) * block + chunk_start, block // CHUNKS)

        def both(ref):
            return jnp.concatenate([ref[rows, :], ref[rows_too, :]], axis=0)

        def put(ref, value):
            low = value.astype(BF)
            ref[rows, :] = low[: block // CHUNKS]
            ref[rows_too, :] = low[block // CHUNKS :]

        hidden = dot_nn(both(r.normed_two), flat_weight(r.full_b, r.wide)) + r.vecs[6:7, :]
        below = 0.5 + 0.5 * lax.erf(hidden * 0.7071067811865476)
        density = 0.3989422804014327 * jnp.exp(-0.5 * hidden * hidden)
        put(r.active, hidden * below)
        grad_active = dot_nn(both(r.given_all), flat_weight(r.full_c, r.wide))
        back = (grad_active * (below + hidden * density)).astype(BF)
        put(r.grad_hidden, back)
        put(r.part_two, dot_nt(back, flat_weight(r.full_b, r.wide)))
        r.small_grads[6:7, :] += column_sum(back.astype(F32))

        for chunk in range(CHUNKS):

            @when_at(2 * chunk)
            def near_done(chunk=chunk):
                sum_two.home_in[chunk].start()

            @when_at(2 * chunk + 1)
            def remote_done(chunk=chunk):
                sum_two.side_in[chunk].start()

    sum_two.pass_on(CHUNKS - 1)
    scatter_b = GradScatter(links, r.grads_b, r.beside_b, r.landed_b, r.out_b)
    scatter_c = GradScatter(links, r.grads_c, r.beside_c, r.landed_c, r.out_c)

    spread_three = RowSpread(links, r.attended_own, r.rows_all)

    def second_norm_back(chunk):
        cut = sum_two.cut(chunk)
        grad = sum_two.total(chunk)
        back, unit = layer_norm_back(r.middle[cut, :], grad, vec(gain_two))
        given = r.cotangent[cut, :].astype(F32)
        row = given + back
        r.grad_middle[cut, :] = row
        low = row.astype(BF)
        r.attended_own[cut, :] = low
        spread_three.give(chunk)
        r.small_grads[gain_two : gain_two + 1, :] += column_sum(grad * unit)
        r.small_grads[shift_two : shift_two + 1, :] += column_sum(grad)
        r.small_grads[bias_out : bias_out + 1, :] += column_sum(low.astype(F32))
        r.small_grads[bias_fc2 : bias_fc2 + 1, :] += column_sum(given)

    second_norm_back(0)

    @pl.loop(0, width // block)
    def weigh_one(at):
        columns = rows_at(at * block, block)
        made = dot_tn(r.normed_two[:, columns], r.grad_hidden[...])
        split_rows(made, r.grads_b, at * block, r.wide)

    scatter_b.begin()
    second_norm_back(1)

    @pl.loop(0, width // block)
    def weigh_two(at):
        columns = rows_at(at * block, block)
        made = dot_tn(r.given_all[:, columns], r.active[...])
        split_rows(made, r.grads_c, at * block, r.wide)

    scatter_c.begin()
    second_norm_back(2)
    links.sent(spread_two.corner_in)

    @pl.loop(0, 4)
    def branch(at):
        rows = rows_at((me ^ (3 - at)) * block, block)
        made = dot_nt(r.active[rows, :], flat_weight(r.full_c, r.wide))
        r.normed_two[rows, :] = made.astype(BF)

        @pl.when(at == 0)
        def corner_done():
            sum_three.begin_side()

        @pl.when(at == 2)
        def sibling_done():
            sum_three.begin_home()

    r.grad_keys[...] = jnp.zeros_like(r.grad_keys)
    r.grad_values[...] = jnp.zeros_like(r.grad_values)

    @pl.loop(0, num_blocks)
    def turn_keys(at):
        rows = rows_at(at * BLOCK, BLOCK)
        r.turned[:, rows] = jnp.transpose(r.keys[rows, :])

    spread_three.await_sibling()

    @pl.loop(0, num_blocks)
    def attend_back(at):
        def when_at(step):
            return pl.when(at == step)

        @when_at(1)
        def first_service():
            for chunk in range(CHUNKS):
                sum_three.pass_on(chunk)
            spread_three.hand_over(0)
            scatter_b.pass_on(1)
            scatter_b.pass_on(2)

        @when_at(2)
        def second_service():
            spread_three.hand_over(1)
            for step in range(3, links.num_far):
                scatter_b.pass_on(step)

        @when_at(3)
        def third_service():
            spread_three.hand_over(2)
            spread_three.await_corner()

        @when_at(4)
        def fourth_service():
            scatter_c.pass_on(1)

        @when_at(5)
        def fifth_service():
            for step in range(2, links.num_far):
                scatter_c.pass_on(step)

        spot = lax.rem(at + upper * (num_blocks // 2), num_blocks)
        rows = rows_at(spot * BLOCK, BLOCK)
        asked = r.query[rows, :]
        given = dot_nn(r.rows_all[rows, :], flat_weight(r.full_a, r.wide)[:, qkv:]).astype(BF)
        joint = jnp.transpose(given.astype(F32) * r.mixed[rows, :].astype(F32))
        keys_ids = jnp.concatenate([r.seg_wide[...]] * (BLOCK // 128), axis=1)
        query_ids = r.seg_row[0:1, rows].astype(F32)
        r.mask[...] = jnp.where(keys_ids == query_ids, 0.0, -1e30)
        asked_heads = [head_part(asked, head) for head in range(heads)]
        given_heads = [head_part(given, head) for head in range(heads)]
        made = []
        for head in range(heads):
            lanes = slice(head * BLOCK, (head + 1) * BLOCK)
            scores = dot_nt(r.keys[...], asked_heads[head]) + r.mask[...]
            probs = jnp.exp(scores - r.stats[spot, head : head + 1, :])
            inner = column_sum(joint[head * HD : (head + 1) * HD, :])
            slopes = dot_nt(r.values[...], given_heads[head]) - inner
            slopes = (probs * slopes).astype(BF)
            r.active[:, lanes] = probs.astype(BF)
            r.grad_hidden[:, lanes] = slopes
            made.append(dot_nn(r.turned[head * HD : (head + 1) * HD, :], slopes))
        r.grad_values[...] += dot_nn(r.active[...], jnp.concatenate(given_heads, axis=0))
        r.grad_keys[...] += dot_nn(r.grad_hidden[...], jnp.concatenate(asked_heads, axis=0))
        turned = jnp.transpose(jnp.concatenate(made, axis=0)) * 0.125
        r.grad_proj[rows, :heads_width] = turned.astype(BF)

    links.sent(sum_one.side_in + sum_one.home_in)
    sum_four = RowSum(links, r.part_one, r.side_one, r.home_one, r.far_one)

    @pl.loop(0, 4)
    def project_back(at):
        rows = rows_at((me ^ (3 - at)) * block, block)
        low_keys = r.grad_keys[rows, :].astype(BF)
        low_values = r.grad_values[rows, :].astype(BF)
        low_query = r.grad_proj[rows, :heads_width]
        whole = jnp.concatenate([low_query, low_keys, low_values], axis=1)
        r.grad_proj[rows, :] = whole
        made = dot_nt(whole, flat_weight(r.full_a, r.wide)[:, :qkv])
        r.part_one[rows, :] = made.astype(BF)
        wide_sum = column_sum(whole.astype(F32))
        r.small_grads[7:8, 0:heads_width] += wide_sum[:, 0:heads_width]
        r.small_grads[7:8, LANE_GAP : LANE_GAP + heads_width] += wide_sum[:, 2 * heads_width :]

        @pl.when(at == 0)
        def corner_done():
            sum_four.begin_side()

        @pl.when(at == 1)
        def across_done():
            for chunk in range(CHUNKS):
                sum_four.pass_on(chunk)

        @pl.when(at == 2)
        def sibling_done():
            sum_four.begin_home()

    scatter_a = GradScatter(links, r.grads_a, r.beside_a, r.landed_a, r.out_a)

    @pl.loop(0, width // block)
    def weigh_in(at):
        columns = rows_at(at * block, block)
        both = jnp.concatenate(
            [
                dot_tn(r.normed[:, columns], r.grad_proj[...]),
                dot_tn(r.rows_all[:, columns], r.mixed[...]),
            ],
            axis=1,
        )
        split_rows(both, r.grads_a, at * block, r.wide)

    scatter_a.begin()
    for chunk in range(CHUNKS):
        cut = sum_three.cut(chunk)
        row = r.middle[cut, :] + (sum_three.total(chunk) + vec(bias_fc2))
        r.output[cut, :] = row.astype(BF)
    for step in range(1, links.num_far):
        scatter_a.pass_on(step)
    scatter_b.end()
    scatter_c.end()

    for chunk in range(CHUNKS):
        cut = sum_four.cut(chunk)
        grad = sum_four.total(chunk)
        back, unit = layer_norm_back(r.frames[cut, :].astype(F32), grad, vec(gain_one))
        r.grad_frames[cut, :] = r.grad_middle[cut, :] + back
        r.small_grads[gain_one : gain_one + 1, :] += column_sum(grad * unit)
        r.small_grads[shift_one : shift_one + 1, :] += column_sum(grad)

    back_group = [
        links.copy(r.small_grads, r.small_group_back.at[at], device)
        for at, device in enumerate((links.sibling, links.across, links.corner))
    ]
    back_dp = [
        links.copy(r.small_total, r.small_dp.at[at], other)
        for at, other in enumerate(links.others)
    ]
    for made in back_group:
        made.start()
    total = r.small_grads[...]
    for at, made in enumerate(back_group):
        made.wait_recv()
        total = total + jnp.where(
            lax.broadcasted_iota(jnp.int32, total.shape, 0) < 6, r.small_group_back[at], 0.0
        )
    r.small_total[...] = total
    for made in back_dp:
        made.start()
    scatter_a.end()
    for at, made in enumerate(back_dp):
        made.wait_recv()
        total = total + r.small_dp[at]
    own = (dp * 4 + me) * (width // (4 * num_dp))
    r.small_out[0:6, :] = pltpu.roll(total[0:6, :], lax.rem(width - own, width), 1)
    own = dp * (HD // num_dp)
    r.small_out[6:8, :] = pltpu.roll(total[6:8, :], lax.rem(width - own, width), 1)
    links.finish()


def copy_count(num_dp):
    far = num_dp // 2
    smalls = 2 * (num_dp - 1 + 3)
    spreads = 4 * 3 * CHUNKS
    weights = 3 * 2 * (2 * far - 1)
    sums = 4 * 3 * CHUNKS
    scatters = 3 * (2 * far - 1)
    return smalls + spreads + weights + sums + scatters


def layer(num_dp, seg, frames, cotangent, small, shard_a, shard_b, shard_c):
    block, width = frames.shape
    length, slab = 4 * block, shard_a.shape[0]
    heads_width = width // 4
    num_blocks = length // BLOCK
    vmem, hbm = pl.BlockSpec(memory_space=pltpu.VMEM), pl.BlockSpec(memory_space=pl.ANY)
    inputs = [
        ("seg_row", seg, vmem),
        ("frames", frames, vmem),
        ("cotangent", cotangent, vmem),
        ("small", small, vmem),
        ("shard_a", shard_a, vmem),
        ("shard_b", shard_b, vmem),
        ("shard_c", shard_c, vmem),
    ]
    outputs = [
        ("output", (block, width), BF),
        ("grad_frames", (block, width), F32),
        ("out_a", (slab, width), F32),
        ("out_b", (slab, width), F32),
        ("out_c", (slab, width), F32),
        ("small_out", (8, width), F32),
    ]
    scratch = [("rows_all", (length, width), BF), ("given_all", (length, width), BF)]
    scratch += [("normed", (length, width), BF), ("normed_two", (length, width), BF)]
    scratch += [("active", (length, width), BF), ("grad_hidden", (length, width), BF)]
    scratch += [(f"full_{tag}", (num_dp, slab, width), BF) for tag in "abc"]
    scratch += [(f"grads_{tag}", (num_dp, slab, width), BF) for tag in "abc"]
    for tag in "abc":
        scratch += [
            (f"{kind}_{tag}", (num_dp // 2, slab, width), BF)
            for kind in ("beside", "landed")
        ]
    for tag in ("one", "two", "three"):
        if tag != "three":
            scratch += [(f"part_{tag}", (length, width), BF)]
        scratch += [
            (f"{kind}_{tag}", (block, width), BF) for kind in ("side", "home", "far")
        ]
    scratch += [
        (name, (length, heads_width), BF)
        for name in ("query", "keys", "values", "mixed")
    ]
    scratch += [
        ("turned", (heads_width, length), BF),
        ("grad_keys", (length, heads_width), F32),
        ("grad_values", (length, heads_width), F32),
        ("grad_proj", (length, 3 * heads_width), BF),
        ("mask", (length, BLOCK), F32),
        ("seg_wide", (length, 128), F32),
        ("stats", (num_blocks, 8, BLOCK), F32),
        ("middle", (block, width), F32),
        ("grad_middle", (block, width), F32),
        ("normed_own", (block, width), BF),
        ("attended_own", (block, width), BF),
        ("vecs", (8, width), F32),
        ("wide", (width if slab % 16 else 8, width), F32),
    ]
    for name in ("small_mine", "small_sum", "small_grads", "small_total"):
        scratch += [(name, (8, width), F32)]
    for name in ("small_group", "small_group_back"):
        scratch += [(name, (3, 8, width), F32)]
    scratch += [("small_dp", (num_dp - 1, 8, width), F32)]
    count = copy_count(num_dp)
    names = [name for name, _, _ in inputs + outputs + scratch] + ["send_sems", "recv_sems"]
    return pl.pallas_call(
        functools.partial(layer_kernel, num_dp, names),
        out_shape=[jax.ShapeDtypeStruct(shape, kind) for _, shape, kind in outputs],
        in_specs=[spec for _, _, spec in inputs],
        out_specs=[vmem] * len(outputs),
        scratch_shapes=[pltpu.VMEM(shape, kind) for _, shape, kind in scratch]
        + [pltpu.SemaphoreType.DMA((count,))] * 2,
        compiler_params=pltpu.CompilerParams(
            collective_id=0, has_side_effects=True, vmem_limit_bytes=VMEM_BYTES
        ),
        name="layer",
    )(*[value for _, value, _ in inputs])


def on_device(
    num_dp,
    frames,
    segments,
    norm1_gain,
    norm1_shift,
    in_weight,
    proj_bias,
    out_weight,
    out_bias,
    norm2_gain,
    norm2_shift,
    fc1_weight,
    fc1_bias,
    fc2_weight,
    fc2_bias,
    cotangent,
):
    width = frames.shape[1]
    slab, _, heads_width = in_weight.shape
    heads = heads_width // HD
    own = norm1_gain.shape[0]
    share = HD // num_dp
    vecs = jnp.stack([norm1_gain, norm1_shift, norm2_gain, norm2_shift, out_bias, fc2_bias])
    vecs = jnp.pad(vecs, ((0, 0), (0, width - own)))
    fc1_row = jnp.pad(fc1_bias.astype(F32), ((0, 0), (0, HD - share))).reshape(1, width)
    proj_row = jnp.pad(
        proj_bias.astype(F32),
        ((0, 0), (0, LANE_GAP // HD - heads), (0, HD - share)),
    ).reshape(1, 2 * LANE_GAP)
    proj_row = jnp.pad(proj_row, ((0, 0), (0, width - 2 * LANE_GAP)))
    small = jnp.concatenate([vecs, fc1_row, proj_row], axis=0)
    shard_a = jnp.concatenate([in_weight.reshape(slab, 3 * heads_width), out_weight.T], axis=1)
    output, grad_frames, g_a, g_b, g_c, sums = layer(
        num_dp, segments, frames, cotangent, small, shard_a, fc1_weight, fc2_weight.T
    )
    g_in = g_a[:, : 3 * heads_width].reshape(slab, 3, heads_width)
    g_out = g_a[:, 3 * heads_width :].T
    mine = sums[0:6, :own]
    g_fc1b = sums[6].reshape(-1, HD)[:, :share]
    g_proj = sums[7, : 2 * LANE_GAP].reshape(2, LANE_GAP // HD, HD)[:, :heads, :share]
    return (
        output,
        grad_frames,
        mine[0],
        mine[1],
        g_in,
        g_proj,
        g_out,
        mine[4],
        mine[2],
        mine[3],
        g_b,
        g_fc1b,
        g_c.T,
        mine[5],
    )


def solution(mesh):
    in_specs = (
        P(("dp", "tensor"), None),
        P("dp", None),
        P(("dp", "tensor")),
        P(("dp", "tensor")),
        P("dp", None, "tensor"),
        P(None, "tensor", "dp"),
        P("tensor", "dp"),
        P(("dp", "tensor")),
        P(("dp", "tensor")),
        P(("dp", "tensor")),
        P("dp", "tensor"),
        P("tensor", "dp"),
        P("tensor", "dp"),
        P(("dp", "tensor")),
        P(("dp", "tensor"), None),
    )
    out_specs = (
        P(("dp", "tensor"), None),
        P(("dp", "tensor"), None),
        P(("dp", "tensor")),
        P(("dp", "tensor")),
        P("dp", None, "tensor"),
        P(None, "tensor", "dp"),
        P("tensor", "dp"),
        P(("dp", "tensor")),
        P(("dp", "tensor")),
        P(("dp", "tensor")),
        P("dp", "tensor"),
        P("tensor", "dp"),
        P("tensor", "dp"),
        P(("dp", "tensor")),
    )
    return jax.shard_map(
        functools.partial(on_device, mesh.shape["dp"]),
        mesh=mesh,
        in_specs=in_specs,
        out_specs=out_specs,
        check_vma=False,
    )
```

```python
import functools

import jax
import jax.numpy as jnp
from jax import lax
from jax.experimental import pallas as pl
from jax.experimental.pallas import tpu as pltpu
from jax.sharding import PartitionSpec as P

HD = 64
BF = jnp.bfloat16
F32 = jnp.float32
VMEM_BYTES = 62 << 20
BLOCK = 256
CHUNKS = 3
LANE_GAP = 256


def layer_norm(row_block, norm_gain, norm_shift):
    row_mean = jnp.mean(row_block, axis=-1, keepdims=True)
    centred = row_block - row_mean
    row_var = jnp.mean(centred * centred, axis=-1, keepdims=True)
    return centred * lax.rsqrt(row_var + 1e-05) * norm_gain + norm_shift


def layer_norm_back(row, grad, gain):
    mean = jnp.mean(row, axis=-1, keepdims=True)
    centred = row - mean
    scale = lax.rsqrt(jnp.mean(centred * centred, axis=-1, keepdims=True) + 1e-05)
    unit = centred * scale
    scaled = grad * gain
    back = scale * (
        scaled
        - jnp.mean(scaled, axis=-1, keepdims=True)
        - unit * jnp.mean(scaled * unit, axis=-1, keepdims=True)
    )
    return back, unit


def dot_nn(left, right):
    return jnp.dot(left, right, preferred_element_type=F32)


def dot_nt(left, right):
    return lax.dot_general(left, right, (((1,), (1,)), ((), ())), preferred_element_type=F32)


def dot_tn(left, right):
    return lax.dot_general(left, right, (((0,), (0,)), ((), ())), preferred_element_type=F32)


def normal_parts(hidden):
    bell = jnp.exp(-0.5 * hidden * hidden)
    near = 1.0 / (1.0 + 0.23164189 * jnp.abs(hidden))
    tail = near * (
        0.127414796
        + near * (-0.142248368 + near * (0.7107068705 + near * (-0.7265760135 + near * 0.5307027145)))
    )
    above = tail * bell
    return jnp.where(hidden < 0.0, above, 1.0 - above), 0.3989422804014327 * bell


def column_sum(block):
    return jnp.sum(block, axis=0, keepdims=True)


def head_part(block, head):
    lanes = lax.broadcasted_iota(jnp.int32, block.shape, 1)
    inside = (lanes >= head * HD) & (lanes < (head + 1) * HD)
    return jnp.where(inside, block, jnp.zeros_like(block))


def rows_at(start, size):
    return pl.ds(pl.multiple_of(start, 128), size)


class Links:
    def __init__(self, num_dp, send_sems, recv_sems):
        self.num_dp, self.num_far = num_dp, num_dp // 2
        self.dp, self.tensor = lax.axis_index("dp"), lax.axis_index("tensor")
        self.send_sems, self.recv_sems, self.made, self.done = send_sems, recv_sems, [], []
        self.sibling = (self.dp, self.tensor ^ 1)
        self.across = (self.dp, self.tensor ^ 2)
        self.corner = (self.dp, self.tensor ^ 3)
        self.beside = (self.dp ^ 1, self.tensor)
        self.others = [(lax.rem(self.dp + step, num_dp), self.tensor) for step in range(1, num_dp)]

    def far(self, step):
        return lax.rem(self.dp + 2 * step, self.num_dp)

    def far_from(self, step):
        return lax.rem(self.dp + self.num_dp - 2 * step, self.num_dp)

    def copy(self, src, dst, device):
        at = len(self.made)
        made = pltpu.make_async_remote_copy(
            src_ref=src,
            dst_ref=dst,
            send_sem=self.send_sems.at[at],
            recv_sem=self.recv_sems.at[at],
            device_id=device,
            device_id_type=pl.DeviceIdType.MESH,
        )
        self.made.append(made)
        return made

    def greet(self, devices):
        barrier = pltpu.get_barrier_semaphore()
        for device in devices:
            pl.semaphore_signal(
                barrier, inc=1, device_id=device, device_id_type=pl.DeviceIdType.MESH
            )
        return lambda: pl.semaphore_wait(barrier, len(devices))

    def sent(self, copies):
        for made in copies:
            made.wait_send()
            self.done.append(made)

    def finish(self):
        for made in self.made:
            if not any(made is other for other in self.done):
                made.wait_send()


class WeightSpread:
    def __init__(self, links, shard, full, edges):
        self.links, self.shard, self.full = links, shard, full

        def part(ref, half):
            return ref.at[:, pl.ds(edges[half], edges[half + 1] - edges[half])]

        def place(origin, half):
            return full.at[origin, :, pl.ds(edges[half], edges[half + 1] - edges[half])]

        self.first, self.second = {}, {}
        for half in range(len(edges) - 1):
            for step in range(1, links.num_far):
                self.first[half, step] = links.copy(
                    part(shard, half), place(links.dp, half), (links.far(step), links.tensor)
                )
            self.second[half, 0] = links.copy(
                part(shard, half), place(links.dp, half), links.beside
            )
            for step in range(1, links.num_far):
                spot = place(links.far_from(step), half)
                self.second[half, step] = links.copy(spot, spot, links.beside)

    def begin(self, half):
        for step in range(1, self.links.num_far):
            self.first[half, step].start()

    def begin_beside(self, half):
        self.second[half, 0].start()

    def keep_own(self):
        self.full[self.links.dp] = self.shard[...]

    def forward(self, half):
        for step in range(1, self.links.num_far):
            self.first[half, step].wait_recv()
            self.second[half, step].start()

    def end(self, halves):
        for half in halves:
            for step in range(self.links.num_far):
                self.second[half, step].wait_recv()


class RowSum:
    def __init__(self, links, part, side, home, far):
        self.links, self.part = links, part
        self.side, self.home, self.far = side, home, far
        self.block = part.shape[0] // 4
        self.rows = self.block // CHUNKS
        me = links.tensor
        cuts = [self.cut(chunk) for chunk in range(CHUNKS)]
        self.side_in = [
            links.copy(part.at[self.of(me ^ 3, chunk)], side.at[cuts[chunk]], links.sibling)
            for chunk in range(CHUNKS)
        ]
        self.home_in = [
            links.copy(part.at[self.of(me ^ 1, chunk)], home.at[cuts[chunk]], links.sibling)
            for chunk in range(CHUNKS)
        ]
        self.far_in = [
            links.copy(side.at[cuts[chunk]], far.at[cuts[chunk]], links.across)
            for chunk in range(CHUNKS)
        ]

    def cut(self, chunk):
        return pl.ds(chunk * self.rows, self.rows)

    def of(self, member, chunk):
        return rows_at(member * self.block + chunk * self.rows, self.rows)

    def begin_side(self):
        for made in self.side_in:
            made.start()

    def begin_home(self):
        for made in self.home_in:
            made.start()

    def pass_on(self, chunk):
        cut = self.cut(chunk)
        self.side_in[chunk].wait_recv()
        mine = self.part[self.of(self.links.tensor ^ 2, chunk), :]
        self.side[cut, :] = (mine.astype(F32) + self.side[cut, :].astype(F32)).astype(BF)
        self.far_in[chunk].start()

    def total(self, chunk):
        cut = self.cut(chunk)
        self.home_in[chunk].wait_recv()
        self.far_in[chunk].wait_recv()
        return (
            self.part[self.of(self.links.tensor, chunk), :].astype(F32)
            + self.home[cut, :].astype(F32)
            + self.far[cut, :].astype(F32)
        )


class RowSpread:
    def __init__(self, links, own, gathered):
        self.block = own.shape[0]
        self.rows = self.block // CHUNKS
        self.own, self.gathered, self.links = own, gathered, links
        me = links.tensor
        self.across_in, self.sibling_in, self.corner_in = [], [], []
        for chunk in range(CHUNKS):
            source, place = own.at[self.cut(chunk)], gathered.at[self.of(me, chunk)]
            self.across_in.append(links.copy(source, place, links.across))
            self.sibling_in.append(links.copy(source, place, links.sibling))
        for chunk in range(CHUNKS):
            place = gathered.at[self.of(me ^ 2, chunk)]
            self.corner_in.append(links.copy(place, place, links.sibling))

    def cut(self, chunk):
        return pl.ds(chunk * self.rows, self.rows)

    def of(self, member, chunk):
        return rows_at(member * self.block + chunk * self.rows, self.rows)

    def give(self, chunk):
        self.across_in[chunk].start()
        self.sibling_in[chunk].start()
        self.gathered[self.of(self.links.tensor, chunk), :] = self.own[self.cut(chunk), :]

    def hand_over(self, chunk):
        self.across_in[chunk].wait_recv()
        self.corner_in[chunk].start()

    def await_sibling(self):
        for made in self.sibling_in:
            made.wait_recv()

    def await_corner(self):
        for made in self.corner_in:
            made.wait_recv()


class GradScatter:
    def __init__(self, links, grads, beside, landed, result):
        self.links, self.grads, self.beside = links, grads, beside
        self.landed, self.result = landed, result
        self.slab = beside.shape[1]
        self.beside_in, self.far_in = {}, {}
        for step in range(links.num_far):
            target = links.far(step)
            self.beside_in[step] = links.copy(
                grads.at[target ^ 1], beside.at[step], links.beside
            )
            if step:
                self.far_in[step] = links.copy(
                    beside.at[step], landed.at[step], (target, links.tensor)
                )

    def begin(self):
        for step in range(1, self.links.num_far + 1):
            self.beside_in[step % self.links.num_far].start()

    def pass_on(self, step):
        self.beside_in[step].wait_recv()
        mine = self.grads[self.links.far(step)]
        self.beside[step] = (mine.astype(F32) + self.beside[step].astype(F32)).astype(BF)
        self.far_in[step].start()

    def end(self):
        self.beside_in[0].wait_recv()
        total = self.grads[self.links.dp].astype(F32) + self.beside[0].astype(F32)
        for step in range(1, self.links.num_far):
            self.far_in[step].wait_recv()
            total = total + self.landed[step].astype(F32)
        self.result[...] = total


class Refs:
    def __init__(self, names, refs):
        for name, ref in zip(names, refs, strict=True):
            setattr(self, name, ref)


def flat_weight(full, wide, start=0, stop=None):
    count, slab, width = full.shape
    stop = stop or width
    if slab % 16 == 0:
        return full[:, :, start:stop].reshape(count * slab, stop - start)
    for at in range(count):
        wide[at * slab : (at + 1) * slab, start:stop] = full[at, :, start:stop].astype(F32)
    return wide[:, start:stop].astype(BF)


def split_rows(value, grads, start, wide):
    count, slab, width = grads.shape
    rows = value.shape[0]
    if slab % 16 == 0:
        grads[pl.ds(start // slab, rows // slab)] = value.astype(BF).reshape(
            rows // slab, slab, width
        )
        return
    wide[0:rows, :] = value
    for at in range(rows // slab):
        grads[start // slab + at] = wide[at * slab : (at + 1) * slab, :].astype(BF)


def turn(value):
    rows, columns = value.shape
    tall = jnp.concatenate(
        [value.astype(F32), jnp.zeros((rows, 128 - columns), F32)], axis=1
    )
    return jnp.transpose(tall)[:columns, :].astype(value.dtype)


def layer_kernel(num_dp, names, *refs):
    r = Refs(names, refs)
    links = Links(num_dp, r.send_sems, r.recv_sems)
    me, dp = links.tensor, links.dp
    block, width = r.frames.shape
    length = 4 * block
    num_blocks = length // BLOCK
    heads_width = width // 4
    heads = heads_width // HD
    qkv = 3 * heads_width
    upper = me // 2

    await_all = links.greet(links.others + [links.sibling, links.across, links.corner])

    small_group = [
        links.copy(r.small_mine, r.small_group.at[at], device)
        for at, device in enumerate((links.sibling, links.across, links.corner))
    ]
    small_dp = [
        links.copy(r.small_sum, r.small_dp.at[at], other) for at, other in enumerate(links.others)
    ]
    frame_rows = RowSpread(links, r.frames, r.rows_all)
    given_rows = RowSpread(links, r.cotangent, r.given_all)
    spread_a = WeightSpread(links, r.shard_a, r.full_a, (0, width // 2, width * 5 // 6, width))
    spread_b = WeightSpread(links, r.shard_b, r.full_b, (0, width // 2, width))
    spread_c = WeightSpread(links, r.shard_c, r.full_c, (0, width // 2, width))

    r.shard_a[:, :qkv] = jnp.concatenate([r.in_weight[at] for at in range(3)], axis=1)
    r.shard_a[:, qkv:] = turn(r.out_weight[...])
    own, share = width // (4 * num_dp), HD // num_dp
    r.small_mine[...] = jnp.zeros_like(r.small_mine)
    for at in range(6):
        r.small_mine[at : at + 1, 0:own] = getattr(r, f"vec_{at}")[...]
    r.small_mine[0:6, :] = pltpu.roll(r.small_mine[0:6, :], (dp * 4 + me) * own, 1)
    lane = lax.broadcasted_iota(jnp.int32, (1, width), 1)

    def one_hot(rows, target):
        return jnp.where(
            lax.broadcasted_iota(jnp.int32, (rows, width), 0) == target, 1.0, 0.0
        ).astype(BF)

    tall = dot_nn(r.fc1_bias[...], one_hot(width // HD, lane // HD))
    within = lane % HD - dp * share
    r.small_mine[6:7, :] = column_sum(
        jnp.where(lax.broadcasted_iota(jnp.int32, tall.shape, 0) == within, tall, 0.0)
    )
    row = jnp.zeros((1, width), F32)
    for head in range(heads):
        pair = dot_nn(r.proj_bias[head], one_hot(share, within))
        for at in range(2):
            here = lane // HD == at * (LANE_GAP // HD) + head
            row = row + jnp.where(here, pair[at : at + 1, :], 0.0)
    r.small_mine[7:8, :] = row
    ids = r.seg_row[0:1, :].astype(F32)
    r.seg_wide[...] = jnp.transpose(jnp.broadcast_to(ids, (128, length)))
    await_all()
    for made in small_group:
        made.start()
    for chunk in range(CHUNKS):
        frame_rows.give(chunk)
    spread_a.begin(0)
    spread_a.begin_beside(0)

    total = r.small_mine[...]
    for at, made in enumerate(small_group):
        made.wait_recv()
        total = total + jnp.where(
            lax.broadcasted_iota(jnp.int32, total.shape, 0) < 6, r.small_group[at], 0.0
        )
    r.small_sum[...] = total
    for made in small_dp:
        made.start()
    for half in (1, 2):
        spread_a.begin(half)
        spread_a.begin_beside(half)
    for chunk in range(CHUNKS):
        given_rows.give(chunk)
    for spread in (spread_b, spread_c):
        for half in range(2):
            spread.begin(half)
    for spread in (spread_a, spread_b, spread_c):
        spread.keep_own()

    gain_one, shift_one, gain_two, shift_two, bias_out, bias_fc2 = range(6)

    def vec(at):
        return r.vecs[at : at + 1, :]

    def normalise(first):
        @pl.loop(0, num_blocks // 2)
        def first_norm(at):
            rows = rows_at((at + first * (num_blocks // 2)) * BLOCK, BLOCK)
            low = layer_norm(r.rows_all[rows, :].astype(F32), vec(gain_one), vec(shift_one))
            r.normed[rows, :] = low.astype(BF)

    frame_rows.hand_over(0)
    spread_a.forward(0)
    for at, made in enumerate(small_dp):
        made.wait_recv()
        total = total + r.small_dp[at]
    r.vecs[...] = total
    frame_rows.await_sibling()
    normalise(upper)
    frame_rows.hand_over(1)
    spread_a.forward(1)
    frame_rows.hand_over(2)
    spread_a.forward(2)
    for spread in (spread_b, spread_c):
        for half in range(2):
            spread.begin_beside(half)
    frame_rows.await_corner()
    normalise(1 - upper)
    spread_a.end((0, 1))

    @pl.loop(0, num_blocks)
    def project(at):
        rows = rows_at(at * BLOCK, BLOCK)
        low = r.normed[rows, :]
        made = dot_nn(low, flat_weight(r.full_a, r.wide, 0, qkv))
        made_query = (made[:, :heads_width] + r.vecs[7:8, 0:heads_width]).astype(BF)
        r.query[rows, :] = made_query * jnp.asarray(0.125, BF)
        r.keys[rows, :] = made[:, heads_width : 2 * heads_width].astype(BF)
        shift = r.vecs[7:8, LANE_GAP : LANE_GAP + heads_width]
        made_values = (made[:, 2 * heads_width :] + shift).astype(BF)
        r.values[rows, :] = made_values
        r.turned[:, rows] = jnp.transpose(made_values)

    spread_a.end((2,))
    sum_one = RowSum(links, r.part_one, r.side_one, r.home_one, r.far_one)
    spread_two = RowSpread(links, r.normed_own, r.normed_two)

    @pl.loop(0, num_blocks)
    def attend(at):
        spot = lax.rem(at + (1 - upper) * (num_blocks // 2), num_blocks)
        rows = rows_at(spot * BLOCK, BLOCK)
        asked = r.query[rows, :]
        keys_ids = jnp.concatenate([r.seg_wide[...]] * (BLOCK // 128), axis=1)
        query_ids = r.seg_row[0:1, rows].astype(F32)
        r.mask[...] = jnp.where(keys_ids == query_ids, 0.0, -1e30)
        made = []
        for head in range(heads):
            scores = dot_nt(r.keys[...], head_part(asked, head)) + r.mask[...]
            top = jnp.max(scores, axis=0, keepdims=True)
            weights = jnp.exp(scores - top)
            whole = column_sum(weights)
            mixed = dot_nn(r.turned[head * HD : (head + 1) * HD, :], weights.astype(BF))
            made.append(mixed / whole)
            r.stats[spot, head : head + 1, :] = top + jnp.log(whole)
        out = jnp.transpose(jnp.concatenate(made, axis=0)).astype(BF)
        r.mixed[rows, :] = out
        r.part_one[rows, :] = dot_nt(out, flat_weight(r.full_a, r.wide, qkv)).astype(BF)

        def after(step, core=None):
            return pl.when((at == step) if core is None else ((at == step) & (me % 2 == core)))

        @after(0, 1)
        def upper_first():
            sum_one.side_in[0].start()
            sum_one.side_in[1].start()

        @after(0)
        def weights_first():
            spread_b.forward(0)

        @after(1, 0)
        def lower_second():
            sum_one.pass_on(0)
            sum_one.pass_on(1)
            sum_one.side_in[0].start()

        @after(1, 1)
        def upper_second():
            sum_one.side_in[2].start()

        @after(1)
        def rows_first():
            given_rows.hand_over(0)

        @after(2, 0)
        def lower_third():
            sum_one.side_in[1].start()
            sum_one.side_in[2].start()
            sum_one.pass_on(2)

        @after(2, 1)
        def upper_third():
            sum_one.pass_on(0)

        @after(3, 1)
        def upper_fourth():
            sum_one.pass_on(1)
            sum_one.pass_on(2)

        @after(3)
        def rows_second():
            given_rows.hand_over(1)

        @after(4)
        def weights_second():
            spread_b.forward(1)

        @after(5)
        def weights_third():
            spread_c.forward(0)

    sum_one.begin_home()
    given_rows.hand_over(2)
    for chunk in range(CHUNKS):
        cut = sum_one.cut(chunk)
        row = r.frames[cut, :].astype(F32) + (sum_one.total(chunk) + vec(bias_out))
        r.middle[cut, :] = row
        r.normed_own[cut, :] = layer_norm(row, vec(gain_two), vec(shift_two)).astype(BF)
        spread_two.give(chunk)
        if chunk == 1:
            spread_c.forward(1)
    links.sent(sum_one.far_in + frame_rows.corner_in)
    given_rows.await_sibling()
    given_rows.await_corner()
    spread_b.end((0, 1))
    spread_c.end((0, 1))

    sum_two = RowSum(links, r.part_two, r.side_two, r.home_two, r.far_two)
    sum_three = RowSum(links, r.normed_two, r.side_three, r.home_three, r.far_three)
    r.small_grads[...] = jnp.zeros_like(r.small_grads)

    @pl.loop(0, 2 * CHUNKS)
    def feed(at):
        def when_at(step):
            return pl.when(at == step)

        for chunk in range(CHUNKS):

            @when_at(2 * chunk)
            def near(chunk=chunk):
                spread_two.sibling_in[chunk].wait_recv()

            @when_at(2 * chunk + 1)
            def remote(chunk=chunk):
                spread_two.hand_over(chunk)
                if chunk:
                    sum_two.pass_on(chunk - 1)
                spread_two.corner_in[chunk].wait_recv()

        chunk_start = (at // 2) * (block // CHUNKS)
        member = me ^ (2 * (at % 2))
        rows = rows_at(member * block + chunk_start, block // CHUNKS)
        rows_too = rows_at((member ^ 1) * block + chunk_start, block // CHUNKS)

        def both(ref):
            return jnp.concatenate([ref[rows, :], ref[rows_too, :]], axis=0)

        def put(ref, value):
            low = value.astype(BF)
            ref[rows, :] = low[: block // CHUNKS]
            ref[rows_too, :] = low[block // CHUNKS :]

        hidden = dot_nn(both(r.normed_two), flat_weight(r.full_b, r.wide)) + r.vecs[6:7, :]
        below, density = normal_parts(hidden)
        put(r.active, hidden * below)
        grad_active = dot_nn(both(r.given_all), flat_weight(r.full_c, r.wide))
        back = (grad_active * (below + hidden * density)).astype(BF)
        put(r.grad_hidden, back)
        put(r.part_two, dot_nt(back, flat_weight(r.full_b, r.wide)))
        r.small_grads[6:7, :] += column_sum(back.astype(F32))

        for chunk in range(CHUNKS):

            @when_at(2 * chunk)
            def near_done(chunk=chunk):
                sum_two.home_in[chunk].start()

            @when_at(2 * chunk + 1)
            def remote_done(chunk=chunk):
                sum_two.side_in[chunk].start()

    sum_two.pass_on(CHUNKS - 1)
    scatter_b = GradScatter(links, r.grads_b, r.beside_b, r.landed_b, r.out_b)
    scatter_c = GradScatter(links, r.grads_c, r.beside_c, r.landed_c, r.out_c)

    spread_three = RowSpread(links, r.attended_own, r.rows_all)

    def second_norm_back(chunk):
        cut = sum_two.cut(chunk)
        grad = sum_two.total(chunk)
        back, unit = layer_norm_back(r.middle[cut, :], grad, vec(gain_two))
        given = r.cotangent[cut, :].astype(F32)
        row = given + back
        r.grad_middle[cut, :] = row
        low = row.astype(BF)
        r.attended_own[cut, :] = low
        spread_three.give(chunk)
        r.small_grads[gain_two : gain_two + 1, :] += column_sum(grad * unit)
        r.small_grads[shift_two : shift_two + 1, :] += column_sum(grad)
        r.small_grads[bias_out : bias_out + 1, :] += column_sum(low.astype(F32))
        r.small_grads[bias_fc2 : bias_fc2 + 1, :] += column_sum(given)

    def weigh_one(at):
        columns = rows_at(at * block, block)
        made = dot_tn(r.normed_two[:, columns], r.grad_hidden[...])
        split_rows(made, r.grads_b, at * block, r.wide)

    second_norm_back(0)
    weigh_one(0)
    second_norm_back(1)
    weigh_one(1)
    scatter_b.begin()
    second_norm_back(2)

    @pl.loop(0, width // block)
    def weigh_two(at):
        columns = rows_at(at * block, block)
        made = dot_tn(r.given_all[:, columns], r.active[...])
        split_rows(made, r.grads_c, at * block, r.wide)

    scatter_c.begin()
    links.sent(spread_two.corner_in)

    @pl.loop(0, 4)
    def branch(at):
        rows = rows_at((me ^ (3 - at)) * block, block)
        made = dot_nt(r.active[rows, :], flat_weight(r.full_c, r.wide))
        r.normed_two[rows, :] = made.astype(BF)

        @pl.when(at == 0)
        def corner_done():
            sum_three.begin_side()

        @pl.when(at == 2)
        def sibling_done():
            sum_three.begin_home()

    r.grad_keys[...] = jnp.zeros_like(r.grad_keys)
    r.grad_values[...] = jnp.zeros_like(r.grad_values)

    @pl.loop(0, num_blocks)
    def turn_keys(at):
        rows = rows_at(at * BLOCK, BLOCK)
        r.turned[:, rows] = jnp.transpose(r.keys[rows, :])

    spread_three.await_sibling()

    @pl.loop(0, num_blocks)
    def attend_back(at):
        def when_at(step):
            return pl.when(at == step)

        @when_at(1)
        def first_service():
            for chunk in range(CHUNKS):
                sum_three.pass_on(chunk)
            spread_three.hand_over(0)
            scatter_b.pass_on(1)
            scatter_b.pass_on(2)

        @when_at(2)
        def second_service():
            spread_three.hand_over(1)
            for step in range(3, links.num_far):
                scatter_b.pass_on(step)

        @when_at(3)
        def third_service():
            spread_three.hand_over(2)
            spread_three.await_corner()

        @when_at(4)
        def fourth_service():
            scatter_c.pass_on(1)

        @when_at(5)
        def fifth_service():
            for step in range(2, links.num_far):
                scatter_c.pass_on(step)

        spot = lax.rem(at + upper * (num_blocks // 2), num_blocks)
        rows = rows_at(spot * BLOCK, BLOCK)
        asked = r.query[rows, :]
        given = dot_nn(r.rows_all[rows, :], flat_weight(r.full_a, r.wide, qkv)).astype(BF)
        joint = jnp.transpose(given.astype(F32) * r.mixed[rows, :].astype(F32))
        keys_ids = jnp.concatenate([r.seg_wide[...]] * (BLOCK // 128), axis=1)
        query_ids = r.seg_row[0:1, rows].astype(F32)
        r.mask[...] = jnp.where(keys_ids == query_ids, 0.0, -1e30)
        asked_heads = [head_part(asked, head) for head in range(heads)]
        given_heads = [head_part(given, head) for head in range(heads)]
        made = []
        for head in range(heads):
            lanes = slice(head * BLOCK, (head + 1) * BLOCK)
            scores = dot_nt(r.keys[...], asked_heads[head]) + r.mask[...]
            probs = jnp.exp(scores - r.stats[spot, head : head + 1, :])
            inner = column_sum(joint[head * HD : (head + 1) * HD, :])
            slopes = dot_nt(r.values[...], given_heads[head]) - inner
            slopes = (probs * slopes).astype(BF)
            r.active[:, lanes] = probs.astype(BF)
            r.grad_hidden[:, lanes] = slopes
            made.append(dot_nn(r.turned[head * HD : (head + 1) * HD, :], slopes))
        r.grad_values[...] += dot_nn(r.active[...], jnp.concatenate(given_heads, axis=0))
        r.grad_keys[...] += dot_nn(r.grad_hidden[...], jnp.concatenate(asked_heads, axis=0))
        turned = jnp.transpose(jnp.concatenate(made, axis=0)) * 0.125
        r.grad_proj[rows, :heads_width] = turned.astype(BF)

    links.sent(sum_one.side_in + sum_one.home_in)
    sum_four = RowSum(links, r.part_one, r.side_one, r.home_one, r.far_one)

    def join(rows):
        low_keys = r.grad_keys[rows, :].astype(BF)
        low_values = r.grad_values[rows, :].astype(BF)
        low_query = r.grad_proj[rows, :heads_width]
        whole = jnp.concatenate([low_query, low_keys, low_values], axis=1)
        r.grad_proj[rows, :] = whole
        wide_sum = column_sum(whole.astype(F32))
        r.small_grads[7:8, 0:heads_width] += wide_sum[:, 0:heads_width]
        r.small_grads[7:8, LANE_GAP : LANE_GAP + heads_width] += wide_sum[:, 2 * heads_width :]

    def push(rows):
        made = dot_nt(r.grad_proj[rows, :], flat_weight(r.full_a, r.wide, 0, qkv))
        r.part_one[rows, :] = made.astype(BF)

    @pl.loop(0, 2)
    def project_remote(at):
        rows = rows_at((me ^ (3 - at)) * block, block)
        join(rows)
        push(rows)

        @pl.when(at == 0)
        def corner_done():
            sum_four.begin_side()

        @pl.when(at == 1)
        def across_done():
            for chunk in range(CHUNKS):
                sum_four.pass_on(chunk)

    @pl.loop(0, 2)
    def join_near(at):
        join(rows_at((me ^ at) * block, block))

    scatter_a = GradScatter(links, r.grads_a, r.beside_a, r.landed_a, r.out_a)

    @pl.loop(0, width // block)
    def weigh_in(at):
        columns = rows_at(at * block, block)
        both = jnp.concatenate(
            [
                dot_tn(r.normed[:, columns], r.grad_proj[...]),
                dot_tn(r.rows_all[:, columns], r.mixed[...]),
            ],
            axis=1,
        )
        split_rows(both, r.grads_a, at * block, r.wide)

    scatter_a.begin()

    @pl.loop(0, 2)
    def project_near(at):
        push(rows_at((me ^ (1 - at)) * block, block))

    sum_four.begin_home()
    for chunk in range(CHUNKS):
        cut = sum_three.cut(chunk)
        row = r.middle[cut, :] + (sum_three.total(chunk) + vec(bias_fc2))
        r.output[cut, :] = row.astype(BF)
    for step in range(1, links.num_far):
        scatter_a.pass_on(step)
    scatter_b.end()
    scatter_c.end()

    for chunk in range(CHUNKS):
        cut = sum_four.cut(chunk)
        grad = sum_four.total(chunk)
        back, unit = layer_norm_back(r.frames[cut, :].astype(F32), grad, vec(gain_one))
        r.grad_frames[cut, :] = r.grad_middle[cut, :] + back
        r.small_grads[gain_one : gain_one + 1, :] += column_sum(grad * unit)
        r.small_grads[shift_one : shift_one + 1, :] += column_sum(grad)

    back_group = [
        links.copy(r.small_grads, r.small_group_back.at[at], device)
        for at, device in enumerate((links.sibling, links.across, links.corner))
    ]
    back_dp = [
        links.copy(r.small_total, r.small_dp.at[at], other)
        for at, other in enumerate(links.others)
    ]
    for made in back_group:
        made.start()
    total = r.small_grads[...]
    for at, made in enumerate(back_group):
        made.wait_recv()
        total = total + jnp.where(
            lax.broadcasted_iota(jnp.int32, total.shape, 0) < 6, r.small_group_back[at], 0.0
        )
    r.small_total[...] = total
    for made in back_dp:
        made.start()
    scatter_a.end()
    for at, made in enumerate(back_dp):
        made.wait_recv()
        total = total + r.small_dp[at]
    start = (dp * 4 + me) * own
    r.small_out[0:6, :] = pltpu.roll(total[0:6, :], lax.rem(width - start, width), 1)
    start = dp * share
    r.small_out[6:8, :] = pltpu.roll(total[6:8, :], lax.rem(width - start, width), 1)
    links.finish()


def copy_count(num_dp):
    far = num_dp // 2
    smalls = 2 * (num_dp - 1 + 3)
    spreads = 4 * 3 * CHUNKS
    weights = (3 + 2 + 2) * (2 * far - 1)
    sums = 4 * 3 * CHUNKS
    scatters = 3 * (2 * far - 1)
    return smalls + spreads + weights + sums + scatters


def layer(num_dp, seg, frames, cotangent, vecs, proj_bias, fc1_bias, in_weight, out_weight, shard_b, shard_c):
    block, width = frames.shape
    length, slab = 4 * block, shard_b.shape[0]
    heads_width = width // 4
    num_blocks = length // BLOCK
    vmem = pl.BlockSpec(memory_space=pltpu.VMEM)
    inputs = [
        ("seg_row", seg, vmem),
        ("frames", frames, vmem),
        ("cotangent", cotangent, vmem),
        ("proj_bias", proj_bias, vmem),
        ("fc1_bias", fc1_bias, vmem),
        ("in_weight", in_weight, vmem),
        ("out_weight", out_weight, vmem),
        ("shard_b", shard_b, vmem),
        ("shard_c", shard_c, vmem),
    ]
    inputs += [(f"vec_{at}", value, vmem) for at, value in enumerate(vecs)]
    outputs = [
        ("output", (block, width), BF),
        ("grad_frames", (block, width), F32),
        ("out_a", (slab, width), F32),
        ("out_b", (slab, width), F32),
        ("out_c", (slab, width), F32),
        ("small_out", (8, width), F32),
    ]
    scratch = [("rows_all", (length, width), BF), ("given_all", (length, width), BF)]
    scratch += [("normed", (length, width), BF), ("normed_two", (length, width), BF)]
    scratch += [("active", (length, width), BF), ("grad_hidden", (length, width), BF)]
    scratch += [(f"full_{tag}", (num_dp, slab, width), BF) for tag in "abc"]
    scratch += [(f"grads_{tag}", (num_dp, slab, width), BF) for tag in "abc"]
    for tag in "abc":
        scratch += [
            (f"{kind}_{tag}", (num_dp // 2, slab, width), BF)
            for kind in ("beside", "landed")
        ]
    for tag in ("one", "two", "three"):
        if tag != "three":
            scratch += [(f"part_{tag}", (length, width), BF)]
        scratch += [
            (f"{kind}_{tag}", (block, width), BF) for kind in ("side", "home", "far")
        ]
    scratch += [
        (name, (length, heads_width), BF)
        for name in ("query", "keys", "values", "mixed")
    ]
    scratch += [
        ("turned", (heads_width, length), BF),
        ("grad_keys", (length, heads_width), F32),
        ("grad_values", (length, heads_width), F32),
        ("grad_proj", (length, 3 * heads_width), BF),
        ("mask", (length, BLOCK), F32),
        ("seg_wide", (length, 128), F32),
        ("stats", (num_blocks, 8, BLOCK), F32),
        ("middle", (block, width), F32),
        ("grad_middle", (block, width), F32),
        ("normed_own", (block, width), BF),
        ("attended_own", (block, width), BF),
        ("vecs", (8, width), F32),
        ("shard_a", (slab, width), BF),
        ("wide", (width if slab % 16 else 8, width), F32),
    ]
    for name in ("small_mine", "small_sum", "small_grads", "small_total"):
        scratch += [(name, (8, width), F32)]
    for name in ("small_group", "small_group_back"):
        scratch += [(name, (3, 8, width), F32)]
    scratch += [("small_dp", (num_dp - 1, 8, width), F32)]
    count = copy_count(num_dp)
    names = [name for name, _, _ in inputs + outputs + scratch] + ["send_sems", "recv_sems"]
    return pl.pallas_call(
        functools.partial(layer_kernel, num_dp, names),
        out_shape=[jax.ShapeDtypeStruct(shape, kind) for _, shape, kind in outputs],
        in_specs=[spec for _, _, spec in inputs],
        out_specs=[vmem] * len(outputs),
        scratch_shapes=[pltpu.VMEM(shape, kind) for _, shape, kind in scratch]
        + [pltpu.SemaphoreType.DMA((count,))] * 2,
        compiler_params=pltpu.CompilerParams(
            collective_id=0, has_side_effects=True, vmem_limit_bytes=VMEM_BYTES
        ),
        name="layer",
    )(*[value for _, value, _ in inputs])


def unpack_kernel(own, share, output, grad_frames, grads_a, grads_b, grads_c, sums, output_too, grad_frames_too, g_in, g_proj, g_out, grads_b_too, g_fc1b, grads_c_too, vec_0, vec_1, vec_2, vec_3, vec_4, vec_5, sems):
    pairs = (
        (output, output_too),
        (grad_frames, grad_frames_too),
        (grads_b, grads_b_too),
        (grads_c, grads_c_too),
    )
    copies = [pltpu.make_async_copy(*pair, sems.at[at]) for at, pair in enumerate(pairs)]
    for made in copies:
        made.start()
    heads_width = g_in.shape[2]
    for at in range(3):
        g_in[at] = grads_a[:, at * heads_width : (at + 1) * heads_width]
    g_out[...] = jnp.transpose(grads_a[:, 3 * heads_width :])
    for at, vec in enumerate((vec_0, vec_1, vec_2, vec_3, vec_4, vec_5)):
        vec[...] = sums[at : at + 1, 0:own]
    width = sums.shape[1]
    pieces = [
        pltpu.roll(sums[...], (width - at * HD) % width, 1)[6:7, 0:128] for at in range(width // HD)
    ]
    pieces.append(jnp.zeros((16 - len(pieces), 128), F32))
    g_fc1b[...] = jnp.transpose(jnp.concatenate(pieces, axis=0))[0:share, 0 : width // HD]
    for head in range(heads_width // HD):
        for at in range(2):
            start = at * LANE_GAP + head * HD
            piece = pltpu.roll(sums[...], (width - start) % width, 1)
            g_proj[head, at : at + 1, :] = piece[7:8, 0:share]
    for made in copies:
        made.wait()


def unpack(own, share, results):
    output, grad_frames, grads_a, grads_b, grads_c, sums = results
    slab, width = grads_a.shape
    heads_width = width // 4
    vmem, hbm = pl.BlockSpec(memory_space=pltpu.VMEM), pl.BlockSpec(memory_space=pl.ANY)
    shapes = [
        (output.shape, BF, hbm),
        (grad_frames.shape, F32, hbm),
        ((3, slab, heads_width), F32, vmem),
        ((heads_width // HD, 2, share), F32, vmem),
        ((heads_width, slab), F32, vmem),
        ((slab, width), F32, hbm),
        ((share, width // HD), F32, vmem),
        ((slab, width), F32, hbm),
    ] + [((1, own), F32, vmem)] * 6
    return pl.pallas_call(
        functools.partial(unpack_kernel, own, share),
        out_shape=[jax.ShapeDtypeStruct(shape, kind) for shape, kind, _ in shapes],
        in_specs=[vmem] * 6,
        out_specs=[spec for _, _, spec in shapes],
        scratch_shapes=[pltpu.SemaphoreType.DMA((4,))],
        compiler_params=pltpu.CompilerParams(vmem_limit_bytes=VMEM_BYTES),
        name="unpack",
    )(*results)


def on_device(
    num_dp,
    frames,
    segments,
    norm1_gain,
    norm1_shift,
    in_weight,
    proj_bias,
    out_weight,
    out_bias,
    norm2_gain,
    norm2_shift,
    fc1_weight,
    fc1_bias,
    fc2_weight,
    fc2_bias,
    cotangent,
):
    slab, _, heads_width = in_weight.shape
    vecs = [norm1_gain, norm1_shift, norm2_gain, norm2_shift, out_bias, fc2_bias]
    results = layer(
        num_dp,
        segments,
        frames,
        cotangent,
        [value[None] for value in vecs],
        proj_bias.transpose(1, 0, 2),
        fc1_bias.T,
        in_weight.transpose(1, 0, 2),
        out_weight,
        fc1_weight,
        fc2_weight.T,
    )
    output, grad_frames, g_in, g_proj, g_out, g_b, g_fc1b, g_c, *rows = unpack(
        norm1_gain.shape[0], HD // num_dp, results
    )
    rows = [row[0] for row in rows]
    return (
        output,
        grad_frames,
        rows[0],
        rows[1],
        g_in.transpose(1, 0, 2),
        g_proj.transpose(1, 0, 2),
        g_out,
        rows[4],
        rows[2],
        rows[3],
        g_b,
        g_fc1b.T,
        g_c.T,
        rows[5],
    )


def solution(mesh):
    in_specs = (
        P(("dp", "tensor"), None),
        P("dp", None),
        P(("dp", "tensor")),
        P(("dp", "tensor")),
        P("dp", None, "tensor"),
        P(None, "tensor", "dp"),
        P("tensor", "dp"),
        P(("dp", "tensor")),
        P(("dp", "tensor")),
        P(("dp", "tensor")),
        P("dp", "tensor"),
        P("tensor", "dp"),
        P("tensor", "dp"),
        P(("dp", "tensor")),
        P(("dp", "tensor"), None),
    )
    out_specs = (
        P(("dp", "tensor"), None),
        P(("dp", "tensor"), None),
        P(("dp", "tensor")),
        P(("dp", "tensor")),
        P("dp", None, "tensor"),
        P(None, "tensor", "dp"),
        P("tensor", "dp"),
        P(("dp", "tensor")),
        P(("dp", "tensor")),
        P(("dp", "tensor")),
        P("dp", "tensor"),
        P("tensor", "dp"),
        P("tensor", "dp"),
        P(("dp", "tensor")),
    )
    return jax.shard_map(
        functools.partial(on_device, mesh.shape["dp"]),
        mesh=mesh,
        in_specs=in_specs,
        out_specs=out_specs,
        check_vma=False,
    )
```

```python
import functools

import jax
import jax.numpy as jnp
from jax import lax
from jax.experimental import pallas as pl
from jax.experimental.pallas import tpu as pltpu
from jax.sharding import PartitionSpec as P

HD = 64
BF = jnp.bfloat16
F32 = jnp.float32
VMEM_BYTES = 62 << 20
BLOCK = 256
CHUNKS = 3
LANE_GAP = 256


def layer_norm(row_block, norm_gain, norm_shift):
    row_mean = jnp.mean(row_block, axis=-1, keepdims=True)
    centred = row_block - row_mean
    row_var = jnp.mean(centred * centred, axis=-1, keepdims=True)
    return centred * lax.rsqrt(row_var + 1e-05) * norm_gain + norm_shift


def layer_norm_back(row, grad, gain):
    mean = jnp.mean(row, axis=-1, keepdims=True)
    centred = row - mean
    scale = lax.rsqrt(jnp.mean(centred * centred, axis=-1, keepdims=True) + 1e-05)
    unit = centred * scale
    scaled = grad * gain
    back = scale * (
        scaled
        - jnp.mean(scaled, axis=-1, keepdims=True)
        - unit * jnp.mean(scaled * unit, axis=-1, keepdims=True)
    )
    return back, unit


def dot_nn(left, right):
    return jnp.dot(left, right, preferred_element_type=F32)


def dot_nt(left, right):
    return lax.dot_general(left, right, (((1,), (1,)), ((), ())), preferred_element_type=F32)


def dot_tn(left, right):
    return lax.dot_general(left, right, (((0,), (0,)), ((), ())), preferred_element_type=F32)


def normal_parts(hidden):
    below = 0.5 + 0.5 * lax.erf(hidden * 0.7071067811865476)
    return below, 0.3989422804014327 * jnp.exp(-0.5 * hidden * hidden)


def column_sum(block):
    return jnp.sum(block, axis=0, keepdims=True)


def head_part(block, head):
    lanes = lax.broadcasted_iota(jnp.int32, block.shape, 1)
    inside = (lanes >= head * HD) & (lanes < (head + 1) * HD)
    return jnp.where(inside, block, jnp.zeros_like(block))


def rows_at(start, size):
    return pl.ds(pl.multiple_of(start, 128), size)


class Links:
    def __init__(self, num_dp, send_sems, recv_sems):
        self.num_dp, self.num_far = num_dp, num_dp // 2
        self.dp, self.tensor = lax.axis_index("dp"), lax.axis_index("tensor")
        self.send_sems, self.recv_sems, self.made, self.done = send_sems, recv_sems, [], []
        self.sibling = (self.dp, self.tensor ^ 1)
        self.across = (self.dp, self.tensor ^ 2)
        self.corner = (self.dp, self.tensor ^ 3)
        self.beside = (self.dp ^ 1, self.tensor)
        self.others = [(lax.rem(self.dp + step, num_dp), self.tensor) for step in range(1, num_dp)]

    def far(self, step):
        return lax.rem(self.dp + 2 * step, self.num_dp)

    def far_from(self, step):
        return lax.rem(self.dp + self.num_dp - 2 * step, self.num_dp)

    def copy(self, src, dst, device):
        at = len(self.made)
        made = pltpu.make_async_remote_copy(
            src_ref=src,
            dst_ref=dst,
            send_sem=self.send_sems.at[at],
            recv_sem=self.recv_sems.at[at],
            device_id=device,
            device_id_type=pl.DeviceIdType.MESH,
        )
        self.made.append(made)
        return made

    def greet(self, devices):
        barrier = pltpu.get_barrier_semaphore()
        for device in devices:
            pl.semaphore_signal(
                barrier, inc=1, device_id=device, device_id_type=pl.DeviceIdType.MESH
            )
        return lambda: pl.semaphore_wait(barrier, len(devices))

    def sent(self, copies):
        for made in copies:
            made.wait_send()
            self.done.append(made)

    def finish(self):
        for made in self.made:
            if not any(made is other for other in self.done):
                made.wait_send()


class WeightSpread:
    def __init__(self, links, shard, full, edges):
        self.links, self.shard, self.full = links, shard, full

        def part(ref, half):
            return ref.at[:, pl.ds(edges[half], edges[half + 1] - edges[half])]

        def place(origin, half):
            return full.at[origin, :, pl.ds(edges[half], edges[half + 1] - edges[half])]

        self.first, self.second = {}, {}
        for half in range(len(edges) - 1):
            for step in range(1, links.num_far):
                self.first[half, step] = links.copy(
                    part(shard, half), place(links.dp, half), (links.far(step), links.tensor)
                )
            self.second[half, 0] = links.copy(
                part(shard, half), place(links.dp, half), links.beside
            )
            for step in range(1, links.num_far):
                spot = place(links.far_from(step), half)
                self.second[half, step] = links.copy(spot, spot, links.beside)

    def begin(self, half):
        for step in range(1, self.links.num_far):
            self.first[half, step].start()

    def begin_beside(self, half):
        self.second[half, 0].start()

    def keep_own(self):
        self.full[self.links.dp] = self.shard[...]

    def forward(self, half):
        for step in range(1, self.links.num_far):
            self.first[half, step].wait_recv()
            self.second[half, step].start()

    def end(self, halves):
        for half in halves:
            for step in range(self.links.num_far):
                self.second[half, step].wait_recv()


class RowSum:
    def __init__(self, links, part, side, home, far):
        self.links, self.part = links, part
        self.side, self.home, self.far = side, home, far
        self.block = part.shape[0] // 4
        self.rows = self.block // CHUNKS
        me = links.tensor
        cuts = [self.cut(chunk) for chunk in range(CHUNKS)]
        self.side_in = [
            links.copy(part.at[self.of(me ^ 3, chunk)], side.at[cuts[chunk]], links.sibling)
            for chunk in range(CHUNKS)
        ]
        self.home_in = [
            links.copy(part.at[self.of(me ^ 1, chunk)], home.at[cuts[chunk]], links.sibling)
            for chunk in range(CHUNKS)
        ]
        self.far_in = [
            links.copy(side.at[cuts[chunk]], far.at[cuts[chunk]], links.across)
            for chunk in range(CHUNKS)
        ]

    def cut(self, chunk):
        return pl.ds(chunk * self.rows, self.rows)

    def of(self, member, chunk):
        return rows_at(member * self.block + chunk * self.rows, self.rows)

    def begin_side(self):
        for made in self.side_in:
            made.start()

    def begin_home(self):
        for made in self.home_in:
            made.start()

    def pass_on(self, chunk):
        cut = self.cut(chunk)
        self.side_in[chunk].wait_recv()
        mine = self.part[self.of(self.links.tensor ^ 2, chunk), :]
        self.side[cut, :] = (mine.astype(F32) + self.side[cut, :].astype(F32)).astype(BF)
        self.far_in[chunk].start()

    def total(self, chunk):
        cut = self.cut(chunk)
        self.home_in[chunk].wait_recv()
        self.far_in[chunk].wait_recv()
        return (
            self.part[self.of(self.links.tensor, chunk), :].astype(F32)
            + self.home[cut, :].astype(F32)
            + self.far[cut, :].astype(F32)
        )


class RowSpread:
    def __init__(self, links, own, gathered):
        self.block = own.shape[0]
        self.rows = self.block // CHUNKS
        self.own, self.gathered, self.links = own, gathered, links
        me = links.tensor
        self.across_in, self.sibling_in, self.corner_in = [], [], []
        for chunk in range(CHUNKS):
            source, place = own.at[self.cut(chunk)], gathered.at[self.of(me, chunk)]
            self.across_in.append(links.copy(source, place, links.across))
            self.sibling_in.append(links.copy(source, place, links.sibling))
        for chunk in range(CHUNKS):
            place = gathered.at[self.of(me ^ 2, chunk)]
            self.corner_in.append(links.copy(place, place, links.sibling))

    def cut(self, chunk):
        return pl.ds(chunk * self.rows, self.rows)

    def of(self, member, chunk):
        return rows_at(member * self.block + chunk * self.rows, self.rows)

    def give(self, chunk):
        self.across_in[chunk].start()
        self.sibling_in[chunk].start()
        self.gathered[self.of(self.links.tensor, chunk), :] = self.own[self.cut(chunk), :]

    def hand_over(self, chunk):
        self.across_in[chunk].wait_recv()
        self.corner_in[chunk].start()

    def await_sibling(self):
        for made in self.sibling_in:
            made.wait_recv()

    def await_corner(self):
        for made in self.corner_in:
            made.wait_recv()


class GradScatter:
    def __init__(self, links, grads, beside, landed, result, start=0, stop=None):
        stop = stop or grads.shape[2]
        lanes = pl.ds(start, stop - start)
        grads, beside, landed = (ref.at[:, :, lanes] for ref in (grads, beside, landed))
        result = result.at[:, lanes]
        self.links, self.grads, self.beside = links, grads, beside
        self.landed, self.result = landed, result
        self.slab = beside.shape[1]
        self.beside_in, self.far_in = {}, {}
        for step in range(links.num_far):
            target = links.far(step)
            self.beside_in[step] = links.copy(
                grads.at[target ^ 1], beside.at[step], links.beside
            )
            if step:
                self.far_in[step] = links.copy(
                    beside.at[step], landed.at[step], (target, links.tensor)
                )

    def begin(self):
        for step in range(1, self.links.num_far + 1):
            self.beside_in[step % self.links.num_far].start()

    def pass_on(self, step):
        self.beside_in[step].wait_recv()
        mine = self.grads[self.links.far(step)]
        self.beside[step] = (mine.astype(F32) + self.beside[step].astype(F32)).astype(BF)
        self.far_in[step].start()

    def end(self):
        self.beside_in[0].wait_recv()
        total = self.grads[self.links.dp].astype(F32) + self.beside[0].astype(F32)
        for step in range(1, self.links.num_far):
            self.far_in[step].wait_recv()
            total = total + self.landed[step].astype(F32)
        self.result[...] = total


class Refs:
    def __init__(self, names, refs):
        for name, ref in zip(names, refs, strict=True):
            setattr(self, name, ref)


def flat_weight(full, wide, start=0, stop=None):
    count, slab, width = full.shape
    stop = stop or width
    if slab % 16 == 0:
        return full[:, :, start:stop].reshape(count * slab, stop - start)
    for at in range(count):
        wide[at * slab : (at + 1) * slab, start:stop] = full[at, :, start:stop].astype(F32)
    return wide[:, start:stop].astype(BF)


def split_rows(value, grads, start, wide, lane=0):
    count, slab, width = grads.shape
    rows, columns = value.shape
    lanes = slice(lane, lane + columns)
    if slab % 16 == 0:
        low = value.astype(BF).reshape(rows // slab, slab, columns)
        grads[pl.ds(start // slab, rows // slab), :, lanes] = low
        return
    wide[0:rows, lanes] = value
    for at in range(rows // slab):
        grads[start // slab + at, :, lanes] = wide[at * slab : (at + 1) * slab, lanes].astype(BF)


def turn(value):
    rows, columns = value.shape
    tall = jnp.concatenate(
        [value.astype(F32), jnp.zeros((rows, 128 - columns), F32)], axis=1
    )
    return jnp.transpose(tall)[:columns, :].astype(value.dtype)


def layer_kernel(num_dp, names, *refs):
    r = Refs(names, refs)
    links = Links(num_dp, r.send_sems, r.recv_sems)
    me, dp = links.tensor, links.dp
    block, width = r.frames.shape
    length = 4 * block
    num_blocks = length // BLOCK
    heads_width = width // 4
    heads = heads_width // HD
    qkv = 3 * heads_width
    upper = me // 2

    await_all = links.greet(links.others + [links.sibling, links.across, links.corner])

    small_group = [
        links.copy(r.small_mine, r.small_group.at[at], device)
        for at, device in enumerate((links.sibling, links.across, links.corner))
    ]
    small_dp = [
        links.copy(r.small_sum, r.small_dp.at[at], other) for at, other in enumerate(links.others)
    ]
    frame_rows = RowSpread(links, r.frames, r.rows_all)
    given_rows = RowSpread(links, r.cotangent, r.given_all)
    spread_a = WeightSpread(links, r.shard_a, r.full_a, (0, width // 2, width * 5 // 6, width))
    spread_b = WeightSpread(links, r.shard_b, r.full_b, (0, width // 2, width))
    spread_c = WeightSpread(links, r.shard_c, r.full_c, (0, width // 2, width))

    r.shard_a[:, :qkv] = jnp.concatenate([r.in_weight[at] for at in range(3)], axis=1)
    r.shard_a[:, qkv:] = turn(r.out_weight[...])
    own, share = width // (4 * num_dp), HD // num_dp
    r.small_mine[...] = jnp.zeros_like(r.small_mine)
    for at in range(6):
        r.small_mine[at : at + 1, 0:own] = getattr(r, f"vec_{at}")[...]
    r.small_mine[0:6, :] = pltpu.roll(r.small_mine[0:6, :], (dp * 4 + me) * own, 1)
    lane = lax.broadcasted_iota(jnp.int32, (1, width), 1)

    def one_hot(rows, target):
        return jnp.where(
            lax.broadcasted_iota(jnp.int32, (rows, width), 0) == target, 1.0, 0.0
        ).astype(BF)

    tall = dot_nn(r.fc1_bias[...], one_hot(width // HD, lane // HD))
    within = lane % HD - dp * share
    r.small_mine[6:7, :] = column_sum(
        jnp.where(lax.broadcasted_iota(jnp.int32, tall.shape, 0) == within, tall, 0.0)
    )
    row = jnp.zeros((1, width), F32)
    for head in range(heads):
        pair = dot_nn(r.proj_bias[head], one_hot(share, within))
        for at in range(2):
            here = lane // HD == at * (LANE_GAP // HD) + head
            row = row + jnp.where(here, pair[at : at + 1, :], 0.0)
    r.small_mine[7:8, :] = row
    ids = r.seg_row[0:1, :].astype(F32)
    r.seg_wide[...] = jnp.transpose(jnp.broadcast_to(ids, (128, length)))
    await_all()
    for made in small_group:
        made.start()
    for chunk in range(CHUNKS):
        frame_rows.give(chunk)
    spread_a.begin(0)
    spread_a.begin_beside(0)

    total = r.small_mine[...]
    for at, made in enumerate(small_group):
        made.wait_recv()
        total = total + jnp.where(
            lax.broadcasted_iota(jnp.int32, total.shape, 0) < 6, r.small_group[at], 0.0
        )
    r.small_sum[...] = total
    for made in small_dp:
        made.start()
    for half in (1, 2):
        spread_a.begin(half)
        spread_a.begin_beside(half)
    for chunk in range(CHUNKS):
        given_rows.give(chunk)
    for spread in (spread_b, spread_c):
        for half in range(2):
            spread.begin(half)
            spread.begin_beside(half)
    for spread in (spread_a, spread_b, spread_c):
        spread.keep_own()

    gain_one, shift_one, gain_two, shift_two, bias_out, bias_fc2 = range(6)

    def vec(at):
        return r.vecs[at : at + 1, :]

    def normalise(first):
        @pl.loop(0, num_blocks // 2)
        def first_norm(at):
            rows = rows_at((at + first * (num_blocks // 2)) * BLOCK, BLOCK)
            low = layer_norm(r.rows_all[rows, :].astype(F32), vec(gain_one), vec(shift_one))
            r.normed[rows, :] = low.astype(BF)

    frame_rows.hand_over(0)
    spread_a.forward(0)
    for at, made in enumerate(small_dp):
        made.wait_recv()
        total = total + r.small_dp[at]
    r.vecs[...] = total
    frame_rows.await_sibling()
    normalise(upper)
    frame_rows.hand_over(1)
    spread_a.forward(1)
    frame_rows.hand_over(2)
    spread_a.forward(2)
    frame_rows.await_corner()
    normalise(1 - upper)
    spread_a.end((0, 1))

    @pl.loop(0, num_blocks)
    def project(at):
        rows = rows_at(at * BLOCK, BLOCK)
        low = r.normed[rows, :]
        made = dot_nn(low, flat_weight(r.full_a, r.wide, 0, qkv))
        made_query = (made[:, :heads_width] + r.vecs[7:8, 0:heads_width]).astype(BF)
        r.query[rows, :] = made_query * jnp.asarray(0.125, BF)
        r.keys[rows, :] = made[:, heads_width : 2 * heads_width].astype(BF)
        shift = r.vecs[7:8, LANE_GAP : LANE_GAP + heads_width]
        made_values = (made[:, 2 * heads_width :] + shift).astype(BF)
        r.values[rows, :] = made_values
        r.turned[:, rows] = jnp.transpose(made_values)

    spread_a.end((2,))
    spread_b.forward(0)
    sum_one = RowSum(links, r.part_one, r.side_one, r.home_one, r.far_one)
    spread_two = RowSpread(links, r.normed_own, r.normed_two)

    @pl.loop(0, num_blocks)
    def attend(at):
        spot = lax.rem(at + (1 - upper) * (num_blocks // 2), num_blocks)
        rows = rows_at(spot * BLOCK, BLOCK)
        asked = r.query[rows, :]
        keys_ids = jnp.concatenate([r.seg_wide[...]] * (BLOCK // 128), axis=1)
        query_ids = r.seg_row[0:1, rows].astype(F32)
        r.mask[...] = jnp.where(keys_ids == query_ids, 0.0, -1e30)
        made = []
        for head in range(heads):
            scores = dot_nt(r.keys[...], head_part(asked, head)) + r.mask[...]
            top = jnp.max(scores, axis=0, keepdims=True)
            weights = jnp.exp(scores - top)
            whole = column_sum(weights)
            mixed = dot_nn(r.turned[head * HD : (head + 1) * HD, :], weights.astype(BF))
            made.append(mixed / whole)
            r.stats[spot, head : head + 1, :] = top + jnp.log(whole)
        out = jnp.transpose(jnp.concatenate(made, axis=0)).astype(BF)
        r.mixed[rows, :] = out
        r.part_one[rows, :] = dot_nt(out, flat_weight(r.full_a, r.wide, qkv)).astype(BF)

        def after(step, core=None):
            return pl.when((at == step) if core is None else ((at == step) & (me % 2 == core)))

        @after(0, 1)
        def upper_first():
            sum_one.side_in[0].start()
            sum_one.side_in[1].start()

        @after(1, 0)
        def lower_second():
            sum_one.pass_on(0)
            sum_one.pass_on(1)
            sum_one.side_in[0].start()

        @after(1, 1)
        def upper_second():
            sum_one.side_in[2].start()

        @after(1)
        def rows_first():
            given_rows.hand_over(0)
            spread_b.forward(1)

        @after(2, 0)
        def lower_third():
            sum_one.side_in[1].start()
            sum_one.side_in[2].start()
            sum_one.pass_on(2)

        @after(2, 1)
        def upper_third():
            sum_one.pass_on(0)

        @after(3, 1)
        def upper_fourth():
            sum_one.pass_on(1)
            sum_one.pass_on(2)

        @after(3)
        def rows_second():
            given_rows.hand_over(1)

        @after(4)
        def weights_second():
            spread_c.forward(0)

    sum_one.begin_home()
    given_rows.hand_over(2)
    r.grad_keys[...] = jnp.zeros_like(r.grad_keys)
    r.grad_values[...] = jnp.zeros_like(r.grad_values)

    @pl.loop(0, num_blocks)
    def turn_keys(at):
        rows = rows_at(at * BLOCK, BLOCK)
        r.turned[:, rows] = jnp.transpose(r.keys[rows, :])

    spread_b.end((0, 1))

    def pair_rows(chunk, member):
        start = chunk * (block // CHUNKS)
        return (
            rows_at(member * block + start, block // CHUNKS),
            rows_at((member ^ 1) * block + start, block // CHUNKS),
        )

    def both(ref, pair):
        return jnp.concatenate([ref[rows, :] for rows in pair], axis=0)

    def put(ref, pair, value):
        low = value.astype(BF)
        ref[pair[0], :] = low[: block // CHUNKS]
        ref[pair[1], :] = low[block // CHUNKS :]

    def hide(pair):
        hidden = dot_nn(both(r.normed_two, pair), flat_weight(r.full_b, r.wide)) + r.vecs[6:7, :]
        below, density = normal_parts(hidden)
        put(r.active, pair, hidden * below)
        put(r.part_two, pair, below + hidden * density)

    @pl.loop(0, CHUNKS)
    def second_norm(at):
        for chunk in range(CHUNKS):

            @pl.when(at == chunk)
            def rows_of(chunk=chunk):
                cut = sum_one.cut(chunk)
                row = r.frames[cut, :].astype(F32) + (sum_one.total(chunk) + vec(bias_out))
                r.middle[cut, :] = row
                r.normed_own[cut, :] = layer_norm(row, vec(gain_two), vec(shift_two)).astype(BF)
                spread_two.give(chunk)
                if chunk == 0:
                    spread_c.forward(1)
                spread_two.sibling_in[chunk].wait_recv()

        hide(pair_rows(at, me))

    links.sent(sum_one.far_in + frame_rows.corner_in)
    given_rows.await_sibling()
    given_rows.await_corner()
    spread_c.end((0, 1))

    sum_two = RowSum(links, r.part_two, r.side_two, r.home_two, r.far_two)
    sum_three = RowSum(links, r.normed_two, r.side_three, r.home_three, r.far_three)
    r.small_grads[...] = jnp.zeros_like(r.small_grads)

    @pl.loop(0, 2 * CHUNKS)
    def feed(at):
        def when_at(step):
            return pl.when(at == step)

        for chunk in range(CHUNKS):

            @when_at(2 * chunk)
            def bring(chunk=chunk):
                spread_two.hand_over(chunk)

            @when_at(2 * chunk + 1)
            def remote(chunk=chunk):
                if chunk:
                    sum_two.pass_on(chunk - 1)
                spread_two.corner_in[chunk].wait_recv()

        pair = pair_rows(at // 2, me ^ (2 * (at % 2)))

        @pl.when(at % 2 == 1)
        def remote_first():
            hide(pair)

        grad_active = dot_nn(both(r.given_all, pair), flat_weight(r.full_c, r.wide))
        back = (grad_active * both(r.part_two, pair).astype(F32)).astype(BF)
        put(r.grad_hidden, pair, back)
        put(r.part_two, pair, dot_nt(back, flat_weight(r.full_b, r.wide)))
        r.small_grads[6:7, :] += column_sum(back.astype(F32))

        for chunk in range(CHUNKS):

            @when_at(2 * chunk)
            def near_done(chunk=chunk):
                sum_two.home_in[chunk].start()

            @when_at(2 * chunk + 1)
            def remote_done(chunk=chunk):
                sum_two.side_in[chunk].start()

    sum_two.pass_on(CHUNKS - 1)
    scatter_b = GradScatter(links, r.grads_b, r.beside_b, r.landed_b, r.out_b)
    scatter_c = GradScatter(links, r.grads_c, r.beside_c, r.landed_c, r.out_c)

    spread_three = RowSpread(links, r.attended_own, r.rows_all)

    def second_norm_back(chunk):
        cut = sum_two.cut(chunk)
        grad = sum_two.total(chunk)
        back, unit = layer_norm_back(r.middle[cut, :], grad, vec(gain_two))
        given = r.cotangent[cut, :].astype(F32)
        row = given + back
        r.grad_middle[cut, :] = row
        low = row.astype(BF)
        r.attended_own[cut, :] = low
        spread_three.give(chunk)
        r.small_grads[gain_two : gain_two + 1, :] += column_sum(grad * unit)
        r.small_grads[shift_two : shift_two + 1, :] += column_sum(grad)
        r.small_grads[bias_out : bias_out + 1, :] += column_sum(low.astype(F32))
        r.small_grads[bias_fc2 : bias_fc2 + 1, :] += column_sum(given)

    def weigh_one(at):
        columns = rows_at(at * block, block)
        made = dot_tn(r.normed_two[:, columns], r.grad_hidden[...])
        split_rows(made, r.grads_b, at * block, r.wide)

    def weigh_two(at):
        columns = rows_at(at * block, block)
        made = dot_tn(r.given_all[:, columns], r.active[...])
        split_rows(made, r.grads_c, at * block, r.wide)

    second_norm_back(0)
    weigh_one(0)
    second_norm_back(1)
    weigh_one(1)
    scatter_b.begin()
    weigh_two(0)
    second_norm_back(2)
    weigh_two(1)
    scatter_c.begin()
    links.sent(spread_two.corner_in)

    @pl.loop(0, 4)
    def branch(at):
        rows = rows_at((me ^ (3 - at)) * block, block)
        made = dot_nt(r.active[rows, :], flat_weight(r.full_c, r.wide))
        r.normed_two[rows, :] = made.astype(BF)

        @pl.when(at == 0)
        def corner_done():
            sum_three.begin_side()

        @pl.when(at == 2)
        def sibling_done():
            sum_three.begin_home()

    spread_three.await_sibling()

    @pl.loop(0, num_blocks)
    def attend_back(at):
        def when_at(step):
            return pl.when(at == step)

        @when_at(1)
        def first_service():
            for chunk in range(CHUNKS):
                sum_three.pass_on(chunk)
            spread_three.hand_over(0)
            spread_three.hand_over(1)
            scatter_b.pass_on(1)
            scatter_b.pass_on(2)

        @when_at(2)
        def second_service():
            spread_three.hand_over(2)
            for step in range(3, links.num_far):
                scatter_b.pass_on(step)

        @when_at(3)
        def third_service():
            spread_three.await_corner()

        @when_at(4)
        def fourth_service():
            scatter_c.pass_on(1)

        @when_at(5)
        def fifth_service():
            for step in range(2, links.num_far):
                scatter_c.pass_on(step)

        spot = lax.rem(at + upper * (num_blocks // 2), num_blocks)
        rows = rows_at(spot * BLOCK, BLOCK)
        asked = r.query[rows, :]
        given = dot_nn(r.rows_all[rows, :], flat_weight(r.full_a, r.wide, qkv)).astype(BF)
        joint = jnp.transpose(given.astype(F32) * r.mixed[rows, :].astype(F32))
        keys_ids = jnp.concatenate([r.seg_wide[...]] * (BLOCK // 128), axis=1)
        query_ids = r.seg_row[0:1, rows].astype(F32)
        r.mask[...] = jnp.where(keys_ids == query_ids, 0.0, -1e30)
        asked_heads = [head_part(asked, head) for head in range(heads)]
        given_heads = [head_part(given, head) for head in range(heads)]
        made = []
        for head in range(heads):
            lanes = slice(head * BLOCK, (head + 1) * BLOCK)
            scores = dot_nt(r.keys[...], asked_heads[head]) + r.mask[...]
            probs = jnp.exp(scores - r.stats[spot, head : head + 1, :])
            inner = column_sum(joint[head * HD : (head + 1) * HD, :])
            slopes = dot_nt(r.values[...], given_heads[head]) - inner
            slopes = (probs * slopes).astype(BF)
            r.active[:, lanes] = probs.astype(BF)
            r.grad_hidden[:, lanes] = slopes
            made.append(dot_nn(r.turned[head * HD : (head + 1) * HD, :], slopes))
        r.grad_values[...] += dot_nn(r.active[...], jnp.concatenate(given_heads, axis=0))
        r.grad_keys[...] += dot_nn(r.grad_hidden[...], jnp.concatenate(asked_heads, axis=0))
        turned = jnp.transpose(jnp.concatenate(made, axis=0)) * 0.125
        r.grad_proj[rows, :heads_width] = turned.astype(BF)

    links.sent(sum_one.side_in + sum_one.home_in)
    sum_four = RowSum(links, r.part_one, r.side_one, r.home_one, r.far_one)

    def join(rows):
        low_keys = r.grad_keys[rows, :].astype(BF)
        low_values = r.grad_values[rows, :].astype(BF)
        low_query = r.grad_proj[rows, :heads_width]
        whole = jnp.concatenate([low_query, low_keys, low_values], axis=1)
        r.grad_proj[rows, :] = whole
        wide_sum = column_sum(whole.astype(F32))
        r.small_grads[7:8, 0:heads_width] += wide_sum[:, 0:heads_width]
        r.small_grads[7:8, LANE_GAP : LANE_GAP + heads_width] += wide_sum[:, 2 * heads_width :]

    def push(rows):
        made = dot_nt(r.grad_proj[rows, :], flat_weight(r.full_a, r.wide, 0, qkv))
        r.part_one[rows, :] = made.astype(BF)

    @pl.loop(0, 2)
    def project_remote(at):
        rows = rows_at((me ^ (3 - at)) * block, block)
        join(rows)
        push(rows)

        @pl.when(at == 0)
        def corner_done():
            sum_four.begin_side()

        @pl.when(at == 1)
        def across_done():
            for chunk in range(CHUNKS):
                sum_four.pass_on(chunk)

    @pl.loop(0, 2)
    def join_near(at):
        join(rows_at((me ^ at) * block, block))

    middle_lane = width // 2
    scatter_a = [
        GradScatter(links, r.grads_a, r.beside_a, r.landed_a, r.out_a, *lanes)
        for lanes in ((0, middle_lane), (middle_lane, width))
    ]

    @pl.loop(0, width // block)
    def weigh_in(at):
        columns = rows_at(at * block, block)
        made = dot_tn(r.normed[:, columns], r.grad_proj[:, 0:middle_lane])
        split_rows(made, r.grads_a, at * block, r.wide, 0)

    scatter_a[0].begin()

    @pl.loop(0, width // block)
    def weigh_in_too(at):
        columns = rows_at(at * block, block)
        made = jnp.concatenate(
            [
                dot_tn(r.normed[:, columns], r.grad_proj[:, middle_lane:qkv]),
                dot_tn(r.rows_all[:, columns], r.mixed[...]),
            ],
            axis=1,
        )
        split_rows(made, r.grads_a, at * block, r.wide, middle_lane)

    scatter_a[1].begin()

    @pl.loop(0, 2)
    def project_near(at):
        push(rows_at((me ^ (1 - at)) * block, block))

    sum_four.begin_home()
    def first_norm_back(chunk):
        cut = sum_four.cut(chunk)
        grad = sum_four.total(chunk)
        back, unit = layer_norm_back(r.frames[cut, :].astype(F32), grad, vec(gain_one))
        r.grad_frames[cut, :] = r.grad_middle[cut, :] + back
        r.small_grads[gain_one : gain_one + 1, :] += column_sum(grad * unit)
        r.small_grads[shift_one : shift_one + 1, :] += column_sum(grad)

    scatter_b.end()
    scatter_a[0].pass_on(1)
    first_norm_back(0)
    for step in range(2, links.num_far):
        scatter_a[0].pass_on(step)
    for chunk in range(CHUNKS):
        cut = sum_three.cut(chunk)
        row = r.middle[cut, :] + (sum_three.total(chunk) + vec(bias_fc2))
        r.output[cut, :] = row.astype(BF)
    first_norm_back(1)
    scatter_a[1].pass_on(1)
    scatter_a[1].pass_on(2)
    first_norm_back(2)

    back_group = [
        links.copy(r.small_grads, r.small_group_back.at[at], device)
        for at, device in enumerate((links.sibling, links.across, links.corner))
    ]
    back_dp = [
        links.copy(r.small_total, r.small_dp.at[at], other)
        for at, other in enumerate(links.others)
    ]
    for made in back_group:
        made.start()
    for step in range(3, links.num_far):
        scatter_a[1].pass_on(step)
    total = r.small_grads[...]
    for at, made in enumerate(back_group):
        made.wait_recv()
        total = total + jnp.where(
            lax.broadcasted_iota(jnp.int32, total.shape, 0) < 6, r.small_group_back[at], 0.0
        )
    r.small_total[...] = total
    for made in back_dp:
        made.start()
    scatter_c.end()
    for scatter in scatter_a:
        scatter.end()
    for at, made in enumerate(back_dp):
        made.wait_recv()
        total = total + r.small_dp[at]
    start = (dp * 4 + me) * own
    r.small_out[0:6, :] = pltpu.roll(total[0:6, :], lax.rem(width - start, width), 1)
    start = dp * share
    r.small_out[6:8, :] = pltpu.roll(total[6:8, :], lax.rem(width - start, width), 1)
    links.finish()


def copy_count(num_dp):
    far = num_dp // 2
    smalls = 2 * (num_dp - 1 + 3)
    spreads = 4 * 3 * CHUNKS
    weights = (3 + 2 + 2) * (2 * far - 1)
    sums = 4 * 3 * CHUNKS
    scatters = 4 * (2 * far - 1)
    return smalls + spreads + weights + sums + scatters


def layer(num_dp, seg, frames, cotangent, vecs, proj_bias, fc1_bias, in_weight, out_weight, shard_b, shard_c):
    block, width = frames.shape
    length, slab = 4 * block, shard_b.shape[0]
    heads_width = width // 4
    num_blocks = length // BLOCK
    vmem = pl.BlockSpec(memory_space=pltpu.VMEM)
    inputs = [
        ("seg_row", seg, vmem),
        ("frames", frames, vmem),
        ("cotangent", cotangent, vmem),
        ("proj_bias", proj_bias, vmem),
        ("fc1_bias", fc1_bias, vmem),
        ("in_weight", in_weight, vmem),
        ("out_weight", out_weight, vmem),
        ("shard_b", shard_b, vmem),
        ("shard_c", shard_c, vmem),
    ]
    inputs += [(f"vec_{at}", value, vmem) for at, value in enumerate(vecs)]
    outputs = [
        ("output", (block, width), BF),
        ("grad_frames", (block, width), F32),
        ("out_a", (slab, width), F32),
        ("out_b", (slab, width), F32),
        ("out_c", (slab, width), F32),
        ("small_out", (8, width), F32),
    ]
    scratch = [("rows_all", (length, width), BF), ("given_all", (length, width), BF)]
    scratch += [("normed", (length, width), BF), ("normed_two", (length, width), BF)]
    scratch += [("active", (length, width), BF), ("grad_hidden", (length, width), BF)]
    scratch += [(f"full_{tag}", (num_dp, slab, width), BF) for tag in "abc"]
    scratch += [(f"grads_{tag}", (num_dp, slab, width), BF) for tag in "abc"]
    for tag in "abc":
        scratch += [
            (f"{kind}_{tag}", (num_dp // 2, slab, width), BF)
            for kind in ("beside", "landed")
        ]
    for tag in ("one", "two", "three"):
        if tag != "three":
            scratch += [(f"part_{tag}", (length, width), BF)]
        scratch += [
            (f"{kind}_{tag}", (block, width), BF) for kind in ("side", "home", "far")
        ]
    scratch += [
        (name, (length, heads_width), BF)
        for name in ("query", "keys", "values", "mixed")
    ]
    scratch += [
        ("turned", (heads_width, length), BF),
        ("grad_keys", (length, heads_width), F32),
        ("grad_values", (length, heads_width), F32),
        ("grad_proj", (length, 3 * heads_width), BF),
        ("mask", (length, BLOCK), F32),
        ("seg_wide", (length, 128), F32),
        ("stats", (num_blocks, 8, BLOCK), F32),
        ("middle", (block, width), F32),
        ("grad_middle", (block, width), F32),
        ("normed_own", (block, width), BF),
        ("attended_own", (block, width), BF),
        ("vecs", (8, width), F32),
        ("shard_a", (slab, width), BF),
        ("wide", (width if slab % 16 else 8, width), F32),
    ]
    for name in ("small_mine", "small_sum", "small_grads", "small_total"):
        scratch += [(name, (8, width), F32)]
    for name in ("small_group", "small_group_back"):
        scratch += [(name, (3, 8, width), F32)]
    scratch += [("small_dp", (num_dp - 1, 8, width), F32)]
    count = copy_count(num_dp)
    names = [name for name, _, _ in inputs + outputs + scratch] + ["send_sems", "recv_sems"]
    return pl.pallas_call(
        functools.partial(layer_kernel, num_dp, names),
        out_shape=[jax.ShapeDtypeStruct(shape, kind) for _, shape, kind in outputs],
        in_specs=[spec for _, _, spec in inputs],
        out_specs=[vmem] * len(outputs),
        scratch_shapes=[pltpu.VMEM(shape, kind) for _, shape, kind in scratch]
        + [pltpu.SemaphoreType.DMA((count,))] * 2,
        compiler_params=pltpu.CompilerParams(
            collective_id=0, has_side_effects=True, vmem_limit_bytes=VMEM_BYTES
        ),
        name="layer",
    )(*[value for _, value, _ in inputs])


def unpack_kernel(own, share, output, grad_frames, grads_a, grads_b, grads_c, sums, output_too, grad_frames_too, g_in, g_proj, g_out, grads_b_too, g_fc1b, grads_c_too, vec_0, vec_1, vec_2, vec_3, vec_4, vec_5, sems):
    pairs = (
        (output, output_too),
        (grad_frames, grad_frames_too),
        (grads_b, grads_b_too),
        (grads_c, grads_c_too),
    )
    copies = [pltpu.make_async_copy(*pair, sems.at[at]) for at, pair in enumerate(pairs)]
    for made in copies:
        made.start()
    heads_width = g_in.shape[2]
    for at in range(3):
        g_in[at] = grads_a[:, at * heads_width : (at + 1) * heads_width]
    g_out[...] = jnp.transpose(grads_a[:, 3 * heads_width :])
    for at, vec in enumerate((vec_0, vec_1, vec_2, vec_3, vec_4, vec_5)):
        vec[...] = sums[at : at + 1, 0:own]
    width = sums.shape[1]
    pieces = [
        pltpu.roll(sums[...], (width - at * HD) % width, 1)[6:7, 0:128] for at in range(width // HD)
    ]
    pieces.append(jnp.zeros((16 - len(pieces), 128), F32))
    g_fc1b[...] = jnp.transpose(jnp.concatenate(pieces, axis=0))[0:share, 0 : width // HD]
    for head in range(heads_width // HD):
        for at in range(2):
            start = at * LANE_GAP + head * HD
            piece = pltpu.roll(sums[...], (width - start) % width, 1)
            g_proj[head, at : at + 1, :] = piece[7:8, 0:share]
    for made in copies:
        made.wait()


def unpack(own, share, results):
    output, grad_frames, grads_a, grads_b, grads_c, sums = results
    slab, width = grads_a.shape
    heads_width = width // 4
    vmem, hbm = pl.BlockSpec(memory_space=pltpu.VMEM), pl.BlockSpec(memory_space=pl.ANY)
    shapes = [
        (output.shape, BF, hbm),
        (grad_frames.shape, F32, hbm),
        ((3, slab, heads_width), F32, vmem),
        ((heads_width // HD, 2, share), F32, vmem),
        ((heads_width, slab), F32, vmem),
        ((slab, width), F32, hbm),
        ((share, width // HD), F32, vmem),
        ((slab, width), F32, hbm),
    ] + [((1, own), F32, vmem)] * 6
    return pl.pallas_call(
        functools.partial(unpack_kernel, own, share),
        out_shape=[jax.ShapeDtypeStruct(shape, kind) for shape, kind, _ in shapes],
        in_specs=[vmem] * 6,
        out_specs=[spec for _, _, spec in shapes],
        scratch_shapes=[pltpu.SemaphoreType.DMA((4,))],
        compiler_params=pltpu.CompilerParams(vmem_limit_bytes=VMEM_BYTES),
        name="unpack",
    )(*results)


def on_device(
    num_dp,
    frames,
    segments,
    norm1_gain,
    norm1_shift,
    in_weight,
    proj_bias,
    out_weight,
    out_bias,
    norm2_gain,
    norm2_shift,
    fc1_weight,
    fc1_bias,
    fc2_weight,
    fc2_bias,
    cotangent,
):
    slab, _, heads_width = in_weight.shape
    vecs = [norm1_gain, norm1_shift, norm2_gain, norm2_shift, out_bias, fc2_bias]
    results = layer(
        num_dp,
        segments,
        frames,
        cotangent,
        [value[None] for value in vecs],
        proj_bias.transpose(1, 0, 2),
        fc1_bias.T,
        in_weight.transpose(1, 0, 2),
        out_weight,
        fc1_weight,
        fc2_weight.T,
    )
    output, grad_frames, g_in, g_proj, g_out, g_b, g_fc1b, g_c, *rows = unpack(
        norm1_gain.shape[0], HD // num_dp, results
    )
    rows = [row[0] for row in rows]
    return (
        output,
        grad_frames,
        rows[0],
        rows[1],
        g_in.transpose(1, 0, 2),
        g_proj.transpose(1, 0, 2),
        g_out,
        rows[4],
        rows[2],
        rows[3],
        g_b,
        g_fc1b.T,
        g_c.T,
        rows[5],
    )


def solution(mesh):
    in_specs = (
        P(("dp", "tensor"), None),
        P("dp", None),
        P(("dp", "tensor")),
        P(("dp", "tensor")),
        P("dp", None, "tensor"),
        P(None, "tensor", "dp"),
        P("tensor", "dp"),
        P(("dp", "tensor")),
        P(("dp", "tensor")),
        P(("dp", "tensor")),
        P("dp", "tensor"),
        P("tensor", "dp"),
        P("tensor", "dp"),
        P(("dp", "tensor")),
        P(("dp", "tensor"), None),
    )
    out_specs = (
        P(("dp", "tensor"), None),
        P(("dp", "tensor"), None),
        P(("dp", "tensor")),
        P(("dp", "tensor")),
        P("dp", None, "tensor"),
        P(None, "tensor", "dp"),
        P("tensor", "dp"),
        P(("dp", "tensor")),
        P(("dp", "tensor")),
        P(("dp", "tensor")),
        P("dp", "tensor"),
        P("tensor", "dp"),
        P("tensor", "dp"),
        P(("dp", "tensor")),
    )
    return jax.shard_map(
        functools.partial(on_device, mesh.shape["dp"]),
        mesh=mesh,
        in_specs=in_specs,
        out_specs=out_specs,
        check_vma=False,
    )
```

```python
import functools

import jax
import jax.numpy as jnp
from jax import lax
from jax.experimental import pallas as pl
from jax.experimental.pallas import tpu as pltpu
from jax.sharding import PartitionSpec as P

HD = 64
BF = jnp.bfloat16
F32 = jnp.float32
VMEM_BYTES = 62 << 20
BLOCK = 256
CHUNKS = 3
DOCUMENT_LIMIT = 768
LANE_GAP = 256


def layer_norm(row_block, norm_gain, norm_shift):
    row_mean = jnp.mean(row_block, axis=-1, keepdims=True)
    centred = row_block - row_mean
    row_var = jnp.mean(centred * centred, axis=-1, keepdims=True)
    return centred * lax.rsqrt(row_var + 1e-05) * norm_gain + norm_shift


def layer_norm_back(row, grad, gain):
    mean = jnp.mean(row, axis=-1, keepdims=True)
    centred = row - mean
    scale = lax.rsqrt(jnp.mean(centred * centred, axis=-1, keepdims=True) + 1e-05)
    unit = centred * scale
    scaled = grad * gain
    back = scale * (
        scaled
        - jnp.mean(scaled, axis=-1, keepdims=True)
        - unit * jnp.mean(scaled * unit, axis=-1, keepdims=True)
    )
    return back, unit


def dot_nn(left, right):
    return jnp.dot(left, right, preferred_element_type=F32)


def dot_nt(left, right):
    return lax.dot_general(left, right, (((1,), (1,)), ((), ())), preferred_element_type=F32)


def dot_tn(left, right):
    return lax.dot_general(left, right, (((0,), (0,)), ((), ())), preferred_element_type=F32)


def normal_parts(hidden):
    below = 0.5 + 0.5 * lax.erf(hidden * 0.7071067811865476)
    return below, 0.3989422804014327 * jnp.exp(-0.5 * hidden * hidden)


def column_sum(block):
    return jnp.sum(block, axis=0, keepdims=True)


def head_part(block, head):
    lanes = lax.broadcasted_iota(jnp.int32, block.shape, 1)
    inside = (lanes >= head * HD) & (lanes < (head + 1) * HD)
    return jnp.where(inside, block, jnp.zeros_like(block))


def rows_at(start, size):
    return pl.ds(pl.multiple_of(start, 128), size)


class Links:
    def __init__(self, num_dp, send_sems, recv_sems):
        self.num_dp, self.num_far = num_dp, num_dp // 2
        self.dp, self.tensor = lax.axis_index("dp"), lax.axis_index("tensor")
        self.send_sems, self.recv_sems, self.made, self.done = send_sems, recv_sems, [], []
        self.sibling = (self.dp, self.tensor ^ 1)
        self.across = (self.dp, self.tensor ^ 2)
        self.corner = (self.dp, self.tensor ^ 3)
        self.beside = (self.dp ^ 1, self.tensor)
        self.others = [(lax.rem(self.dp + step, num_dp), self.tensor) for step in range(1, num_dp)]

    def far(self, step):
        return lax.rem(self.dp + 2 * step, self.num_dp)

    def far_from(self, step):
        return lax.rem(self.dp + self.num_dp - 2 * step, self.num_dp)

    def copy(self, src, dst, device):
        at = len(self.made)
        made = pltpu.make_async_remote_copy(
            src_ref=src,
            dst_ref=dst,
            send_sem=self.send_sems.at[at],
            recv_sem=self.recv_sems.at[at],
            device_id=device,
            device_id_type=pl.DeviceIdType.MESH,
        )
        self.made.append(made)
        return made

    def greet(self, devices):
        barrier = pltpu.get_barrier_semaphore()
        for device in devices:
            pl.semaphore_signal(
                barrier, inc=1, device_id=device, device_id_type=pl.DeviceIdType.MESH
            )
        return lambda: pl.semaphore_wait(barrier, len(devices))

    def sent(self, copies):
        for made in copies:
            made.wait_send()
            self.done.append(made)

    def finish(self):
        for made in self.made:
            if not any(made is other for other in self.done):
                made.wait_send()


class WeightSpread:
    def __init__(self, links, shard, full, edges):
        self.links, self.shard, self.full = links, shard, full

        def part(ref, half):
            return ref.at[:, pl.ds(edges[half], edges[half + 1] - edges[half])]

        def place(origin, half):
            return full.at[origin, :, pl.ds(edges[half], edges[half + 1] - edges[half])]

        self.first, self.second = {}, {}
        for half in range(len(edges) - 1):
            for step in range(1, links.num_far):
                self.first[half, step] = links.copy(
                    part(shard, half), place(links.dp, half), (links.far(step), links.tensor)
                )
            self.second[half, 0] = links.copy(
                part(shard, half), place(links.dp, half), links.beside
            )
            for step in range(1, links.num_far):
                spot = place(links.far_from(step), half)
                self.second[half, step] = links.copy(spot, spot, links.beside)

    def begin(self, half):
        for step in range(1, self.links.num_far):
            self.first[half, step].start()

    def begin_beside(self, half):
        self.second[half, 0].start()

    def keep_own(self):
        self.full[self.links.dp] = self.shard[...]

    def forward(self, half):
        for step in range(1, self.links.num_far):
            self.first[half, step].wait_recv()
            self.second[half, step].start()

    def end(self, halves):
        for half in halves:
            for step in range(self.links.num_far):
                self.second[half, step].wait_recv()


class RowSum:
    def __init__(self, links, part, side, home, far):
        self.links, self.part = links, part
        self.side, self.home, self.far = side, home, far
        self.block = part.shape[0] // 4
        self.rows = self.block // CHUNKS
        me = links.tensor
        cuts = [self.cut(chunk) for chunk in range(CHUNKS)]
        self.side_in = [
            links.copy(part.at[self.of(me ^ 3, chunk)], side.at[cuts[chunk]], links.sibling)
            for chunk in range(CHUNKS)
        ]
        self.home_in = [
            links.copy(part.at[self.of(me ^ 1, chunk)], home.at[cuts[chunk]], links.sibling)
            for chunk in range(CHUNKS)
        ]
        self.far_in = [
            links.copy(side.at[cuts[chunk]], far.at[cuts[chunk]], links.across)
            for chunk in range(CHUNKS)
        ]

    def cut(self, chunk):
        return pl.ds(chunk * self.rows, self.rows)

    def of(self, member, chunk):
        return rows_at(member * self.block + chunk * self.rows, self.rows)

    def begin_side(self):
        for made in self.side_in:
            made.start()

    def begin_home(self):
        for made in self.home_in:
            made.start()

    def pass_on(self, chunk):
        cut = self.cut(chunk)
        self.side_in[chunk].wait_recv()
        mine = self.part[self.of(self.links.tensor ^ 2, chunk), :]
        self.side[cut, :] = (mine.astype(F32) + self.side[cut, :].astype(F32)).astype(BF)
        self.far_in[chunk].start()

    def total(self, chunk):
        cut = self.cut(chunk)
        self.home_in[chunk].wait_recv()
        self.far_in[chunk].wait_recv()
        return (
            self.part[self.of(self.links.tensor, chunk), :].astype(F32)
            + self.home[cut, :].astype(F32)
            + self.far[cut, :].astype(F32)
        )


class RowSpread:
    def __init__(self, links, own, gathered):
        self.block = own.shape[0]
        self.rows = self.block // CHUNKS
        self.own, self.gathered, self.links = own, gathered, links
        me = links.tensor
        self.across_in, self.sibling_in, self.corner_in = [], [], []
        for chunk in range(CHUNKS):
            source, place = own.at[self.cut(chunk)], gathered.at[self.of(me, chunk)]
            self.across_in.append(links.copy(source, place, links.across))
            self.sibling_in.append(links.copy(source, place, links.sibling))
        for chunk in range(CHUNKS):
            place = gathered.at[self.of(me ^ 2, chunk)]
            self.corner_in.append(links.copy(place, place, links.sibling))

    def cut(self, chunk):
        return pl.ds(chunk * self.rows, self.rows)

    def of(self, member, chunk):
        return rows_at(member * self.block + chunk * self.rows, self.rows)

    def give(self, chunk):
        self.across_in[chunk].start()
        self.sibling_in[chunk].start()
        self.gathered[self.of(self.links.tensor, chunk), :] = self.own[self.cut(chunk), :]

    def hand_over(self, chunk):
        self.across_in[chunk].wait_recv()
        self.corner_in[chunk].start()

    def await_sibling(self):
        for made in self.sibling_in:
            made.wait_recv()

    def await_corner(self):
        for made in self.corner_in:
            made.wait_recv()


class GradScatter:
    def __init__(self, links, grads, beside, landed, result, start=0, stop=None):
        stop = stop or grads.shape[2]
        lanes = pl.ds(start, stop - start)
        grads, beside, landed = (ref.at[:, :, lanes] for ref in (grads, beside, landed))
        result = result.at[:, lanes]
        self.links, self.grads, self.beside = links, grads, beside
        self.landed, self.result = landed, result
        self.slab = beside.shape[1]
        self.beside_in, self.far_in = {}, {}
        for step in range(links.num_far):
            target = links.far(step)
            self.beside_in[step] = links.copy(
                grads.at[target ^ 1], beside.at[step], links.beside
            )
            if step:
                self.far_in[step] = links.copy(
                    beside.at[step], landed.at[step], (target, links.tensor)
                )

    def begin(self):
        for step in range(1, self.links.num_far + 1):
            self.beside_in[step % self.links.num_far].start()

    def pass_on(self, step):
        self.beside_in[step].wait_recv()
        mine = self.grads[self.links.far(step)]
        self.beside[step] = (mine.astype(F32) + self.beside[step].astype(F32)).astype(BF)
        self.far_in[step].start()

    def end(self):
        self.beside_in[0].wait_recv()
        total = self.grads[self.links.dp].astype(F32) + self.beside[0].astype(F32)
        for step in range(1, self.links.num_far):
            self.far_in[step].wait_recv()
            total = total + self.landed[step].astype(F32)
        self.result[...] = total


class Refs:
    def __init__(self, names, refs):
        for name, ref in zip(names, refs, strict=True):
            setattr(self, name, ref)


def flat_weight(full, wide, start=0, stop=None):
    count, slab, width = full.shape
    stop = stop or width
    if slab % 16 == 0:
        return full[:, :, start:stop].reshape(count * slab, stop - start)
    for at in range(count):
        wide[at * slab : (at + 1) * slab, start:stop] = full[at, :, start:stop].astype(F32)
    return wide[:, start:stop].astype(BF)


def split_rows(value, grads, start, wide, lane=0):
    count, slab, width = grads.shape
    rows, columns = value.shape
    lanes = slice(lane, lane + columns)
    if slab % 16 == 0:
        low = value.astype(BF).reshape(rows // slab, slab, columns)
        grads[pl.ds(start // slab, rows // slab), :, lanes] = low
        return
    wide[0:rows, lanes] = value
    for at in range(rows // slab):
        grads[start // slab + at, :, lanes] = wide[at * slab : (at + 1) * slab, lanes].astype(BF)


def turn(value):
    rows, columns = value.shape
    tall = jnp.concatenate(
        [value.astype(F32), jnp.zeros((rows, 128 - columns), F32)], axis=1
    )
    return jnp.transpose(tall)[:columns, :].astype(value.dtype)


def layer_kernel(num_dp, names, *refs):
    r = Refs(names, refs)
    links = Links(num_dp, r.send_sems, r.recv_sems)
    me, dp = links.tensor, links.dp
    block, width = r.frames.shape
    length = 4 * block
    num_blocks = length // BLOCK
    heads_width = width // 4
    heads = heads_width // HD
    qkv = 3 * heads_width
    upper = me // 2

    await_all = links.greet(links.others + [links.sibling, links.across, links.corner])

    small_group = [
        links.copy(r.small_mine, r.small_group.at[at], device)
        for at, device in enumerate((links.sibling, links.across, links.corner))
    ]
    small_dp = [
        links.copy(r.small_sum, r.small_dp.at[at], other) for at, other in enumerate(links.others)
    ]
    frame_rows = RowSpread(links, r.frames, r.rows_all)
    given_rows = RowSpread(links, r.cotangent, r.given_all)
    spread_a = WeightSpread(links, r.shard_a, r.full_a, (0, width // 2, width * 5 // 6, width))
    spread_b = WeightSpread(links, r.shard_b, r.full_b, (0, width // 2, width))
    spread_c = WeightSpread(links, r.shard_c, r.full_c, (0, width // 2, width))

    r.shard_a[:, :qkv] = jnp.concatenate([r.in_weight[at] for at in range(3)], axis=1)
    r.shard_a[:, qkv:] = turn(r.out_weight[...])
    own, share = width // (4 * num_dp), HD // num_dp
    r.small_mine[...] = jnp.zeros_like(r.small_mine)
    for at in range(6):
        r.small_mine[at : at + 1, 0:own] = getattr(r, f"vec_{at}")[...]
    r.small_mine[0:6, :] = pltpu.roll(r.small_mine[0:6, :], (dp * 4 + me) * own, 1)
    lane = lax.broadcasted_iota(jnp.int32, (1, width), 1)

    def one_hot(rows, target):
        return jnp.where(
            lax.broadcasted_iota(jnp.int32, (rows, width), 0) == target, 1.0, 0.0
        ).astype(BF)

    tall = dot_nn(r.fc1_bias[...], one_hot(width // HD, lane // HD))
    within = lane % HD - dp * share
    r.small_mine[6:7, :] = column_sum(
        jnp.where(lax.broadcasted_iota(jnp.int32, tall.shape, 0) == within, tall, 0.0)
    )
    row = jnp.zeros((1, width), F32)
    for head in range(heads):
        pair = dot_nn(r.proj_bias[head], one_hot(share, within))
        for at in range(2):
            here = lane // HD == at * (LANE_GAP // HD) + head
            row = row + jnp.where(here, pair[at : at + 1, :], 0.0)
    r.small_mine[7:8, :] = row
    ids = r.seg_row[0:1, :].astype(F32)
    r.seg_wide[...] = jnp.transpose(jnp.broadcast_to(ids, (128, length)))
    await_all()
    for made in small_group:
        made.start()
    for chunk in range(CHUNKS):
        frame_rows.give(chunk)
    spread_a.begin(0)
    spread_a.begin_beside(0)

    total = r.small_mine[...]
    for at, made in enumerate(small_group):
        made.wait_recv()
        total = total + jnp.where(
            lax.broadcasted_iota(jnp.int32, total.shape, 0) < 6, r.small_group[at], 0.0
        )
    r.small_sum[...] = total
    for made in small_dp:
        made.start()
    for half in (1, 2):
        spread_a.begin(half)
        spread_a.begin_beside(half)
    for chunk in range(CHUNKS):
        given_rows.give(chunk)
    for spread in (spread_b, spread_c):
        for half in range(2):
            spread.begin(half)
            spread.begin_beside(half)
    for spread in (spread_a, spread_b, spread_c):
        spread.keep_own()

    gain_one, shift_one, gain_two, shift_two, bias_out, bias_fc2 = range(6)

    def vec(at):
        return r.vecs[at : at + 1, :]

    def normalise(first):
        @pl.loop(0, num_blocks // 2)
        def first_norm(at):
            rows = rows_at((at + first * (num_blocks // 2)) * BLOCK, BLOCK)
            low = layer_norm(r.rows_all[rows, :].astype(F32), vec(gain_one), vec(shift_one))
            r.normed[rows, :] = low.astype(BF)

    frame_rows.hand_over(0)
    spread_a.forward(0)
    for at, made in enumerate(small_dp):
        made.wait_recv()
        total = total + r.small_dp[at]
    r.vecs[...] = total
    frame_rows.await_sibling()
    normalise(upper)
    frame_rows.hand_over(1)
    spread_a.forward(1)
    frame_rows.hand_over(2)
    spread_a.forward(2)
    frame_rows.await_corner()
    normalise(1 - upper)
    spread_a.end((0, 1))

    @pl.loop(0, num_blocks)
    def project(at):
        rows = rows_at(at * BLOCK, BLOCK)
        low = r.normed[rows, :]
        made = dot_nn(low, flat_weight(r.full_a, r.wide, 0, qkv))
        made_query = (made[:, :heads_width] + r.vecs[7:8, 0:heads_width]).astype(BF)
        r.query[rows, :] = made_query * jnp.asarray(0.125, BF)
        r.keys[rows, :] = made[:, heads_width : 2 * heads_width].astype(BF)
        shift = r.vecs[7:8, LANE_GAP : LANE_GAP + heads_width]
        made_values = (made[:, 2 * heads_width :] + shift).astype(BF)
        r.values[rows, :] = made_values
        r.turned[:, rows] = jnp.transpose(made_values)

    reach = (DOCUMENT_LIMIT - 2) // BLOCK + 1
    spans = sorted(
        {
            min(num_blocks - 1, spot + reach) - max(0, spot - reach) + 1
            for spot in range(num_blocks)
        }
    )

    def by_span(spot, run):
        first = jnp.maximum(spot - reach, 0)
        count = jnp.minimum(spot + reach, num_blocks - 1) - first + 1
        for span in spans:

            @pl.when(count == span)
            def this_span(span=span):
                run(first * BLOCK, span * BLOCK)

    def mask_of(rows, near, size):
        keys_ids = jnp.concatenate([r.seg_wide[near, :]] * (BLOCK // 128), axis=1)
        query_ids = r.seg_row[0:1, rows].astype(F32)
        r.mask[0:size, :] = jnp.where(keys_ids == query_ids, 0.0, -1e30)

    spread_a.end((2,))
    spread_b.forward(0)
    sum_one = RowSum(links, r.part_one, r.side_one, r.home_one, r.far_one)
    spread_two = RowSpread(links, r.normed_own, r.normed_two)

    @pl.loop(0, num_blocks)
    def attend(at):
        spot = lax.rem(at + (1 - upper) * (num_blocks // 2), num_blocks)
        rows = rows_at(spot * BLOCK, BLOCK)

        def mix(start, size):
            near = rows_at(start, size)
            mask_of(rows, near, size)
            asked = r.query[rows, :]
            made = []
            for head in range(heads):
                scores = dot_nt(r.keys[near, :], head_part(asked, head)) + r.mask[0:size, :]
                top = jnp.max(scores, axis=0, keepdims=True)
                weights = jnp.exp(scores - top)
                whole = column_sum(weights)
                given_t = r.turned[head * HD : (head + 1) * HD, near]
                made.append(dot_nn(given_t, weights.astype(BF)) / whole)
                r.stats[spot, head : head + 1, :] = top + jnp.log(whole)
            r.mixed[rows, :] = jnp.transpose(jnp.concatenate(made, axis=0)).astype(BF)

        by_span(spot, mix)
        out = r.mixed[rows, :]
        r.part_one[rows, :] = dot_nt(out, flat_weight(r.full_a, r.wide, qkv)).astype(BF)

        def after(step, core=None):
            return pl.when((at == step) if core is None else ((at == step) & (me % 2 == core)))

        @after(0, 1)
        def upper_first():
            sum_one.side_in[0].start()
            sum_one.side_in[1].start()

        @after(1, 0)
        def lower_second():
            sum_one.pass_on(0)
            sum_one.pass_on(1)
            sum_one.side_in[0].start()

        @after(1, 1)
        def upper_second():
            sum_one.side_in[2].start()

        @after(1)
        def rows_first():
            given_rows.hand_over(0)
            spread_b.forward(1)

        @after(2, 0)
        def lower_third():
            sum_one.side_in[1].start()
            sum_one.side_in[2].start()
            sum_one.pass_on(2)

        @after(2, 1)
        def upper_third():
            sum_one.pass_on(0)

        @after(3, 1)
        def upper_fourth():
            sum_one.pass_on(1)
            sum_one.pass_on(2)

        @after(3)
        def rows_second():
            given_rows.hand_over(1)

        @after(4)
        def weights_second():
            spread_c.forward(0)

    sum_one.begin_home()
    given_rows.hand_over(2)
    r.grad_keys[...] = jnp.zeros_like(r.grad_keys)
    r.grad_values[...] = jnp.zeros_like(r.grad_values)

    @pl.loop(0, num_blocks)
    def turn_keys(at):
        rows = rows_at(at * BLOCK, BLOCK)
        r.turned[:, rows] = jnp.transpose(r.keys[rows, :])

    spread_b.end((0, 1))

    def pair_rows(chunk, member):
        start = chunk * (block // CHUNKS)
        return (
            rows_at(member * block + start, block // CHUNKS),
            rows_at((member ^ 1) * block + start, block // CHUNKS),
        )

    def both(ref, pair):
        return jnp.concatenate([ref[rows, :] for rows in pair], axis=0)

    def put(ref, pair, value):
        low = value.astype(BF)
        ref[pair[0], :] = low[: block // CHUNKS]
        ref[pair[1], :] = low[block // CHUNKS :]

    def hide(pair):
        hidden = dot_nn(both(r.normed_two, pair), flat_weight(r.full_b, r.wide)) + r.vecs[6:7, :]
        below, density = normal_parts(hidden)
        put(r.active, pair, hidden * below)
        put(r.part_two, pair, below + hidden * density)

    @pl.loop(0, CHUNKS)
    def second_norm(at):
        for chunk in range(CHUNKS):

            @pl.when(at == chunk)
            def rows_of(chunk=chunk):
                cut = sum_one.cut(chunk)
                row = r.frames[cut, :].astype(F32) + (sum_one.total(chunk) + vec(bias_out))
                r.middle[cut, :] = row
                r.normed_own[cut, :] = layer_norm(row, vec(gain_two), vec(shift_two)).astype(BF)
                spread_two.give(chunk)
                if chunk == 0:
                    spread_c.forward(1)
                spread_two.sibling_in[chunk].wait_recv()

        hide(pair_rows(at, me))

    links.sent(sum_one.far_in + frame_rows.corner_in)
    given_rows.await_sibling()
    given_rows.await_corner()
    spread_c.end((0, 1))

    sum_two = RowSum(links, r.part_two, r.side_two, r.home_two, r.far_two)
    sum_three = RowSum(links, r.normed_two, r.side_three, r.home_three, r.far_three)
    r.small_grads[...] = jnp.zeros_like(r.small_grads)

    @pl.loop(0, 2 * CHUNKS)
    def feed(at):
        def when_at(step):
            return pl.when(at == step)

        for chunk in range(CHUNKS):

            @when_at(2 * chunk)
            def bring(chunk=chunk):
                spread_two.hand_over(chunk)

            @when_at(2 * chunk + 1)
            def remote(chunk=chunk):
                if chunk:
                    sum_two.pass_on(chunk - 1)
                spread_two.corner_in[chunk].wait_recv()

        pair = pair_rows(at // 2, me ^ (2 * (at % 2)))

        @pl.when(at % 2 == 1)
        def remote_first():
            hide(pair)

        grad_active = dot_nn(both(r.given_all, pair), flat_weight(r.full_c, r.wide))
        back = (grad_active * both(r.part_two, pair).astype(F32)).astype(BF)
        put(r.grad_hidden, pair, back)
        put(r.part_two, pair, dot_nt(back, flat_weight(r.full_b, r.wide)))
        r.small_grads[6:7, :] += column_sum(back.astype(F32))

        for chunk in range(CHUNKS):

            @when_at(2 * chunk)
            def near_done(chunk=chunk):
                sum_two.home_in[chunk].start()

            @when_at(2 * chunk + 1)
            def remote_done(chunk=chunk):
                sum_two.side_in[chunk].start()

    sum_two.pass_on(CHUNKS - 1)
    scatter_b = GradScatter(links, r.grads_b, r.beside_b, r.landed_b, r.out_b)
    scatter_c = GradScatter(links, r.grads_c, r.beside_c, r.landed_c, r.out_c)

    spread_three = RowSpread(links, r.attended_own, r.rows_all)

    def second_norm_back(chunk):
        cut = sum_two.cut(chunk)
        grad = sum_two.total(chunk)
        back, unit = layer_norm_back(r.middle[cut, :], grad, vec(gain_two))
        given = r.cotangent[cut, :].astype(F32)
        row = given + back
        r.grad_middle[cut, :] = row
        low = row.astype(BF)
        r.attended_own[cut, :] = low
        spread_three.give(chunk)
        r.small_grads[gain_two : gain_two + 1, :] += column_sum(grad * unit)
        r.small_grads[shift_two : shift_two + 1, :] += column_sum(grad)
        r.small_grads[bias_out : bias_out + 1, :] += column_sum(low.astype(F32))
        r.small_grads[bias_fc2 : bias_fc2 + 1, :] += column_sum(given)

    def weigh_one(at):
        columns = rows_at(at * block, block)
        made = dot_tn(r.normed_two[:, columns], r.grad_hidden[...])
        split_rows(made, r.grads_b, at * block, r.wide)

    def weigh_two(at):
        columns = rows_at(at * block, block)
        made = dot_tn(r.given_all[:, columns], r.active[...])
        split_rows(made, r.grads_c, at * block, r.wide)

    second_norm_back(0)
    weigh_one(0)
    second_norm_back(1)
    weigh_one(1)
    scatter_b.begin()
    weigh_two(0)
    second_norm_back(2)
    weigh_two(1)
    scatter_c.begin()
    links.sent(spread_two.corner_in)

    @pl.loop(0, 4)
    def branch(at):
        rows = rows_at((me ^ (3 - at)) * block, block)
        made = dot_nt(r.active[rows, :], flat_weight(r.full_c, r.wide))
        r.normed_two[rows, :] = made.astype(BF)

        @pl.when(at == 0)
        def corner_done():
            sum_three.begin_side()

        @pl.when(at == 2)
        def sibling_done():
            sum_three.begin_home()

    spread_three.await_sibling()

    @pl.loop(0, num_blocks)
    def attend_back(at):
        def when_at(step):
            return pl.when(at == step)

        @when_at(1)
        def first_service():
            for chunk in range(CHUNKS):
                sum_three.pass_on(chunk)
            spread_three.hand_over(0)
            spread_three.hand_over(1)
            scatter_b.pass_on(1)
            scatter_b.pass_on(2)

        @when_at(2)
        def second_service():
            spread_three.hand_over(2)
            for step in range(3, links.num_far):
                scatter_b.pass_on(step)

        @when_at(3)
        def third_service():
            spread_three.await_corner()

        @when_at(4)
        def fourth_service():
            scatter_c.pass_on(1)

        @when_at(5)
        def fifth_service():
            for step in range(2, links.num_far):
                scatter_c.pass_on(step)

        spot = lax.rem(at + upper * (num_blocks // 2), num_blocks)
        rows = rows_at(spot * BLOCK, BLOCK)
        asked = r.query[rows, :]
        given = dot_nn(r.rows_all[rows, :], flat_weight(r.full_a, r.wide, qkv)).astype(BF)
        joint = jnp.transpose(given.astype(F32) * r.mixed[rows, :].astype(F32))
        asked_heads = [head_part(asked, head) for head in range(heads)]
        given_heads = [head_part(given, head) for head in range(heads)]

        def unmix(start, size):
            near = rows_at(start, size)
            mask_of(rows, near, size)
            made = []
            for head in range(heads):
                lanes = slice(head * BLOCK, (head + 1) * BLOCK)
                scores = dot_nt(r.keys[near, :], asked_heads[head]) + r.mask[0:size, :]
                probs = jnp.exp(scores - r.stats[spot, head : head + 1, :])
                inner = column_sum(joint[head * HD : (head + 1) * HD, :])
                slopes = dot_nt(r.values[near, :], given_heads[head]) - inner
                slopes = (probs * slopes).astype(BF)
                r.active[0:size, lanes] = probs.astype(BF)
                r.grad_hidden[0:size, lanes] = slopes
                made.append(dot_nn(r.turned[head * HD : (head + 1) * HD, near], slopes))
            given_tall = jnp.concatenate(given_heads, axis=0)
            asked_tall = jnp.concatenate(asked_heads, axis=0)
            r.grad_values[near, :] += dot_nn(r.active[0:size, :], given_tall)
            r.grad_keys[near, :] += dot_nn(r.grad_hidden[0:size, :], asked_tall)
            turned = jnp.transpose(jnp.concatenate(made, axis=0)) * 0.125
            r.grad_proj[rows, :heads_width] = turned.astype(BF)

        by_span(spot, unmix)

    links.sent(sum_one.side_in + sum_one.home_in)
    sum_four = RowSum(links, r.part_one, r.side_one, r.home_one, r.far_one)

    def join(rows):
        low_keys = r.grad_keys[rows, :].astype(BF)
        low_values = r.grad_values[rows, :].astype(BF)
        low_query = r.grad_proj[rows, :heads_width]
        whole = jnp.concatenate([low_query, low_keys, low_values], axis=1)
        r.grad_proj[rows, :] = whole
        wide_sum = column_sum(whole.astype(F32))
        r.small_grads[7:8, 0:heads_width] += wide_sum[:, 0:heads_width]
        r.small_grads[7:8, LANE_GAP : LANE_GAP + heads_width] += wide_sum[:, 2 * heads_width :]

    def push(rows):
        made = dot_nt(r.grad_proj[rows, :], flat_weight(r.full_a, r.wide, 0, qkv))
        r.part_one[rows, :] = made.astype(BF)

    scatter_o = GradScatter(
        links, r.grads_a, r.beside_a, r.landed_a, r.out_a, width * 5 // 6, width
    )

    @pl.loop(0, width // block)
    def weigh_out(at):
        columns = rows_at(at * block, block)
        split_rows(dot_tn(r.rows_all[:, columns], r.mixed[...]), r.grads_a, at * block, r.wide, qkv)

    scatter_o.begin()

    @pl.loop(0, 2)
    def project_remote(at):
        rows = rows_at((me ^ (3 - at)) * block, block)
        join(rows)
        push(rows)

        @pl.when(at == 0)
        def corner_done():
            sum_four.begin_side()

        @pl.when(at == 1)
        def across_done():
            for chunk in range(CHUNKS):
                sum_four.pass_on(chunk)

    @pl.loop(0, 2)
    def join_near(at):
        join(rows_at((me ^ at) * block, block))

    middle_lane = width // 2
    scatter_a = [
        GradScatter(links, r.grads_a, r.beside_a, r.landed_a, r.out_a, *lanes)
        for lanes in ((0, middle_lane), (middle_lane, width * 5 // 6))
    ]

    @pl.loop(0, width // block)
    def weigh_in(at):
        columns = rows_at(at * block, block)
        made = dot_tn(r.normed[:, columns], r.grad_proj[:, 0:middle_lane])
        split_rows(made, r.grads_a, at * block, r.wide, 0)

    scatter_a[0].begin()
    for step in range(1, links.num_far):
        scatter_o.pass_on(step)

    @pl.loop(0, width // block)
    def weigh_in_too(at):
        columns = rows_at(at * block, block)
        made = dot_tn(r.normed[:, columns], r.grad_proj[:, middle_lane:qkv])
        split_rows(made, r.grads_a, at * block, r.wide, middle_lane)

    scatter_a[1].begin()

    @pl.loop(0, 2)
    def project_near(at):
        push(rows_at((me ^ (1 - at)) * block, block))

    sum_four.begin_home()
    def first_norm_back(chunk):
        cut = sum_four.cut(chunk)
        grad = sum_four.total(chunk)
        back, unit = layer_norm_back(r.frames[cut, :].astype(F32), grad, vec(gain_one))
        r.grad_frames[cut, :] = r.grad_middle[cut, :] + back
        keep_result("grad_frames", cut)
        r.small_grads[gain_one : gain_one + 1, :] += column_sum(grad * unit)
        r.small_grads[shift_one : shift_one + 1, :] += column_sum(grad)

    kept = []

    def keep_result(name, cut=None):
        source, place = getattr(r, name), getattr(r, name + "_hbm")
        if cut is not None:
            source, place = source.at[cut], place.at[cut]
        made = pltpu.make_async_copy(source, place, r.local_sems.at[len(kept)])
        made.start()
        kept.append(made)

    scatter_b.end()
    keep_result("out_b")
    scatter_a[0].pass_on(1)
    first_norm_back(0)
    for step in range(2, links.num_far):
        scatter_a[0].pass_on(step)
    for chunk in range(CHUNKS):
        cut = sum_three.cut(chunk)
        row = r.middle[cut, :] + (sum_three.total(chunk) + vec(bias_fc2))
        r.output[cut, :] = row.astype(BF)
    keep_result("output")
    first_norm_back(1)
    scatter_a[1].pass_on(1)
    scatter_a[1].pass_on(2)
    first_norm_back(2)

    back_group = [
        links.copy(r.small_grads, r.small_group_back.at[at], device)
        for at, device in enumerate((links.sibling, links.across, links.corner))
    ]
    back_dp = [
        links.copy(r.small_total, r.small_dp.at[at], other)
        for at, other in enumerate(links.others)
    ]
    for made in back_group:
        made.start()
    for step in range(3, links.num_far):
        scatter_a[1].pass_on(step)
    total = r.small_grads[...]
    for at, made in enumerate(back_group):
        made.wait_recv()
        total = total + jnp.where(
            lax.broadcasted_iota(jnp.int32, total.shape, 0) < 6, r.small_group_back[at], 0.0
        )
    r.small_total[...] = total
    for made in back_dp:
        made.start()
    scatter_c.end()
    keep_result("out_c")
    scatter_o.end()
    for scatter in scatter_a:
        scatter.end()
    keep_result("out_a")
    for at, made in enumerate(back_dp):
        made.wait_recv()
        total = total + r.small_dp[at]
    start = (dp * 4 + me) * own
    r.small_out[0:6, :] = pltpu.roll(total[0:6, :], lax.rem(width - start, width), 1)
    start = dp * share
    r.small_out[6:8, :] = pltpu.roll(total[6:8, :], lax.rem(width - start, width), 1)
    keep_result("small_out")
    links.finish()
    for made in kept:
        made.wait()


def copy_count(num_dp):
    far = num_dp // 2
    smalls = 2 * (num_dp - 1 + 3)
    spreads = 4 * 3 * CHUNKS
    weights = (3 + 2 + 2) * (2 * far - 1)
    sums = 4 * 3 * CHUNKS
    scatters = 5 * (2 * far - 1)
    return smalls + spreads + weights + sums + scatters


def layer(num_dp, seg, frames, cotangent, vecs, proj_bias, fc1_bias, in_weight, out_weight, shard_b, shard_c):
    block, width = frames.shape
    length, slab = 4 * block, shard_b.shape[0]
    heads_width = width // 4
    num_blocks = length // BLOCK
    vmem = pl.BlockSpec(memory_space=pltpu.VMEM)
    inputs = [
        ("seg_row", seg, vmem),
        ("frames", frames, vmem),
        ("cotangent", cotangent, vmem),
        ("proj_bias", proj_bias, vmem),
        ("fc1_bias", fc1_bias, vmem),
        ("in_weight", in_weight, vmem),
        ("out_weight", out_weight, vmem),
        ("shard_b", shard_b, vmem),
        ("shard_c", shard_c, vmem),
    ]
    inputs += [(f"vec_{at}", value, vmem) for at, value in enumerate(vecs)]
    outputs = [
        ("output", (block, width), BF),
        ("grad_frames", (block, width), F32),
        ("out_a", (slab, width), F32),
        ("out_b", (slab, width), F32),
        ("out_c", (slab, width), F32),
        ("small_out", (8, width), F32),
    ]
    scratch = [("rows_all", (length, width), BF), ("given_all", (length, width), BF)]
    scratch += [("normed", (length, width), BF), ("normed_two", (length, width), BF)]
    scratch += [("active", (length, width), BF), ("grad_hidden", (length, width), BF)]
    scratch += [(f"full_{tag}", (num_dp, slab, width), BF) for tag in "abc"]
    scratch += [(f"grads_{tag}", (num_dp, slab, width), BF) for tag in "abc"]
    for tag in "abc":
        scratch += [
            (f"{kind}_{tag}", (num_dp // 2, slab, width), BF)
            for kind in ("beside", "landed")
        ]
    for tag in ("one", "two", "three"):
        if tag != "three":
            scratch += [(f"part_{tag}", (length, width), BF)]
        scratch += [
            (f"{kind}_{tag}", (block, width), BF) for kind in ("side", "home", "far")
        ]
    scratch += [
        (name, (length, heads_width), BF)
        for name in ("query", "keys", "values", "mixed")
    ]
    scratch += [
        ("turned", (heads_width, length), BF),
        ("grad_keys", (length, heads_width), F32),
        ("grad_values", (length, heads_width), F32),
        ("grad_proj", (length, 3 * heads_width), BF),
        ("mask", (length, BLOCK), F32),
        ("seg_wide", (length, 128), F32),
        ("stats", (num_blocks, 8, BLOCK), F32),
        ("middle", (block, width), F32),
        ("grad_middle", (block, width), F32),
        ("normed_own", (block, width), BF),
        ("attended_own", (block, width), BF),
        ("vecs", (8, width), F32),
        ("shard_a", (slab, width), BF),
        ("wide", (width if slab % 16 else 8, width), F32),
    ]
    for name in ("small_mine", "small_sum", "small_grads", "small_total"):
        scratch += [(name, (8, width), F32)]
    for name in ("small_group", "small_group_back"):
        scratch += [(name, (3, 8, width), F32)]
    scratch += [("small_dp", (num_dp - 1, 8, width), F32)]
    scratch += outputs
    outputs = [(name + "_hbm", shape, kind) for name, shape, kind in outputs]
    count = copy_count(num_dp)
    names = [name for name, _, _ in inputs + outputs + scratch]
    names += ["send_sems", "recv_sems", "local_sems"]
    return pl.pallas_call(
        functools.partial(layer_kernel, num_dp, names),
        out_shape=[jax.ShapeDtypeStruct(shape, kind) for _, shape, kind in outputs],
        in_specs=[spec for _, _, spec in inputs],
        out_specs=[pl.BlockSpec(memory_space=pl.ANY)] * len(outputs),
        scratch_shapes=[pltpu.VMEM(shape, kind) for _, shape, kind in scratch]
        + [pltpu.SemaphoreType.DMA((count,))] * 2
        + [pltpu.SemaphoreType.DMA((8,))],
        compiler_params=pltpu.CompilerParams(
            collective_id=0, has_side_effects=True, vmem_limit_bytes=VMEM_BYTES
        ),
        name="layer",
    )(*[value for _, value, _ in inputs])


def unpack_kernel(own, share, output, grad_frames, grads_a_in, grads_b, grads_c, sums_in, output_too, grad_frames_too, g_in, g_proj, g_out, grads_b_too, g_fc1b, grads_c_too, vec_0, vec_1, vec_2, vec_3, vec_4, vec_5, output_v, grad_frames_v, grads_a, grads_b_v, grads_c_v, sums, in_sems, out_sems):
    pieces = grad_frames.shape[0] // CHUNKS
    cuts = [pl.ds(at * pieces, pieces) for at in range(CHUNKS)]
    moves = [(sums_in, sums, None), (grads_a_in, grads_a, None)]
    moves += [(grads_b, grads_b_v, grads_b_too), (grads_c, grads_c_v, grads_c_too)]
    moves += [(output, output_v, output_too)]
    moves += [
        (grad_frames.at[cut], grad_frames_v.at[cut], grad_frames_too.at[cut]) for cut in cuts
    ]
    inward = [
        pltpu.make_async_copy(source, held, in_sems.at[at])
        for at, (source, held, _) in enumerate(moves)
    ]
    for made in inward:
        made.start()
    inward[0].wait()
    inward[1].wait()
    copies = []
    for at in range(2, len(moves)):
        inward[at].wait()
        made = pltpu.make_async_copy(moves[at][1], moves[at][2], out_sems.at[at])
        made.start()
        copies.append(made)
    heads_width = g_in.shape[2]
    for at in range(3):
        g_in[at] = grads_a[:, at * heads_width : (at + 1) * heads_width]
    g_out[...] = jnp.transpose(grads_a[:, 3 * heads_width :])
    for at, vec in enumerate((vec_0, vec_1, vec_2, vec_3, vec_4, vec_5)):
        vec[...] = sums[at : at + 1, 0:own]
    width = sums.shape[1]
    pieces = [
        pltpu.roll(sums[...], (width - at * HD) % width, 1)[6:7, 0:128] for at in range(width // HD)
    ]
    pieces.append(jnp.zeros((16 - len(pieces), 128), F32))
    g_fc1b[...] = jnp.transpose(jnp.concatenate(pieces, axis=0))[0:share, 0 : width // HD]
    for head in range(heads_width // HD):
        for at in range(2):
            start = at * LANE_GAP + head * HD
            piece = pltpu.roll(sums[...], (width - start) % width, 1)
            g_proj[head, at : at + 1, :] = piece[7:8, 0:share]
    for made in copies:
        made.wait()


def unpack(own, share, results):
    output, grad_frames, grads_a, grads_b, grads_c, sums = results
    slab, width = grads_a.shape
    heads_width = width // 4
    vmem, hbm = pl.BlockSpec(memory_space=pltpu.VMEM), pl.BlockSpec(memory_space=pl.ANY)
    shapes = [
        (output.shape, BF, hbm),
        (grad_frames.shape, F32, hbm),
        ((3, slab, heads_width), F32, vmem),
        ((heads_width // HD, 2, share), F32, vmem),
        ((heads_width, slab), F32, vmem),
        ((slab, width), F32, hbm),
        ((share, width // HD), F32, vmem),
        ((slab, width), F32, hbm),
    ] + [((1, own), F32, vmem)] * 6
    return pl.pallas_call(
        functools.partial(unpack_kernel, own, share),
        out_shape=[jax.ShapeDtypeStruct(shape, kind) for shape, kind, _ in shapes],
        in_specs=[hbm] * 6,
        out_specs=[spec for _, _, spec in shapes],
        scratch_shapes=[pltpu.VMEM(value.shape, value.dtype) for value in results]
        + [pltpu.SemaphoreType.DMA((2 + 3 + CHUNKS,))] * 2,
        compiler_params=pltpu.CompilerParams(vmem_limit_bytes=VMEM_BYTES),
        name="unpack",
    )(*results)


def on_device(
    num_dp,
    frames,
    segments,
    norm1_gain,
    norm1_shift,
    in_weight,
    proj_bias,
    out_weight,
    out_bias,
    norm2_gain,
    norm2_shift,
    fc1_weight,
    fc1_bias,
    fc2_weight,
    fc2_bias,
    cotangent,
):
    slab, _, heads_width = in_weight.shape
    vecs = [norm1_gain, norm1_shift, norm2_gain, norm2_shift, out_bias, fc2_bias]
    results = layer(
        num_dp,
        segments,
        frames,
        cotangent,
        [value[None] for value in vecs],
        proj_bias.transpose(1, 0, 2),
        fc1_bias.T,
        in_weight.transpose(1, 0, 2),
        out_weight,
        fc1_weight,
        fc2_weight.T,
    )
    output, grad_frames, g_in, g_proj, g_out, g_b, g_fc1b, g_c, *rows = unpack(
        norm1_gain.shape[0], HD // num_dp, results
    )
    rows = [row[0] for row in rows]
    return (
        output,
        grad_frames,
        rows[0],
        rows[1],
        g_in.transpose(1, 0, 2),
        g_proj.transpose(1, 0, 2),
        g_out,
        rows[4],
        rows[2],
        rows[3],
        g_b,
        g_fc1b.T,
        g_c.T,
        rows[5],
    )


def solution(mesh):
    in_specs = (
        P(("dp", "tensor"), None),
        P("dp", None),
        P(("dp", "tensor")),
        P(("dp", "tensor")),
        P("dp", None, "tensor"),
        P(None, "tensor", "dp"),
        P("tensor", "dp"),
        P(("dp", "tensor")),
        P(("dp", "tensor")),
        P(("dp", "tensor")),
        P("dp", "tensor"),
        P("tensor", "dp"),
        P("tensor", "dp"),
        P(("dp", "tensor")),
        P(("dp", "tensor"), None),
    )
    out_specs = (
        P(("dp", "tensor"), None),
        P(("dp", "tensor"), None),
        P(("dp", "tensor")),
        P(("dp", "tensor")),
        P("dp", None, "tensor"),
        P(None, "tensor", "dp"),
        P("tensor", "dp"),
        P(("dp", "tensor")),
        P(("dp", "tensor")),
        P(("dp", "tensor")),
        P("dp", "tensor"),
        P("tensor", "dp"),
        P("tensor", "dp"),
        P(("dp", "tensor")),
    )
    return jax.shard_map(
        functools.partial(on_device, mesh.shape["dp"]),
        mesh=mesh,
        in_specs=in_specs,
        out_specs=out_specs,
        check_vma=False,
    )
```

```python
import functools

import jax
import jax.numpy as jnp
from jax import lax
from jax.experimental import pallas as pl
from jax.experimental.pallas import tpu as pltpu
from jax.sharding import PartitionSpec as P

HD = 64
BF = jnp.bfloat16
F32 = jnp.float32
VMEM_BYTES = 62 << 20
BLOCK = 256
CHUNKS = 3
DOCUMENT_LIMIT = 768
LANE_GAP = 256


def layer_norm(row_block, norm_gain, norm_shift):
    row_mean = jnp.mean(row_block, axis=-1, keepdims=True)
    centred = row_block - row_mean
    row_var = jnp.mean(centred * centred, axis=-1, keepdims=True)
    return centred * lax.rsqrt(row_var + 1e-05) * norm_gain + norm_shift


def layer_norm_back(row, grad, gain):
    mean = jnp.mean(row, axis=-1, keepdims=True)
    centred = row - mean
    scale = lax.rsqrt(jnp.mean(centred * centred, axis=-1, keepdims=True) + 1e-05)
    unit = centred * scale
    scaled = grad * gain
    back = scale * (
        scaled
        - jnp.mean(scaled, axis=-1, keepdims=True)
        - unit * jnp.mean(scaled * unit, axis=-1, keepdims=True)
    )
    return back, unit


def dot_nn(left, right):
    return jnp.dot(left, right, preferred_element_type=F32)


def dot_nt(left, right):
    return lax.dot_general(left, right, (((1,), (1,)), ((), ())), preferred_element_type=F32)


def dot_tn(left, right):
    return lax.dot_general(left, right, (((0,), (0,)), ((), ())), preferred_element_type=F32)


def normal_parts(hidden):
    below = 0.5 + 0.5 * lax.erf(hidden * 0.7071067811865476)
    return below, 0.3989422804014327 * jnp.exp(-0.5 * hidden * hidden)


def column_sum(block):
    return jnp.sum(block, axis=0, keepdims=True)


def head_part(block, head):
    lanes = lax.broadcasted_iota(jnp.int32, block.shape, 1)
    inside = (lanes >= head * HD) & (lanes < (head + 1) * HD)
    return jnp.where(inside, block, jnp.zeros_like(block))


def rows_at(start, size):
    return pl.ds(pl.multiple_of(start, 128), size)


class Links:
    def __init__(self, num_dp, send_sems, recv_sems):
        self.num_dp, self.num_far = num_dp, num_dp // 2
        self.dp, self.tensor = lax.axis_index("dp"), lax.axis_index("tensor")
        self.send_sems, self.recv_sems, self.made, self.done = send_sems, recv_sems, [], []
        self.sibling = (self.dp, self.tensor ^ 1)
        self.across = (self.dp, self.tensor ^ 2)
        self.corner = (self.dp, self.tensor ^ 3)
        self.beside = (self.dp ^ 1, self.tensor)
        self.others = [(lax.rem(self.dp + step, num_dp), self.tensor) for step in range(1, num_dp)]

    def far(self, step):
        return lax.rem(self.dp + 2 * step, self.num_dp)

    def far_from(self, step):
        return lax.rem(self.dp + self.num_dp - 2 * step, self.num_dp)

    def copy(self, src, dst, device):
        at = len(self.made)
        made = pltpu.make_async_remote_copy(
            src_ref=src,
            dst_ref=dst,
            send_sem=self.send_sems.at[at],
            recv_sem=self.recv_sems.at[at],
            device_id=device,
            device_id_type=pl.DeviceIdType.MESH,
        )
        self.made.append(made)
        return made

    def greet(self, devices):
        barrier = pltpu.get_barrier_semaphore()
        for device in devices:
            pl.semaphore_signal(
                barrier, inc=1, device_id=device, device_id_type=pl.DeviceIdType.MESH
            )
        return lambda: pl.semaphore_wait(barrier, len(devices))

    def sent(self, copies):
        for made in copies:
            made.wait_send()
            self.done.append(made)

    def finish(self):
        for made in self.made:
            if not any(made is other for other in self.done):
                made.wait_send()


class WeightSpread:
    def __init__(self, links, shard, full, edges):
        self.links, self.shard, self.full = links, shard, full

        def part(ref, half):
            return ref.at[:, pl.ds(edges[half], edges[half + 1] - edges[half])]

        def place(origin, half):
            return full.at[origin, :, pl.ds(edges[half], edges[half + 1] - edges[half])]

        self.first, self.second = {}, {}
        for half in range(len(edges) - 1):
            for step in range(1, links.num_far):
                self.first[half, step] = links.copy(
                    part(shard, half), place(links.dp, half), (links.far(step), links.tensor)
                )
            self.second[half, 0] = links.copy(
                part(shard, half), place(links.dp, half), links.beside
            )
            for step in range(1, links.num_far):
                spot = place(links.far_from(step), half)
                self.second[half, step] = links.copy(spot, spot, links.beside)

    def begin(self, half):
        for step in range(1, self.links.num_far):
            self.first[half, step].start()

    def begin_beside(self, half):
        self.second[half, 0].start()

    def keep_own(self):
        self.full[self.links.dp] = self.shard[...]

    def forward(self, half):
        for step in range(1, self.links.num_far):
            self.first[half, step].wait_recv()
            self.second[half, step].start()

    def end(self, halves):
        for half in halves:
            for step in range(self.links.num_far):
                self.second[half, step].wait_recv()


class RowSum:
    def __init__(self, links, part, side, home, far):
        self.links, self.part = links, part
        self.side, self.home, self.far = side, home, far
        self.block = part.shape[0] // 4
        self.rows = self.block // CHUNKS
        me = links.tensor
        cuts = [self.cut(chunk) for chunk in range(CHUNKS)]
        self.side_in = [
            links.copy(part.at[self.of(me ^ 3, chunk)], side.at[cuts[chunk]], links.sibling)
            for chunk in range(CHUNKS)
        ]
        self.home_in = [
            links.copy(part.at[self.of(me ^ 1, chunk)], home.at[cuts[chunk]], links.sibling)
            for chunk in range(CHUNKS)
        ]
        self.far_in = [
            links.copy(side.at[cuts[chunk]], far.at[cuts[chunk]], links.across)
            for chunk in range(CHUNKS)
        ]

    def cut(self, chunk):
        return pl.ds(chunk * self.rows, self.rows)

    def of(self, member, chunk):
        return rows_at(member * self.block + chunk * self.rows, self.rows)

    def begin_side(self):
        for made in self.side_in:
            made.start()

    def begin_home(self):
        for made in self.home_in:
            made.start()

    def pass_on(self, chunk):
        cut = self.cut(chunk)
        self.side_in[chunk].wait_recv()
        mine = self.part[self.of(self.links.tensor ^ 2, chunk), :]
        self.side[cut, :] = (mine.astype(F32) + self.side[cut, :].astype(F32)).astype(BF)
        self.far_in[chunk].start()

    def total(self, chunk):
        cut = self.cut(chunk)
        self.home_in[chunk].wait_recv()
        self.far_in[chunk].wait_recv()
        return (
            self.part[self.of(self.links.tensor, chunk), :].astype(F32)
            + self.home[cut, :].astype(F32)
            + self.far[cut, :].astype(F32)
        )


class RowSpread:
    def __init__(self, links, own, gathered):
        self.block = own.shape[0]
        self.rows = self.block // CHUNKS
        self.own, self.gathered, self.links = own, gathered, links
        me = links.tensor
        self.across_in, self.sibling_in, self.corner_in = [], [], []
        for chunk in range(CHUNKS):
            source, place = own.at[self.cut(chunk)], gathered.at[self.of(me, chunk)]
            self.across_in.append(links.copy(source, place, links.across))
            self.sibling_in.append(links.copy(source, place, links.sibling))
        for chunk in range(CHUNKS):
            place = gathered.at[self.of(me ^ 2, chunk)]
            self.corner_in.append(links.copy(place, place, links.sibling))

    def cut(self, chunk):
        return pl.ds(chunk * self.rows, self.rows)

    def of(self, member, chunk):
        return rows_at(member * self.block + chunk * self.rows, self.rows)

    def give(self, chunk):
        self.across_in[chunk].start()
        self.sibling_in[chunk].start()
        self.gathered[self.of(self.links.tensor, chunk), :] = self.own[self.cut(chunk), :]

    def hand_over(self, chunk):
        self.across_in[chunk].wait_recv()
        self.corner_in[chunk].start()

    def await_sibling(self):
        for made in self.sibling_in:
            made.wait_recv()

    def await_corner(self):
        for made in self.corner_in:
            made.wait_recv()


class GradScatter:
    def __init__(self, links, grads, beside, landed, result, start=0, stop=None):
        stop = stop or grads.shape[2]
        lanes = pl.ds(start, stop - start)
        grads, beside, landed = (ref.at[:, :, lanes] for ref in (grads, beside, landed))
        result = result.at[:, lanes]
        self.links, self.grads, self.beside = links, grads, beside
        self.landed, self.result = landed, result
        self.slab = beside.shape[1]
        self.beside_in, self.far_in = {}, {}
        for step in range(links.num_far):
            target = links.far(step)
            self.beside_in[step] = links.copy(
                grads.at[target ^ 1], beside.at[step], links.beside
            )
            if step:
                self.far_in[step] = links.copy(
                    beside.at[step], landed.at[step], (target, links.tensor)
                )

    def begin(self):
        for step in range(1, self.links.num_far + 1):
            self.beside_in[step % self.links.num_far].start()

    def pass_on(self, step):
        self.beside_in[step].wait_recv()
        mine = self.grads[self.links.far(step)]
        self.beside[step] = (mine.astype(F32) + self.beside[step].astype(F32)).astype(BF)
        self.far_in[step].start()

    def end(self):
        self.beside_in[0].wait_recv()
        total = self.grads[self.links.dp].astype(F32) + self.beside[0].astype(F32)
        for step in range(1, self.links.num_far):
            self.far_in[step].wait_recv()
            total = total + self.landed[step].astype(F32)
        self.result[...] = total


class Refs:
    def __init__(self, names, refs):
        for name, ref in zip(names, refs, strict=True):
            setattr(self, name, ref)


def flat_weight(full, wide, start=0, stop=None):
    count, slab, width = full.shape
    stop = stop or width
    if slab % 16 == 0:
        return full[:, :, start:stop].reshape(count * slab, stop - start)
    for at in range(count):
        wide[at * slab : (at + 1) * slab, start:stop] = full[at, :, start:stop].astype(F32)
    return wide[:, start:stop].astype(BF)


def split_rows(value, grads, start, wide, lane=0):
    count, slab, width = grads.shape
    rows, columns = value.shape
    lanes = slice(lane, lane + columns)
    if slab % 16 == 0:
        low = value.astype(BF).reshape(rows // slab, slab, columns)
        grads[pl.ds(start // slab, rows // slab), :, lanes] = low
        return
    wide[0:rows, lanes] = value
    for at in range(rows // slab):
        grads[start // slab + at, :, lanes] = wide[at * slab : (at + 1) * slab, lanes].astype(BF)


def turn(value):
    rows, columns = value.shape
    tall = jnp.concatenate(
        [value.astype(F32), jnp.zeros((rows, 128 - columns), F32)], axis=1
    )
    return jnp.transpose(tall)[:columns, :].astype(value.dtype)


def layer_kernel(num_dp, names, *refs):
    r = Refs(names, refs)
    links = Links(num_dp, r.send_sems, r.recv_sems)
    me, dp = links.tensor, links.dp
    block, width = r.frames.shape
    length = 4 * block
    num_blocks = length // BLOCK
    heads_width = width // 4
    heads = heads_width // HD
    qkv = 3 * heads_width
    upper = me // 2

    await_all = links.greet(links.others + [links.sibling, links.across, links.corner])

    small_group = [
        links.copy(r.small_mine, r.small_group.at[at], device)
        for at, device in enumerate((links.sibling, links.across, links.corner))
    ]
    small_dp = [
        links.copy(r.small_sum, r.small_dp.at[at], other) for at, other in enumerate(links.others)
    ]
    frame_rows = RowSpread(links, r.frames, r.rows_all)
    given_rows = RowSpread(links, r.cotangent, r.given_all)
    spread_a = WeightSpread(links, r.shard_a, r.full_a, (0, width // 2, width * 5 // 6, width))
    spread_b = WeightSpread(links, r.shard_b, r.full_b, (0, width // 2, width))
    spread_c = WeightSpread(links, r.shard_c, r.full_c, (0, width // 2, width * 5 // 6, width))

    r.shard_a[:, :qkv] = jnp.concatenate([r.in_weight[at] for at in range(3)], axis=1)
    r.shard_a[:, qkv:] = turn(r.out_weight[...])
    own, share = width // (4 * num_dp), HD // num_dp
    r.small_mine[...] = jnp.zeros_like(r.small_mine)
    for at in range(6):
        r.small_mine[at : at + 1, 0:own] = getattr(r, f"vec_{at}")[...]
    r.small_mine[0:6, :] = pltpu.roll(r.small_mine[0:6, :], (dp * 4 + me) * own, 1)
    lane = lax.broadcasted_iota(jnp.int32, (1, width), 1)

    def one_hot(rows, target):
        return jnp.where(
            lax.broadcasted_iota(jnp.int32, (rows, width), 0) == target, 1.0, 0.0
        ).astype(BF)

    tall = dot_nn(r.fc1_bias[...], one_hot(width // HD, lane // HD))
    within = lane % HD - dp * share
    r.small_mine[6:7, :] = column_sum(
        jnp.where(lax.broadcasted_iota(jnp.int32, tall.shape, 0) == within, tall, 0.0)
    )
    row = jnp.zeros((1, width), F32)
    for head in range(heads):
        pair = dot_nn(r.proj_bias[head], one_hot(share, within))
        for at in range(2):
            here = lane // HD == at * (LANE_GAP // HD) + head
            row = row + jnp.where(here, pair[at : at + 1, :], 0.0)
    r.small_mine[7:8, :] = row
    ids = r.seg_row[0:1, :].astype(F32)
    r.seg_wide[...] = jnp.transpose(jnp.broadcast_to(ids, (128, length)))
    await_all()
    for made in small_group:
        made.start()
    for chunk in range(CHUNKS):
        frame_rows.give(chunk)
    spread_a.begin(0)
    spread_a.begin_beside(0)

    total = r.small_mine[...]
    for at, made in enumerate(small_group):
        made.wait_recv()
        total = total + jnp.where(
            lax.broadcasted_iota(jnp.int32, total.shape, 0) < 6, r.small_group[at], 0.0
        )
    r.small_sum[...] = total
    for made in small_dp:
        made.start()
    for half in (1, 2):
        spread_a.begin(half)
        spread_a.begin_beside(half)
    for chunk in range(CHUNKS):
        given_rows.give(chunk)
    for spread, halves in ((spread_b, 2), (spread_c, 3)):
        for half in range(halves):
            spread.begin(half)
            spread.begin_beside(half)
    for spread in (spread_a, spread_b, spread_c):
        spread.keep_own()

    gain_one, shift_one, gain_two, shift_two, bias_out, bias_fc2 = range(6)

    def vec(at):
        return r.vecs[at : at + 1, :]

    def normalise(first):
        @pl.loop(0, num_blocks // 2)
        def first_norm(at):
            rows = rows_at((at + first * (num_blocks // 2)) * BLOCK, BLOCK)
            low = layer_norm(r.rows_all[rows, :].astype(F32), vec(gain_one), vec(shift_one))
            r.normed[rows, :] = low.astype(BF)

    frame_rows.hand_over(0)
    spread_a.forward(0)
    for at, made in enumerate(small_dp):
        made.wait_recv()
        total = total + r.small_dp[at]
    r.vecs[...] = total
    frame_rows.await_sibling()
    normalise(upper)
    frame_rows.hand_over(1)
    spread_a.forward(1)
    frame_rows.hand_over(2)
    spread_a.forward(2)
    frame_rows.await_corner()
    normalise(1 - upper)
    spread_a.end((0, 1))

    @pl.loop(0, num_blocks)
    def project(at):
        rows = rows_at(at * BLOCK, BLOCK)
        low = r.normed[rows, :]
        made = dot_nn(low, flat_weight(r.full_a, r.wide, 0, qkv))
        made_query = (made[:, :heads_width] + r.vecs[7:8, 0:heads_width]).astype(BF)
        r.query[rows, :] = made_query * jnp.asarray(0.125, BF)
        r.keys[rows, :] = made[:, heads_width : 2 * heads_width].astype(BF)
        shift = r.vecs[7:8, LANE_GAP : LANE_GAP + heads_width]
        made_values = (made[:, 2 * heads_width :] + shift).astype(BF)
        r.values[rows, :] = made_values
        r.turned[:, rows] = jnp.transpose(made_values)

    reach = (DOCUMENT_LIMIT - 2) // BLOCK + 1
    spans = sorted(
        {
            min(num_blocks - 1, spot + reach) - max(0, spot - reach) + 1
            for spot in range(num_blocks)
        }
    )

    def by_span(spot, run):
        first = jnp.maximum(spot - reach, 0)
        count = jnp.minimum(spot + reach, num_blocks - 1) - first + 1
        for span in spans:

            @pl.when(count == span)
            def this_span(span=span):
                run(first * BLOCK, span * BLOCK)

    def mask_of(rows, near, size):
        keys_ids = jnp.concatenate([r.seg_wide[near, :]] * (BLOCK // 128), axis=1)
        query_ids = r.seg_row[0:1, rows].astype(F32)
        r.mask[0:size, :] = jnp.where(keys_ids == query_ids, 0.0, -1e30)

    spread_a.end((2,))
    spread_b.forward(0)
    sum_one = RowSum(links, r.part_one, r.side_one, r.home_one, r.far_one)
    spread_two = RowSpread(links, r.normed_own, r.normed_two)

    @pl.loop(0, num_blocks)
    def attend(at):
        spot = lax.rem(at + (1 - upper) * (num_blocks // 2), num_blocks)
        rows = rows_at(spot * BLOCK, BLOCK)

        def mix(start, size):
            near = rows_at(start, size)
            mask_of(rows, near, size)
            asked = r.query[rows, :]
            made = []
            for head in range(heads):
                scores = dot_nt(r.keys[near, :], head_part(asked, head)) + r.mask[0:size, :]
                top = jnp.max(scores, axis=0, keepdims=True)
                weights = jnp.exp(scores - top)
                whole = column_sum(weights)
                given_t = r.turned[head * HD : (head + 1) * HD, near]
                made.append(dot_nn(given_t, weights.astype(BF)) / whole)
                r.stats[spot, head : head + 1, :] = top + jnp.log(whole)
            r.mixed[rows, :] = jnp.transpose(jnp.concatenate(made, axis=0)).astype(BF)

        by_span(spot, mix)
        out = r.mixed[rows, :]
        r.part_one[rows, :] = dot_nt(out, flat_weight(r.full_a, r.wide, qkv)).astype(BF)

        def after(step, core=None):
            return pl.when((at == step) if core is None else ((at == step) & (me % 2 == core)))

        @after(0, 1)
        def upper_first():
            sum_one.side_in[0].start()
            sum_one.side_in[1].start()

        @after(1, 0)
        def lower_second():
            sum_one.pass_on(0)
            sum_one.pass_on(1)
            sum_one.side_in[0].start()

        @after(1, 1)
        def upper_second():
            sum_one.side_in[2].start()

        @after(1)
        def rows_first():
            given_rows.hand_over(0)
            spread_b.forward(1)

        @after(2, 0)
        def lower_third():
            sum_one.side_in[1].start()
            sum_one.side_in[2].start()
            sum_one.pass_on(2)

        @after(2, 1)
        def upper_third():
            sum_one.pass_on(0)

        @after(3, 1)
        def upper_fourth():
            sum_one.pass_on(1)
            sum_one.pass_on(2)

        @after(3)
        def rows_second():
            given_rows.hand_over(1)

        @after(4)
        def weights_second():
            spread_c.forward(0)

    sum_one.begin_home()
    given_rows.hand_over(2)
    r.grad_keys[...] = jnp.zeros_like(r.grad_keys)
    r.grad_values[...] = jnp.zeros_like(r.grad_values)

    @pl.loop(0, num_blocks)
    def turn_keys(at):
        rows = rows_at(at * BLOCK, BLOCK)
        r.turned[:, rows] = jnp.transpose(r.keys[rows, :])

    spread_b.end((0, 1))

    def pair_rows(chunk, member):
        start = chunk * (block // CHUNKS)
        return (
            rows_at(member * block + start, block // CHUNKS),
            rows_at((member ^ 1) * block + start, block // CHUNKS),
        )

    def both(ref, pair):
        return jnp.concatenate([ref[rows, :] for rows in pair], axis=0)

    def put(ref, pair, value):
        low = value.astype(BF)
        ref[pair[0], :] = low[: block // CHUNKS]
        ref[pair[1], :] = low[block // CHUNKS :]

    def hide(pair):
        hidden = dot_nn(both(r.normed_two, pair), flat_weight(r.full_b, r.wide)) + r.vecs[6:7, :]
        below, density = normal_parts(hidden)
        put(r.active, pair, hidden * below)
        put(r.part_two, pair, below + hidden * density)

    @pl.loop(0, CHUNKS)
    def second_norm(at):
        for chunk in range(CHUNKS):

            @pl.when(at == chunk)
            def rows_of(chunk=chunk):
                cut = sum_one.cut(chunk)
                row = r.frames[cut, :].astype(F32) + (sum_one.total(chunk) + vec(bias_out))
                r.middle[cut, :] = row
                r.normed_own[cut, :] = layer_norm(row, vec(gain_two), vec(shift_two)).astype(BF)
                spread_two.give(chunk)
                if chunk < 2:
                    spread_c.forward(1 + chunk)
                spread_two.sibling_in[chunk].wait_recv()

        hide(pair_rows(at, me))

    links.sent(sum_one.far_in + frame_rows.corner_in)
    given_rows.await_sibling()
    given_rows.await_corner()
    spread_c.end((0, 1, 2))

    sum_two = RowSum(links, r.part_two, r.side_two, r.home_two, r.far_two)
    sum_three = RowSum(links, r.normed_two, r.side_three, r.home_three, r.far_three)
    r.small_grads[...] = jnp.zeros_like(r.small_grads)

    @pl.loop(0, 2 * CHUNKS)
    def feed(at):
        def when_at(step):
            return pl.when(at == step)

        for chunk in range(CHUNKS):

            @when_at(2 * chunk)
            def bring(chunk=chunk):
                spread_two.hand_over(chunk)

            @when_at(2 * chunk + 1)
            def remote(chunk=chunk):
                if chunk:
                    sum_two.pass_on(chunk - 1)
                spread_two.corner_in[chunk].wait_recv()

        pair = pair_rows(at // 2, me ^ (2 * (at % 2)))

        @pl.when(at % 2 == 1)
        def remote_first():
            hide(pair)

        grad_active = dot_nn(both(r.given_all, pair), flat_weight(r.full_c, r.wide))
        back = (grad_active * both(r.part_two, pair).astype(F32)).astype(BF)
        put(r.grad_hidden, pair, back)
        put(r.part_two, pair, dot_nt(back, flat_weight(r.full_b, r.wide)))
        r.small_grads[6:7, :] += column_sum(back.astype(F32))

        for chunk in range(CHUNKS):

            @when_at(2 * chunk)
            def near_done(chunk=chunk):
                sum_two.home_in[chunk].start()

            @when_at(2 * chunk + 1)
            def remote_done(chunk=chunk):
                sum_two.side_in[chunk].start()

    sum_two.pass_on(CHUNKS - 1)
    scatter_b = GradScatter(links, r.grads_b, r.beside_b, r.landed_b, r.out_b)
    scatter_c = GradScatter(links, r.grads_c, r.beside_c, r.landed_c, r.out_c)

    spread_three = RowSpread(links, r.attended_own, r.rows_all)

    def second_norm_back(chunk):
        cut = sum_two.cut(chunk)
        grad = sum_two.total(chunk)
        back, unit = layer_norm_back(r.middle[cut, :], grad, vec(gain_two))
        given = r.cotangent[cut, :].astype(F32)
        row = given + back
        r.grad_middle[cut, :] = row
        low = row.astype(BF)
        r.attended_own[cut, :] = low
        spread_three.give(chunk)
        r.small_grads[gain_two : gain_two + 1, :] += column_sum(grad * unit)
        r.small_grads[shift_two : shift_two + 1, :] += column_sum(grad)
        r.small_grads[bias_out : bias_out + 1, :] += column_sum(low.astype(F32))
        r.small_grads[bias_fc2 : bias_fc2 + 1, :] += column_sum(given)

    def weigh_one(at):
        columns = rows_at(at * block, block)
        made = dot_tn(r.normed_two[:, columns], r.grad_hidden[...])
        split_rows(made, r.grads_b, at * block, r.wide)

    def weigh_two(at):
        columns = rows_at(at * block, block)
        made = dot_tn(r.given_all[:, columns], r.active[...])
        split_rows(made, r.grads_c, at * block, r.wide)

    second_norm_back(0)
    weigh_one(0)
    second_norm_back(1)
    weigh_one(1)
    scatter_b.begin()
    weigh_two(0)
    second_norm_back(2)
    weigh_two(1)
    scatter_c.begin()
    links.sent(spread_two.corner_in)

    @pl.loop(0, 4)
    def branch(at):
        rows = rows_at((me ^ (3 - at)) * block, block)
        made = dot_nt(r.active[rows, :], flat_weight(r.full_c, r.wide))
        r.normed_two[rows, :] = made.astype(BF)

        @pl.when(at == 0)
        def corner_done():
            sum_three.begin_side()

        @pl.when(at == 2)
        def sibling_done():
            sum_three.begin_home()

    spread_three.await_sibling()

    @pl.loop(0, num_blocks)
    def attend_back(at):
        def when_at(step):
            return pl.when(at == step)

        @when_at(1)
        def first_service():
            for chunk in range(CHUNKS):
                sum_three.pass_on(chunk)
            spread_three.hand_over(0)
            spread_three.hand_over(1)
            scatter_b.pass_on(1)
            scatter_b.pass_on(2)

        @when_at(2)
        def second_service():
            spread_three.hand_over(2)
            for step in range(3, links.num_far):
                scatter_b.pass_on(step)

        @when_at(3)
        def third_service():
            spread_three.await_corner()

        @when_at(4)
        def fourth_service():
            scatter_c.pass_on(1)

        @when_at(5)
        def fifth_service():
            for step in range(2, links.num_far):
                scatter_c.pass_on(step)

        spot = lax.rem(at + upper * (num_blocks // 2), num_blocks)
        rows = rows_at(spot * BLOCK, BLOCK)
        asked = r.query[rows, :]
        given = dot_nn(r.rows_all[rows, :], flat_weight(r.full_a, r.wide, qkv)).astype(BF)
        joint = jnp.transpose(given.astype(F32) * r.mixed[rows, :].astype(F32))
        asked_heads = [head_part(asked, head) for head in range(heads)]
        given_heads = [head_part(given, head) for head in range(heads)]

        def unmix(start, size):
            near = rows_at(start, size)
            mask_of(rows, near, size)
            made = []
            for head in range(heads):
                lanes = slice(head * BLOCK, (head + 1) * BLOCK)
                scores = dot_nt(r.keys[near, :], asked_heads[head]) + r.mask[0:size, :]
                probs = jnp.exp(scores - r.stats[spot, head : head + 1, :])
                inner = column_sum(joint[head * HD : (head + 1) * HD, :])
                slopes = dot_nt(r.values[near, :], given_heads[head]) - inner
                slopes = (probs * slopes).astype(BF)
                r.active[0:size, lanes] = probs.astype(BF)
                r.grad_hidden[0:size, lanes] = slopes
                made.append(dot_nn(r.turned[head * HD : (head + 1) * HD, near], slopes))
            given_tall = jnp.concatenate(given_heads, axis=0)
            asked_tall = jnp.concatenate(asked_heads, axis=0)
            r.grad_values[near, :] += dot_nn(r.active[0:size, :], given_tall)
            r.grad_keys[near, :] += dot_nn(r.grad_hidden[0:size, :], asked_tall)
            turned = jnp.transpose(jnp.concatenate(made, axis=0)) * 0.125
            r.grad_proj[rows, :heads_width] = turned.astype(BF)

        by_span(spot, unmix)

    links.sent(sum_one.side_in + sum_one.home_in)
    sum_four = RowSum(links, r.part_one, r.side_one, r.home_one, r.far_one)

    def join(rows):
        low_keys = r.grad_keys[rows, :].astype(BF)
        low_values = r.grad_values[rows, :].astype(BF)
        low_query = r.grad_proj[rows, :heads_width]
        whole = jnp.concatenate([low_query, low_keys, low_values], axis=1)
        r.grad_proj[rows, :] = whole
        wide_sum = column_sum(whole.astype(F32))
        r.small_grads[7:8, 0:heads_width] += wide_sum[:, 0:heads_width]
        r.small_grads[7:8, LANE_GAP : LANE_GAP + heads_width] += wide_sum[:, 2 * heads_width :]

    def push(rows):
        made = dot_nt(r.grad_proj[rows, :], flat_weight(r.full_a, r.wide, 0, qkv))
        r.part_one[rows, :] = made.astype(BF)

    scatter_o = GradScatter(
        links, r.grads_a, r.beside_a, r.landed_a, r.out_a, width * 5 // 6, width
    )

    @pl.loop(0, width // block)
    def weigh_out(at):
        columns = rows_at(at * block, block)
        split_rows(dot_tn(r.rows_all[:, columns], r.mixed[...]), r.grads_a, at * block, r.wide, qkv)

    scatter_o.begin()

    @pl.loop(0, 2)
    def project_remote(at):
        rows = rows_at((me ^ (3 - at)) * block, block)
        join(rows)
        push(rows)

        @pl.when(at == 0)
        def corner_done():
            sum_four.begin_side()

        @pl.when(at == 1)
        def across_done():
            for chunk in range(CHUNKS):
                sum_four.pass_on(chunk)

    @pl.loop(0, 2)
    def join_near(at):
        join(rows_at((me ^ at) * block, block))

    middle_lane = width // 2
    scatter_a = [
        GradScatter(links, r.grads_a, r.beside_a, r.landed_a, r.out_a, *lanes)
        for lanes in ((0, middle_lane), (middle_lane, width * 5 // 6))
    ]

    @pl.loop(0, width // block)
    def weigh_in(at):
        columns = rows_at(at * block, block)
        made = dot_tn(r.normed[:, columns], r.grad_proj[:, 0:middle_lane])
        split_rows(made, r.grads_a, at * block, r.wide, 0)

    scatter_a[0].begin()
    for step in range(1, links.num_far):
        scatter_o.pass_on(step)

    @pl.loop(0, width // block)
    def weigh_in_too(at):
        columns = rows_at(at * block, block)
        made = dot_tn(r.normed[:, columns], r.grad_proj[:, middle_lane:qkv])
        split_rows(made, r.grads_a, at * block, r.wide, middle_lane)

    scatter_a[1].begin()

    @pl.loop(0, 2)
    def project_near(at):
        push(rows_at((me ^ (1 - at)) * block, block))

    sum_four.begin_home()
    def first_norm_back(chunk):
        cut = sum_four.cut(chunk)
        grad = sum_four.total(chunk)
        back, unit = layer_norm_back(r.frames[cut, :].astype(F32), grad, vec(gain_one))
        r.grad_frames[cut, :] = r.grad_middle[cut, :] + back
        keep_result("grad_frames", cut)
        r.small_grads[gain_one : gain_one + 1, :] += column_sum(grad * unit)
        r.small_grads[shift_one : shift_one + 1, :] += column_sum(grad)

    kept = []

    def keep_result(name, cut=None):
        source, place = getattr(r, name), getattr(r, name + "_hbm")
        if cut is not None:
            source, place = source.at[cut], place.at[cut]
        made = pltpu.make_async_copy(source, place, r.local_sems.at[len(kept)])
        made.start()
        kept.append(made)

    scatter_b.end()
    keep_result("out_b")
    scatter_a[0].pass_on(1)
    first_norm_back(0)
    for step in range(2, links.num_far):
        scatter_a[0].pass_on(step)
    for chunk in range(CHUNKS):
        cut = sum_three.cut(chunk)
        row = r.middle[cut, :] + (sum_three.total(chunk) + vec(bias_fc2))
        r.output[cut, :] = row.astype(BF)
    keep_result("output")
    first_norm_back(1)
    scatter_a[1].pass_on(1)
    scatter_a[1].pass_on(2)
    first_norm_back(2)

    back_group = [
        links.copy(r.small_grads, r.small_group_back.at[at], device)
        for at, device in enumerate((links.sibling, links.across, links.corner))
    ]
    back_dp = [
        links.copy(r.small_total, r.small_dp.at[at], other)
        for at, other in enumerate(links.others)
    ]
    for made in back_group:
        made.start()
    for step in range(3, links.num_far):
        scatter_a[1].pass_on(step)
    total = r.small_grads[...]
    for at, made in enumerate(back_group):
        made.wait_recv()
        total = total + jnp.where(
            lax.broadcasted_iota(jnp.int32, total.shape, 0) < 6, r.small_group_back[at], 0.0
        )
    r.small_total[...] = total
    for made in back_dp:
        made.start()
    scatter_c.end()
    keep_result("out_c")
    scatter_o.end()
    for scatter in scatter_a:
        scatter.end()
    keep_result("out_a")
    for at, made in enumerate(back_dp):
        made.wait_recv()
        total = total + r.small_dp[at]
    start = (dp * 4 + me) * own
    r.small_out[0:6, :] = pltpu.roll(total[0:6, :], lax.rem(width - start, width), 1)
    start = dp * share
    r.small_out[6:8, :] = pltpu.roll(total[6:8, :], lax.rem(width - start, width), 1)
    keep_result("small_out")
    links.finish()
    for made in kept:
        made.wait()


def copy_count(num_dp):
    far = num_dp // 2
    smalls = 2 * (num_dp - 1 + 3)
    spreads = 4 * 3 * CHUNKS
    weights = (3 + 2 + 3) * (2 * far - 1)
    sums = 4 * 3 * CHUNKS
    scatters = 5 * (2 * far - 1)
    return smalls + spreads + weights + sums + scatters


def layer(num_dp, seg, frames, cotangent, vecs, proj_bias, fc1_bias, in_weight, out_weight, shard_b, shard_c):
    block, width = frames.shape
    length, slab = 4 * block, shard_b.shape[0]
    heads_width = width // 4
    num_blocks = length // BLOCK
    vmem = pl.BlockSpec(memory_space=pltpu.VMEM)
    inputs = [
        ("seg_row", seg, vmem),
        ("frames", frames, vmem),
        ("cotangent", cotangent, vmem),
        ("proj_bias", proj_bias, vmem),
        ("fc1_bias", fc1_bias, vmem),
        ("in_weight", in_weight, vmem),
        ("out_weight", out_weight, vmem),
        ("shard_b", shard_b, vmem),
        ("shard_c", shard_c, vmem),
    ]
    inputs += [(f"vec_{at}", value, vmem) for at, value in enumerate(vecs)]
    outputs = [
        ("output", (block, width), BF),
        ("grad_frames", (block, width), F32),
        ("out_a", (slab, width), F32),
        ("out_b", (slab, width), F32),
        ("out_c", (slab, width), F32),
        ("small_out", (8, width), F32),
    ]
    scratch = [("rows_all", (length, width), BF), ("given_all", (length, width), BF)]
    scratch += [("normed", (length, width), BF), ("normed_two", (length, width), BF)]
    scratch += [("active", (length, width), BF), ("grad_hidden", (length, width), BF)]
    scratch += [(f"full_{tag}", (num_dp, slab, width), BF) for tag in "abc"]
    scratch += [(f"grads_{tag}", (num_dp, slab, width), BF) for tag in "abc"]
    for tag in "abc":
        scratch += [
            (f"{kind}_{tag}", (num_dp // 2, slab, width), BF)
            for kind in ("beside", "landed")
        ]
    for tag in ("one", "two", "three"):
        if tag != "three":
            scratch += [(f"part_{tag}", (length, width), BF)]
        scratch += [
            (f"{kind}_{tag}", (block, width), BF) for kind in ("side", "home", "far")
        ]
    scratch += [
        (name, (length, heads_width), BF)
        for name in ("query", "keys", "values", "mixed")
    ]
    scratch += [
        ("turned", (heads_width, length), BF),
        ("grad_keys", (length, heads_width), F32),
        ("grad_values", (length, heads_width), F32),
        ("grad_proj", (length, 3 * heads_width), BF),
        ("mask", (length, BLOCK), F32),
        ("seg_wide", (length, 128), F32),
        ("stats", (num_blocks, 8, BLOCK), F32),
        ("middle", (block, width), F32),
        ("grad_middle", (block, width), F32),
        ("normed_own", (block, width), BF),
        ("attended_own", (block, width), BF),
        ("vecs", (8, width), F32),
        ("shard_a", (slab, width), BF),
        ("wide", (width if slab % 16 else 8, width), F32),
    ]
    for name in ("small_mine", "small_sum", "small_grads", "small_total"):
        scratch += [(name, (8, width), F32)]
    for name in ("small_group", "small_group_back"):
        scratch += [(name, (3, 8, width), F32)]
    scratch += [("small_dp", (num_dp - 1, 8, width), F32)]
    scratch += outputs
    outputs = [(name + "_hbm", shape, kind) for name, shape, kind in outputs]
    count = copy_count(num_dp)
    names = [name for name, _, _ in inputs + outputs + scratch]
    names += ["send_sems", "recv_sems", "local_sems"]
    return pl.pallas_call(
        functools.partial(layer_kernel, num_dp, names),
        out_shape=[jax.ShapeDtypeStruct(shape, kind) for _, shape, kind in outputs],
        in_specs=[spec for _, _, spec in inputs],
        out_specs=[pl.BlockSpec(memory_space=pl.ANY)] * len(outputs),
        scratch_shapes=[pltpu.VMEM(shape, kind) for _, shape, kind in scratch]
        + [pltpu.SemaphoreType.DMA((count,))] * 2
        + [pltpu.SemaphoreType.DMA((8,))],
        compiler_params=pltpu.CompilerParams(
            collective_id=0, has_side_effects=True, vmem_limit_bytes=VMEM_BYTES
        ),
        name="layer",
    )(*[value for _, value, _ in inputs])


def unpack_kernel(own, share, output, grad_frames, grads_a_in, grads_b, grads_c, sums_in, output_too, grad_frames_too, g_in, g_proj, g_out, grads_b_too, g_fc1b, grads_c_too, vec_0, vec_1, vec_2, vec_3, vec_4, vec_5, output_v, grad_frames_v, grads_a, grads_b_v, grads_c_v, sums, in_sems, out_sems):
    pieces = grad_frames.shape[0] // CHUNKS
    cuts = [pl.ds(at * pieces, pieces) for at in range(CHUNKS)]
    moves = [(sums_in, sums, None), (grads_a_in, grads_a, None)]
    moves += [(grads_b, grads_b_v, grads_b_too), (grads_c, grads_c_v, grads_c_too)]
    moves += [(output, output_v, output_too)]
    moves += [
        (grad_frames.at[cut], grad_frames_v.at[cut], grad_frames_too.at[cut]) for cut in cuts
    ]
    inward = [
        pltpu.make_async_copy(source, held, in_sems.at[at])
        for at, (source, held, _) in enumerate(moves)
    ]
    for made in inward:
        made.start()
    inward[0].wait()
    inward[1].wait()
    copies = []
    for at in range(2, len(moves)):
        inward[at].wait()
        made = pltpu.make_async_copy(moves[at][1], moves[at][2], out_sems.at[at])
        made.start()
        copies.append(made)
    heads_width = g_in.shape[2]
    for at in range(3):
        g_in[at] = grads_a[:, at * heads_width : (at + 1) * heads_width]
    g_out[...] = jnp.transpose(grads_a[:, 3 * heads_width :])
    for at, vec in enumerate((vec_0, vec_1, vec_2, vec_3, vec_4, vec_5)):
        vec[...] = sums[at : at + 1, 0:own]
    width = sums.shape[1]
    pieces = [
        pltpu.roll(sums[...], (width - at * HD) % width, 1)[6:7, 0:128] for at in range(width // HD)
    ]
    pieces.append(jnp.zeros((16 - len(pieces), 128), F32))
    g_fc1b[...] = jnp.transpose(jnp.concatenate(pieces, axis=0))[0:share, 0 : width // HD]
    for head in range(heads_width // HD):
        for at in range(2):
            start = at * LANE_GAP + head * HD
            piece = pltpu.roll(sums[...], (width - start) % width, 1)
            g_proj[head, at : at + 1, :] = piece[7:8, 0:share]
    for made in copies:
        made.wait()


def unpack(own, share, results):
    output, grad_frames, grads_a, grads_b, grads_c, sums = results
    slab, width = grads_a.shape
    heads_width = width // 4
    vmem, hbm = pl.BlockSpec(memory_space=pltpu.VMEM), pl.BlockSpec(memory_space=pl.ANY)
    shapes = [
        (output.shape, BF, hbm),
        (grad_frames.shape, F32, hbm),
        ((3, slab, heads_width), F32, vmem),
        ((heads_width // HD, 2, share), F32, vmem),
        ((heads_width, slab), F32, vmem),
        ((slab, width), F32, hbm),
        ((share, width // HD), F32, vmem),
        ((slab, width), F32, hbm),
    ] + [((1, own), F32, vmem)] * 6
    return pl.pallas_call(
        functools.partial(unpack_kernel, own, share),
        out_shape=[jax.ShapeDtypeStruct(shape, kind) for shape, kind, _ in shapes],
        in_specs=[hbm] * 6,
        out_specs=[spec for _, _, spec in shapes],
        scratch_shapes=[pltpu.VMEM(value.shape, value.dtype) for value in results]
        + [pltpu.SemaphoreType.DMA((2 + 3 + CHUNKS,))] * 2,
        compiler_params=pltpu.CompilerParams(vmem_limit_bytes=VMEM_BYTES),
        name="unpack",
    )(*results)


def on_device(
    num_dp,
    frames,
    segments,
    norm1_gain,
    norm1_shift,
    in_weight,
    proj_bias,
    out_weight,
    out_bias,
    norm2_gain,
    norm2_shift,
    fc1_weight,
    fc1_bias,
    fc2_weight,
    fc2_bias,
    cotangent,
):
    slab, _, heads_width = in_weight.shape
    vecs = [norm1_gain, norm1_shift, norm2_gain, norm2_shift, out_bias, fc2_bias]
    results = layer(
        num_dp,
        segments,
        frames,
        cotangent,
        [value[None] for value in vecs],
        proj_bias.transpose(1, 0, 2),
        fc1_bias.T,
        in_weight.transpose(1, 0, 2),
        out_weight,
        fc1_weight,
        fc2_weight.T,
    )
    output, grad_frames, g_in, g_proj, g_out, g_b, g_fc1b, g_c, *rows = unpack(
        norm1_gain.shape[0], HD // num_dp, results
    )
    rows = [row[0] for row in rows]
    return (
        output,
        grad_frames,
        rows[0],
        rows[1],
        g_in.transpose(1, 0, 2),
        g_proj.transpose(1, 0, 2),
        g_out,
        rows[4],
        rows[2],
        rows[3],
        g_b,
        g_fc1b.T,
        g_c.T,
        rows[5],
    )


def solution(mesh):
    in_specs = (
        P(("dp", "tensor"), None),
        P("dp", None),
        P(("dp", "tensor")),
        P(("dp", "tensor")),
        P("dp", None, "tensor"),
        P(None, "tensor", "dp"),
        P("tensor", "dp"),
        P(("dp", "tensor")),
        P(("dp", "tensor")),
        P(("dp", "tensor")),
        P("dp", "tensor"),
        P("tensor", "dp"),
        P("tensor", "dp"),
        P(("dp", "tensor")),
        P(("dp", "tensor"), None),
    )
    out_specs = (
        P(("dp", "tensor"), None),
        P(("dp", "tensor"), None),
        P(("dp", "tensor")),
        P(("dp", "tensor")),
        P("dp", None, "tensor"),
        P(None, "tensor", "dp"),
        P("tensor", "dp"),
        P(("dp", "tensor")),
        P(("dp", "tensor")),
        P(("dp", "tensor")),
        P("dp", "tensor"),
        P("tensor", "dp"),
        P("tensor", "dp"),
        P(("dp", "tensor")),
    )
    return jax.shard_map(
        functools.partial(on_device, mesh.shape["dp"]),
        mesh=mesh,
        in_specs=in_specs,
        out_specs=out_specs,
        check_vma=False,
    )
```
